32 devices in a mesh: sample: 2 (over x), axial: 16 (over z, y, core).
Axes of the slice: x: 2, y: 2, z: 4, core: 2. Of those that a mesh axis runs over, the one named last changes fastest.
Arguments:
- initial_state: float32 [10, 512, 1024], P('sample', 'axial'), parts along dimension 0, may hold values from -6 to 6
- forcing: float32 [10, 512, 1024], P('sample', 'axial'), parts along dimension 0, may hold values from -6 to 6
- coefficients: float32 [50, 64], P('sample', 'axial'), parts along dimension 0, may hold values from -0.5 to 0.5, as said below
- region_ids: int32 [512, 8], P('axial'), may hold values from 0 to 63
Outputs:
- updated_state: float32 [10, 512, 1024], P('sample', 'axial'), parts along dimension 0
The draws below stay inside these ranges and needn't reach their ends.
There are 2 independent parts, one for each index of `sample`. The reference program is written for one: setup_inputs(seed, part) draws one part's arguments, and reference() takes and returns one part's arrays. A program takes and returns all parts, laid end to end along the dimension named above; an argument that names none is the same for every part. Nothing has to cross between parts.
Inputs may be any that keep to these rules, and one draw needn't show every extreme that they name: `coefficients`: entry 5 f + g holds row f, column g of a region's block; every diagonal entry is positive and exceeds the sum of magnitudes of the other entries of its row.
All inputs are finite; a program needn't handle non-finite values.
Results may differ from the reference program's by a relative error of at most 0.0001.
Values sent between devices are 32-bit elements; how exact they have to be, the bound alone decides.
No kernel may reach another device: no remote copies, remote signals or barrier semaphores. Data moves between devices by JAX's collectives and lax.ppermute only.
A program may use at most 128 MiB of HBM per device.

```python
import math
import jax
import jax.numpy as jnp

FIELDS = 5
RADIAL = 1024
BLOCK_R = 128
SWEEPS_PRE = 2
SWEEPS_POST = 2
SWEEPS_COARSE = 4
CYCLES = 2
REGIONS = 64
NAX = 512


def draw_coefficients(key, part):
    diagonal_key, coupling_key = jax.random.split(key)
    diagonal = jnp.exp(jax.random.uniform(diagonal_key, (FIELDS, REGIONS), jnp.float32, math.log(0.05), math.log(0.5)))
    coupling = jax.random.uniform(coupling_key, (FIELDS, FIELDS, REGIONS), jnp.float32, -0.2, 0.2)
    identity = jnp.eye(FIELDS, dtype=jnp.float32)[:, :, None]
    blocks = coupling * diagonal[:, None, :] * (1.0 - identity) + identity * diagonal[:, None, :]
    return blocks.reshape(FIELDS * FIELDS, REGIONS)


def touch_ends(result, rng, least, largest):
    dims = result.shape
    place = [jax.random.randint(jax.random.fold_in(rng, axis), (), 0, dims[axis]) for axis in range(len(dims))]
    result = result.at[tuple(place)].set(least)
    longest = dims.index(max(dims))
    place[longest] = (place[longest] + 1) % dims[longest]
    return result.at[tuple(place)].set(largest)


def levels(own_key, dims, cuts, low, top_value):
    def one(axis_at, blocks):
        steps = jax.random.uniform(jax.random.fold_in(jax.random.fold_in(own_key, 6), axis_at), (blocks,), jnp.float32, low / len(cuts), top_value / len(cuts))
        return jnp.repeat(jnp.exp(steps), dims[axis_at] // blocks).reshape((-1,) + (1,) * (len(dims) - axis_at - 1))

    level = one(*cuts[0])
    for cut in cuts[1:]:
        level = level * one(*cut)
    return level


def bell_draw(own_key, shape, deviation, bound, cuts=(), held_as=jnp.bfloat16):
    drawn = deviation * jax.random.normal(own_key, shape, jnp.float32)
    if cuts:
        drawn = drawn * levels(own_key, shape, cuts, -0.22, 0.18)
    return jnp.clip(drawn, -bound, bound).astype(held_as)


def setup_inputs(seed: int = 0, part: int = 0) -> dict:
    splits = jax.random.split(jax.random.key(seed), 5)
    own_keys = jax.random.split(jax.random.fold_in(splits[4], part), 5)
    return {
        "initial_state": bell_draw(own_keys[0], (FIELDS, NAX, RADIAL), 1.0, 6.0, ((1, 16),), jnp.float32),
        "forcing": bell_draw(own_keys[1], (FIELDS, NAX, RADIAL), 1.0, 6.0, ((1, 16),), jnp.float32),
        "coefficients": draw_coefficients(jax.random.fold_in(jax.random.fold_in(splits[4], part), 71), part),
        "region_ids": touch_ends(jax.random.randint(splits[3], (NAX, RADIAL // BLOCK_R), 0, REGIONS), jax.random.fold_in(splits[3], 1), 0, REGIONS - 1).astype(jnp.int32),
    }


DIFFUSION = 1.0
RELAXATION = 0.8
SOURCE_GAIN = 0.05


def matvec_block(matrix, vector):
    block_order = vector.shape[0]
    blocks = matrix.reshape((block_order, block_order) + vector.shape[1:])
    return jnp.sum(blocks * vector[None], axis=1)


def invert_blocks(matrix):
    block_order = 5
    ones_block = jnp.ones_like(matrix[0])
    nothing = jnp.zeros_like(matrix[0])
    augmented = [[matrix[block_order * row_at + col_at] for col_at in range(block_order)]
                 + [ones_block if row_at == col_at else nothing for col_at in range(block_order)]
                 for row_at in range(block_order)]
    for column in range(block_order):
        leading = 1.0 / augmented[column][column]
        augmented[column] = [element * leading for element in augmented[column]]
        for row_at in range(block_order):
            if row_at != column:
                factor = augmented[row_at][column]
                augmented[row_at] = [element - factor * source for element, source in zip(augmented[row_at], augmented[column])]
    return jnp.stack([augmented[row_at][block_order + col_at] for row_at in range(block_order) for col_at in range(block_order)])


def diagonal_block(matrix, weight):
    identity = jnp.eye(5, dtype=matrix.dtype).reshape(25, 1, 1)
    return matrix + (4.0 * weight) * identity


def operate(padded, matrix, weight):
    centre = padded[:, 1:-1]
    radial = jnp.pad(centre, ((0, 0), (0, 0), (1, 1)))
    beside = ((padded[:, 2:] + padded[:, :-2]) + radial[:, :, 2:]) + radial[:, :, :-2]
    return (matvec_block(matrix, centre) + weight * (4.0 * centre - beside)) + SOURCE_GAIN * jnp.tanh(centre)


def relax_sweep(padded, forcing, matrix, inverse, weight):
    centre = padded[:, 1:-1]
    return centre + RELAXATION * matvec_block(inverse, forcing - operate(padded, matrix, weight))


def restrict(values):
    return 0.25 * (((values[:, 0::2, 0::2] + values[:, 1::2, 0::2]) + values[:, 0::2, 1::2]) + values[:, 1::2, 1::2])


def prolong(values):
    return jnp.repeat(jnp.repeat(values, 2, axis=1), 2, axis=2)


def pad_axial(values):
    return jnp.pad(values, ((0, 0), (1, 1), (0, 0)))


def reference(initial_state, forcing, coefficients, region_ids):
    picked = coefficients[:, region_ids]
    matrices = [jnp.repeat(picked, BLOCK_R, axis=2)]
    for level_at in range(3):
        matrices.append(restrict(matrices[-1]))
    weights = [DIFFUSION / 4.0 ** level_at for level_at in range(4)]
    inverses = [invert_blocks(diagonal_block(matrices[level_at], weights[level_at])) for level_at in range(4)]

    def vcycle_level(level_at, values, source):
        if level_at == 3:
            for sweep_at in range(SWEEPS_COARSE):
                values = relax_sweep(pad_axial(values), source, matrices[3], inverses[3], weights[3])
            return values
        for sweep_at in range(SWEEPS_PRE):
            values = relax_sweep(pad_axial(values), source, matrices[level_at], inverses[level_at], weights[level_at])
        residual = source - operate(pad_axial(values), matrices[level_at], weights[level_at])
        coarse = restrict(values)
        coarse_source = operate(pad_axial(coarse), matrices[level_at + 1], weights[level_at + 1]) + restrict(residual)
        corrected = vcycle_level(level_at + 1, coarse, coarse_source)
        values = values + prolong(corrected - coarse)
        for sweep_at in range(SWEEPS_POST):
            values = relax_sweep(pad_axial(values), source, matrices[level_at], inverses[level_at], weights[level_at])
        return values

    values = initial_state
    for cycle_at in range(CYCLES):
        values = vcycle_level(0, values, forcing)
    return values
```

```python
import functools

import jax
import jax.numpy as jnp
from jax import lax
from jax.experimental import pallas as pl
from jax.experimental.pallas import tpu as pltpu
from jax.sharding import PartitionSpec as P

DIFFUSION = 1.0
RELAXATION = 0.8
SOURCE_GAIN = 0.05
CYCLES = 2

FIELDS = 5
ENTRIES = FIELDS * FIELDS
SUB, LANES = 8, 128

OWN = 32
FINE_HALO = 11
PAD = 9
HEAD = 8
T0, O0 = 64, 16
T1, O1 = 32, 8
T2, O2 = 40, 16
T3, O3 = 20, 8
GROUP = 4


def padded_rows(rows):
    return HEAD + PAD * rows + 16


def at(row):
    return HEAD + PAD * row


def lane_iota():
    return lax.broadcasted_iota(jnp.int32, (SUB, LANES), 1)


def tile(ref, field, row):
    return ref[field, pl.ds(at(row), SUB), :]


def put(ref, field, row, value):
    ref[field, pl.ds(at(row), SUB), :] = value


def rows_loop(first, last, body):
    def step(row, carry):
        body(row)
        return carry

    lax.fori_loop(first, last, step, 0)


def neighbours(ref, row, level):
    width = 2**level
    lane = lane_iota()
    sums, centres = [], []
    for field in range(FIELDS):
        start = at(row)
        centre = ref[field, pl.ds(start, SUB), :]
        lower = ref[field, pl.ds(start - 1, SUB), :]
        upper = ref[field, pl.ds(start + 1, SUB), :]
        left = pltpu.roll(jnp.where(lane >= LANES - width, lower, centre), width, 1)
        right = pltpu.roll(jnp.where(lane < width, upper, centre), LANES - width, 1)
        axial = ref[field, pl.ds(start - PAD, SUB), :] + ref[field, pl.ds(start + PAD, SUB), :]
        sums.append((left + right) + axial)
        centres.append(centre)
    return sums, centres


def table_tile(table, row):
    return table[pl.ds(pl.multiple_of(row * SUB, SUB), SUB), :]


def block_times(entries, first, vectors):
    out = []
    for row in range(FIELDS):
        total = None
        for column in range(FIELDS):
            lane = first + FIELDS * row + column
            term = jnp.broadcast_to(entries[:, lane : lane + 1], (SUB, LANES)) * vectors[column]
            total = term if total is None else total + term
        out.append(total)
    return out


MATRIX_LANE = 32


def gain_of(level):
    return SOURCE_GAIN * 4.0**level / DIFFUSION


def sweep(source_of, old, new, table, level, first, last):
    gain = gain_of(level)

    def body(row):
        sums, centres = neighbours(old, row, level)
        rest = [
            (source_of(field, row) + sums[field]) - gain * jnp.tanh(centres[field])
            for field in range(FIELDS)
        ]
        moved = block_times(table_tile(table, row), 0, rest)
        for field in range(FIELDS):
            put(new, field, row, (1.0 - RELAXATION) * centres[field] + moved[field])

    rows_loop(first, last, body)


def residual(source_of, values, table, level, row):
    gain = gain_of(level)
    sums, centres = neighbours(values, row, level)
    applied = block_times(table_tile(table, row), MATRIX_LANE, centres)
    left = [
        ((source_of(field, row) + sums[field]) - gain * jnp.tanh(centres[field])) - applied[field]
        for field in range(FIELDS)
    ]
    return left, centres


def pair_sum(value, level):
    width = 2**level
    lane = lane_iota()
    other = jnp.where(
        (lane & width) == 0, pltpu.roll(value, LANES - width, 1), pltpu.roll(value, width, 1)
    )
    return value + other


def coarsen(source_of, values, table, level, row):
    upper_r, upper_v = residual(source_of, values, table, level, 2 * row)
    lower_r, lower_v = residual(source_of, values, table, level, 2 * row + 1)
    coarse = [0.25 * pair_sum(upper_v[f] + lower_v[f], level) for f in range(FIELDS)]
    rest = [pair_sum(upper_r[f] + lower_r[f], level) for f in range(FIELDS)]
    return coarse, rest


def first_sweep(coarse, rest, table, row):
    moved = block_times(table_tile(table, row), 0, rest)
    return [coarse[f] + moved[f] for f in range(FIELDS)]


def make_source(coarse, rest, source, table, level, first, last):
    gain = gain_of(level)

    def body(row):
        sums, centres = neighbours(coarse, row, level)
        applied = block_times(table_tile(table, row), MATRIX_LANE, centres)
        for field in range(FIELDS):
            source[field, row] = (applied[field] - sums[field]) + (
                gain * jnp.tanh(centres[field]) + rest[field, row]
            )

    rows_loop(first, last, body)


def correct(fine, after, before, offset, first, last):
    def body(row):
        coarse_row = row // 2 + offset
        for field in range(FIELDS):
            change = tile(after, field, coarse_row) - tile(before, field, coarse_row)
            put(fine, field, row, tile(fine, field, row) + change)

    rows_loop(first, last, body)


def clear(ref):
    ref[...] = jnp.zeros_like(ref)


def tables_kernel(where_ref, coeff_ref, ids_ref, tab0, tab1, tab2, tab3, mats, full):
    device, devices = where_ref[0], where_ref[1]
    regions = coeff_ref.shape[1]
    wide = 5 * 256
    exact = lax.Precision.HIGHEST
    region = lax.broadcasted_iota(jnp.int32, (regions, LANES), 0)
    coeff = coeff_ref[...]
    for chunk in range(10):
        ids = jnp.broadcast_to(ids_ref[chunk : chunk + 1, :], (regions, LANES)).astype(jnp.int32)
        chosen = (region == ids).astype(jnp.float32)
        mats[:, chunk * LANES : (chunk + 1) * LANES] = jnp.dot(
            coeff, chosen, precision=exact, preferred_element_type=jnp.float32
        )

    def averaged(lanes_in, lanes_out, span, source):
        into = lax.broadcasted_iota(jnp.int32, (lanes_in, lanes_out), 0)
        out = lax.broadcasted_iota(jnp.int32, (lanes_in, lanes_out), 1)
        same = (into // (SUB * span) == out // SUB) & ((into % SUB) == (out % SUB))
        average = jnp.where(same, 1.0 / span, 0.0).astype(jnp.float32)
        return jnp.dot(source, average, precision=exact, preferred_element_type=jnp.float32)

    def build(matrix, level, rows, own_first, out):
        lanes = rows * SUB
        weight = DIFFUSION / 4.0**level
        row = lax.broadcasted_iota(jnp.int32, (SUB, lanes), 1) // SUB
        own = OWN >> level
        whole = (row - own_first) + device * own
        inside = (whole >= 0) & (whole < devices * own)
        full[:, :lanes] = jnp.zeros((LANES, lanes), jnp.float32)
        full[0:32, :lanes] = matrix
        entry = lambda e: jnp.broadcast_to(full[e : e + 1, :lanes], (SUB, lanes))
        block = [[entry(FIELDS * i + j) for j in range(FIELDS)] for i in range(FIELDS)]
        for i in range(FIELDS):
            block[i][i] = block[i][i] + 4.0 * weight
        for i in range(FIELDS):
            for j in range(FIELDS):
                e = MATRIX_LANE + FIELDS * i + j
                full[e : e + 1, :lanes] = (block[i][j] * (1.0 / weight))[0:1]
        right = [[None] * FIELDS for _ in range(FIELDS)]
        for i in range(FIELDS):
            right[i][i] = jnp.ones((SUB, lanes), jnp.float32)
        for c in range(FIELDS):
            lead = 1.0 / block[c][c]
            for j in range(c + 1, FIELDS):
                block[c][j] = block[c][j] * lead
            for j in range(FIELDS):
                if right[c][j] is not None:
                    right[c][j] = right[c][j] * lead
            for i in range(FIELDS):
                if i == c:
                    continue
                factor = block[i][c]
                for j in range(c + 1, FIELDS):
                    block[i][j] = block[i][j] - factor * block[c][j]
                for j in range(FIELDS):
                    if right[c][j] is not None:
                        term = factor * right[c][j]
                        right[i][j] = -term if right[i][j] is None else right[i][j] - term
        for i in range(FIELDS):
            for j in range(FIELDS):
                e = FIELDS * i + j
                scaled = jnp.where(inside, right[i][j] * (RELAXATION * weight), 0.0)
                full[e : e + 1, :lanes] = scaled[0:1]
        padded_lanes = -(-lanes // LANES) * LANES
        for start in range(0, padded_lanes, LANES):
            count = min(LANES, lanes - start)
            turned = jnp.transpose(full[:, start : start + LANES])
            out[start : start + count, :] = turned[:count]

    fine = mats[:, 6 * SUB * 8 : (6 * 8 + T0) * SUB]
    build(fine, 0, T0, O0, tab0)
    build(averaged(T0 * SUB, T1 * SUB, 2, fine), 1, T1, O1, tab1)
    second = averaged(wide, 3 * LANES, 4, mats[...])
    build(second[:, : T2 * SUB], 2, T2, O2, tab2)
    build(averaged(3 * LANES, 2 * LANES, 2, second)[:, : T3 * SUB], 3, T3, O3, tab3)


def split_kernel(where_ref, state_ref, forcing_ref, state_rows, forcing_rows, send_a, send_b):
    odd = where_ref[0] % 2
    for which, (source, target) in enumerate(
        ((state_ref, state_rows), (forcing_ref, forcing_rows))
    ):
        for field in range(FIELDS):
            for block in range(SUB):
                for start in range(0, OWN, SUB):
                    target[field, pl.ds(start * SUB + block, SUB, stride=SUB), :] = source[
                        field, start : start + SUB, block * LANES : (block + 1) * LANES
                    ]
    low, high = 0, (OWN - FINE_HALO) * SUB
    size = FINE_HALO * SUB
    for which, rows in enumerate((state_rows, forcing_rows)):
        for field in range(FIELDS):
            first = rows[field, low : low + size, :]
            last = rows[field, high : high + size, :]
            send_a[which * FIELDS + field] = jnp.where(odd == 1, first, last)
            send_b[which * FIELDS + field] = jnp.where(odd == 1, last, first)


def place_halo(where_ref, buffer, own_rows, got_a, got_b, first, padded):
    odd = where_ref[0] % 2
    row_a = jnp.where(odd == 1, O0 - FINE_HALO, O0 + OWN)
    row_b = jnp.where(odd == 1, O0 + OWN, O0 - FINE_HALO)

    def put_row(field, row, value):
        if padded:
            put(buffer, field, row, value)
        else:
            buffer[field, row] = value

    def own(row):
        start = pl.multiple_of(row * SUB, SUB)
        for field in range(FIELDS):
            put_row(field, O0 + row, own_rows[field, pl.ds(start, SUB), :])

    def halo(row):
        start = pl.multiple_of(row * SUB, SUB)
        for field in range(FIELDS):
            put_row(field, row_a + row, got_a[first + field, pl.ds(start, SUB), :])
            put_row(field, row_b + row, got_b[first + field, pl.ds(start, SUB), :])

    rows_loop(0, OWN, own)
    rows_loop(0, FINE_HALO, halo)


def down_kernel(fresh, *refs):
    if fresh:
        where_ref, state, force, got_a, got_b, tab0, tab1, v0, v1, s1, c1, send, f0, tmp0, tmp1, q1 = refs
    else:
        where_ref, state, got_a, got_b, f0, tab0, tab1, v0, v1, s1, c1, send, tmp0, tmp1, q1 = refs
    for ref in (v0, v1, c1, tmp0, tmp1):
        clear(ref)
    place_halo(where_ref, v0, state, got_a, got_b, 0, True)
    if fresh:
        place_halo(where_ref, f0, force, got_a, got_b, FIELDS, False)
    fine_source = lambda field, row: f0[field, row]
    low, high = O0 - FINE_HALO, O0 + OWN + FINE_HALO
    sweep(fine_source, v0, tmp0, tab0, 0, low + 1, high - 1)
    sweep(fine_source, tmp0, v0, tab0, 0, low + 2, high - 2)

    def to_first(row):
        coarse, rest = coarsen(fine_source, v0, tab0, 0, row)
        start = first_sweep(coarse, rest, tab1, row)
        for field in range(FIELDS):
            put(c1, field, row, coarse[field])
            q1[field, row] = rest[field]
            put(tmp1, field, row, start[field])

    half = OWN // 2
    rows_loop(O1 - 4, O1 + half + 4, to_first)
    make_source(c1, q1, s1, tab1, 1, O1 - 3, O1 + half + 3)
    first_source = lambda field, row: s1[field, row]
    sweep(first_source, tmp1, v1, tab1, 1, O1 - 3, O1 + half + 3)

    lane = lane_iota()

    def to_second(index):
        coarse, rest = coarsen(first_source, v1, tab1, 1, index + O1 // 2)
        group, place = index // GROUP, index % GROUP
        mine = (lane & (GROUP - 1)) == place
        for field in range(FIELDS):
            for which, value in ((field, coarse[field]), (FIELDS + field, rest[field])):
                send[group, which] = jnp.where(mine, value, send[group, which])

    clear(send)
    rows_loop(0, OWN // 4, to_second)


def spread(packed, place):
    lane = lane_iota()
    value = jnp.where((lane & (GROUP - 1)) == place, packed, 0.0)
    near = 1 if place % 2 == 0 else LANES - 1
    far = 2 if place < 2 else LANES - 2
    value = value + pltpu.roll(value, near, 1)
    return value + pltpu.roll(value, far, 1)


def up_kernel(last, *refs):
    if last:
        (where_ref, own, got_a, got_b, got_a2, v0, f0, v1, s1, c1, tab0, tab1, tab2, tab3, out,
         tmp0, work0, tmp1, work1, c2, q2, s2, v2, tmp2, c3, q3, s3, v3, tmp3) = refs
    else:
        (where_ref, own, got_a, got_b, got_a2, v0, f0, v1, s1, c1, tab0, tab1, tab2, tab3, out,
         send_a, send_b, tmp0, work0, tmp1, work1, c2, q2, s2, v2, tmp2, c3, q3, s3, v3, tmp3) = refs
    odd = where_ref[0] % 2
    for ref in (c2, v2, tmp2, c3, v3, tmp3, tmp0, tmp1):
        clear(ref)

    def unpack(source, index, group):
        for place in range(GROUP):
            row = group * GROUP + place
            coarse = [spread(source[index, f], place) for f in range(FIELDS)]
            rest = [spread(source[index, FIELDS + f], place) for f in range(FIELDS)]
            start = first_sweep(coarse, rest, tab2, row)
            for field in range(FIELDS):
                put(c2, field, row, coarse[field])
                q2[field, row] = rest[field]
                put(tmp2, field, row, start[field])

    pick = lambda a, b: jnp.where(odd == 1, b, a)
    rows_loop(0, 2, lambda i: unpack(own, i, 4 + i))
    rows_loop(0, 2, lambda i: unpack(got_a, i, pick(6, 2) + i))
    rows_loop(0, 3, lambda i: unpack(got_b, i, pick(1, 6) + i))
    rows_loop(0, 1, lambda i: unpack(got_a2, i, pick(8, 1) + i))

    quarter, eighth = OWN // 4, OWN // 8
    make_source(c2, q2, s2, tab2, 2, O2 - 11, O2 + quarter + 11)
    second_source = lambda field, row: s2[field, row]
    sweep(second_source, tmp2, v2, tab2, 2, O2 - 11, O2 + quarter + 11)

    def to_third(row):
        coarse, rest = coarsen(second_source, v2, tab2, 2, row)
        start = first_sweep(coarse, rest, tab3, row)
        for field in range(FIELDS):
            put(c3, field, row, coarse[field])
            q3[field, row] = rest[field]
            put(tmp3, field, row, start[field])

    rows_loop(O3 - 5, O3 + eighth + 5, to_third)
    make_source(c3, q3, s3, tab3, 3, O3 - 4, O3 + eighth + 4)
    third_source = lambda field, row: s3[field, row]
    sweep(third_source, tmp3, v3, tab3, 3, O3 - 4, O3 + eighth + 4)
    sweep(third_source, v3, tmp3, tab3, 3, O3 - 3, O3 + eighth + 3)
    sweep(third_source, tmp3, v3, tab3, 3, O3 - 2, O3 + eighth + 2)
    correct(v2, v3, c3, 0, O2 - 4, O2 + quarter + 4)
    sweep(second_source, v2, tmp2, tab2, 2, O2 - 3, O2 + quarter + 3)
    sweep(second_source, tmp2, v2, tab2, 2, O2 - 2, O2 + quarter + 2)

    half = OWN // 2
    work1[...] = v1[...]
    first_source = lambda field, row: s1[field, row]
    correct(work1, v2, c2, O2 - O1 // 2, O1 - 3, O1 + half + 3)
    sweep(first_source, work1, tmp1, tab1, 1, O1 - 2, O1 + half + 2)
    sweep(first_source, tmp1, work1, tab1, 1, O1 - 1, O1 + half + 1)

    work0[...] = v0[...]
    fine_source = lambda field, row: f0[field, row]
    correct(work0, work1, c1, 0, O0 - 2, O0 + OWN + 2)
    sweep(fine_source, work0, tmp0, tab0, 0, O0 - 1, O0 + OWN + 1)
    sweep(fine_source, tmp0, work0, tab0, 0, O0, O0 + OWN)

    if last:
        for field in range(FIELDS):
            for block in range(SUB):
                for start in range(0, OWN, SUB):
                    out[field, start : start + SUB, block * LANES : (block + 1) * LANES] = work0[
                        field, pl.ds(at(O0 + start) + block, SUB, stride=PAD), :
                    ]
        return

    def leave(row):
        start = pl.multiple_of(row * SUB, SUB)
        for field in range(FIELDS):
            out[field, pl.ds(start, SUB), :] = tile(work0, field, O0 + row)

    rows_loop(0, OWN, leave)
    from_a, from_b = pick(OWN - FINE_HALO, 0), pick(0, OWN - FINE_HALO)

    def edge(row):
        start = pl.multiple_of(row * SUB, SUB)
        for field in range(FIELDS):
            send_a[field, pl.ds(start, SUB), :] = tile(work0, field, O0 + from_a + row)
            send_b[field, pl.ds(start, SUB), :] = tile(work0, field, O0 + from_b + row)

    rows_loop(0, FINE_HALO, edge)


VMEM = pl.BlockSpec(memory_space=pltpu.VMEM)
SMEM = pl.BlockSpec(memory_space=pltpu.SMEM)


def f32(*shape):
    return jax.ShapeDtypeStruct(shape, jnp.float32)


def scratch(*shape):
    return pltpu.VMEM(shape, jnp.float32)


def padded(rows):
    return (FIELDS, padded_rows(rows), LANES)


def plain(rows):
    return (FIELDS, rows, SUB, LANES)


def call(kernel, name, outs, operands, scratches=()):
    return pl.pallas_call(
        kernel,
        out_shape=outs,
        in_specs=[SMEM] + [VMEM] * (len(operands) - 1),
        out_specs=[VMEM] * len(outs),
        scratch_shapes=list(scratches),
        name=name,
        compiler_params=pltpu.CompilerParams(vmem_limit_bytes=48 * 1024 * 1024),
    )(*operands)


def per_device(initial_state, forcing, coefficients, region_ids):
    size = lax.axis_size("axial")
    device = lax.axis_index("axial")
    assert initial_state.shape == (FIELDS, OWN, SUB * LANES)
    assert region_ids.shape == (OWN, SUB)
    where_ref = jnp.stack([device, jnp.int32(size)]).astype(jnp.int32)
    odd = device % 2
    pair_a = [(i, i ^ 1) for i in range(size)]
    pair_b = [(i, i + 1 if i % 2 else i - 1) for i in range(1, size - 1)]
    swap_a = lambda x: lax.ppermute(x, "axial", pair_a)
    swap_b = lambda x: lax.ppermute(x, "axial", pair_b)

    share = coefficients.shape[1]
    regions = share * size
    lanes = -(-regions // LANES) * LANES
    table = lax.dynamic_update_slice(
        jnp.zeros((32, lanes), jnp.float32),
        jnp.pad(coefficients, ((0, 32 - ENTRIES), (0, 0))),
        (0, device * share),
    )
    table = jnp.concatenate([table[:, i : i + LANES] for i in range(0, lanes, LANES)], axis=0)
    ids = lax.dynamic_update_slice(
        jnp.zeros((2 * size + 8, LANES), jnp.float32),
        region_ids.reshape(2, LANES).astype(jnp.float32),
        (2 * device + 4, 0),
    )
    gathered = jnp.concatenate([table, ids], axis=0)
    step = 1
    while step < size:
        swap = [(i, i ^ step) for i in range(size)]
        gathered = gathered + lax.ppermute(gathered, "axial", swap)
        step *= 2
    count = 32 * (lanes // LANES)
    table = jnp.concatenate([gathered[i : i + 32] for i in range(0, count, 32)], axis=1)
    near_ids = lax.dynamic_slice(gathered, (count + 2 * device, 0), (10, LANES))
    near_ids = jnp.pad(near_ids, ((0, 6), (0, 0)))

    state, force, send_a, send_b = call(
        split_kernel,
        "split",
        [f32(FIELDS, OWN * SUB, LANES)] * 2 + [f32(2 * FIELDS, FINE_HALO * SUB, LANES)] * 2,
        [where_ref, initial_state, forcing],
    )
    got_b, got_a = swap_b(send_b), swap_a(send_a)
    tables = call(
        tables_kernel,
        "tables",
        [f32(rows * SUB, LANES) for rows in (T0, T1, T2, T3)],
        [where_ref, table, near_ids],
        [scratch(32, 5 * 256), scratch(LANES, T0 * SUB)],
    )

    f0 = None
    for cycle in range(CYCLES):
        outs = [f32(*padded(T0)), f32(*padded(T1)), f32(*plain(T1)), f32(*padded(T1)),
                f32(2, 2 * FIELDS, SUB, LANES)]
        temps = [scratch(*padded(T0)), scratch(*padded(T1)), scratch(*plain(T1))]
        if cycle == 0:
            v0, v1, s1, c1, own, f0 = call(
                functools.partial(down_kernel, True), "down_fresh", outs + [f32(*plain(T0))],
                [where_ref, state, force, got_a, got_b, tables[0], tables[1]], temps,
            )
        else:
            v0, v1, s1, c1, own = call(
                functools.partial(down_kernel, False), "down", outs,
                [where_ref, state, got_a, got_b, f0, tables[0], tables[1]], temps,
            )
        beside = swap_a(own)
        row = jnp.concatenate([beside[1:], own, beside[:1]], axis=0)
        far = swap_b(lax.dynamic_slice_in_dim(row, 1 - odd, 3, axis=0))
        last_one = swap_a(lax.dynamic_slice_in_dim(far, 2 - 2 * odd, 1, axis=0))
        operands = [where_ref, own, beside, far, last_one, v0, f0, v1, s1, c1, *tables]
        temps = [scratch(*padded(T0))] * 2 + [scratch(*padded(T1))] * 2
        temps += [scratch(*padded(T2)), scratch(*plain(T2)), scratch(*plain(T2)), scratch(*padded(T2)), scratch(*padded(T2))]
        temps += [scratch(*padded(T3)), scratch(*plain(T3)), scratch(*plain(T3)), scratch(*padded(T3)), scratch(*padded(T3))]
        if cycle == CYCLES - 1:
            return call(
                functools.partial(up_kernel, True), "up_last",
                [f32(FIELDS, OWN, SUB * LANES)], operands, temps,
            )[0]
        state, send_a, send_b = call(
            functools.partial(up_kernel, False), "up",
            [f32(FIELDS, OWN * SUB, LANES)] + [f32(FIELDS, FINE_HALO * SUB, LANES)] * 2,
            operands, temps,
        )
        got_b, got_a = swap_b(send_b), swap_a(send_a)


def solution(mesh):
    placed = (
        P("sample", "axial", None),
        P("sample", "axial", None),
        P("sample", "axial"),
        P("axial", None),
    )
    return jax.shard_map(
        per_device,
        mesh=mesh,
        in_specs=placed,
        out_specs=P("sample", "axial", None),
        check_vma=False,
    )
```

```python
import functools

import jax
import jax.numpy as jnp
from jax import lax
from jax.experimental import pallas as pl
from jax.experimental.pallas import tpu as pltpu
from jax.sharding import PartitionSpec as P

DIFFUSION = 1.0
RELAXATION = 0.8
SOURCE_GAIN = 0.05
CYCLES = 2

FIELDS = 5
ENTRIES = FIELDS * FIELDS
SUB, LANES = 8, 128

OWN = 32
FINE_HALO = 11
T0, O0 = 64, 16
T1, O1 = 32, 8
T2, O2 = 40, 16
T3, O3 = 20, 8
GROUP = 4
SPREAD = 16


def stride_of(level):
    return SUB + 2 * 2**level


def padded_rows(rows, level):
    return -(-stride_of(level) * rows // SUB) * SUB


def at(row, level):
    return stride_of(level) * row + 2**level


def lane_iota():
    return lax.broadcasted_iota(jnp.int32, (SUB, LANES), 1)


def sub_iota():
    return lax.broadcasted_iota(jnp.int32, (SUB, LANES), 0)


def tile(ref, field, row, level):
    return ref[field, pl.ds(at(row, level), SUB), :]


def put(ref, field, row, level, value):
    start, width, lane = at(row, level), 2**level, lane_iota()
    before = jnp.where(lane == 0, 0.0, pltpu.roll(value, 1, 1))
    after = jnp.where(lane == LANES - 1, 0.0, pltpu.roll(value, LANES - 1, 1))
    ref[field, pl.ds(start, SUB), :] = value
    ref[field, pl.ds(start - width, width), :] = before[SUB - width :]
    ref[field, pl.ds(start + SUB, width), :] = after[:width]


def rows_loop(first, last, body):
    def step(row, carry):
        body(row)
        return carry

    lax.fori_loop(first, last, step, 0)


def batches(first, last, batch, compute, store):
    def body(index):
        rows = [first + index * batch + i for i in range(batch)]
        results = [compute(row) for row in rows]
        for row, result in zip(rows, results):
            store(row, result)

    rows_loop(0, -(-(last - first) // batch), body)


def neighbours(ref, row, level):
    start, width, stride = at(row, level), 2**level, stride_of(level)
    sums, centres = [], []
    for field in range(FIELDS):
        load = lambda first: ref[field, pl.ds(first, SUB), :]
        radial = load(start - width) + load(start + width)
        sums.append(radial + (load(start - stride) + load(start + stride)))
        centres.append(load(start))
    return sums, centres


def block_times(table, row, first, vectors):
    out = []
    for i in range(FIELDS):
        total = None
        for j in range(FIELDS):
            entry = first + FIELDS * i + j
            term = jnp.broadcast_to(table[row, entry : entry + 1, :], (SUB, LANES)) * vectors[j]
            total = term if total is None else total + term
        out.append(total)
    return out


MATRIX_AT = 32
ENTRY_ROWS = 64


def gain_of(level):
    return SOURCE_GAIN * 4.0**level / DIFFUSION


def sweep(source_of, old, new, table, level, first, last):
    gain = gain_of(level)

    def compute(row):
        sums, centres = neighbours(old, row, level)
        rest = [
            (source_of(field, row) + sums[field]) - gain * jnp.tanh(centres[field])
            for field in range(FIELDS)
        ]
        moved = block_times(table, row, 0, rest)
        return [(1.0 - RELAXATION) * centres[f] + moved[f] for f in range(FIELDS)]

    def store(row, values):
        for field in range(FIELDS):
            put(new, field, row, level, values[field])

    batches(first, last, SWEEP_BATCH, compute, store)


def residual(source_of, values, table, level, row):
    gain = gain_of(level)
    sums, centres = neighbours(values, row, level)
    applied = block_times(table, row, MATRIX_AT, centres)
    left = [
        ((source_of(field, row) + sums[field]) - gain * jnp.tanh(centres[field])) - applied[field]
        for field in range(FIELDS)
    ]
    return left, centres


def pair_sum(value, level):
    width = 2**level
    other = pltpu.roll(value, SUB - width, 0)
    if 2 * width != SUB:
        other = jnp.where((sub_iota() & width) == 0, other, pltpu.roll(value, width, 0))
    return value + other


def coarsen(source_of, values, table, level, row):
    upper_r, upper_v = residual(source_of, values, table, level, 2 * row)
    lower_r, lower_v = residual(source_of, values, table, level, 2 * row + 1)
    coarse = [0.25 * pair_sum(upper_v[f] + lower_v[f], level) for f in range(FIELDS)]
    rest = [pair_sum(upper_r[f] + lower_r[f], level) for f in range(FIELDS)]
    return coarse, rest


def first_sweep(coarse, rest, table, row):
    moved = block_times(table, row, 0, rest)
    return [coarse[f] + moved[f] for f in range(FIELDS)]


def descend(source_of, values, table, level, c, q, first_values, coarse_table, first, last):
    def compute(row):
        coarse, rest = coarsen(source_of, values, table, level, row)
        return coarse, rest, first_sweep(coarse, rest, coarse_table, row)

    def store(row, results):
        for field in range(FIELDS):
            put(c, field, row, level + 1, results[0][field])
            q[field, row] = results[1][field]
            put(first_values, field, row, level + 1, results[2][field])

    batches(first, last, COARSEN_BATCH, compute, store)


def make_source(coarse, rest, source, table, level, first, last):
    gain = gain_of(level)

    def compute(row):
        sums, centres = neighbours(coarse, row, level)
        applied = block_times(table, row, MATRIX_AT, centres)
        return [
            (applied[f] - sums[f]) + (gain * jnp.tanh(centres[f]) + rest[f, row])
            for f in range(FIELDS)
        ]

    def store(row, values):
        for field in range(FIELDS):
            source[field, row] = values[field]

    batches(first, last, SWEEP_BATCH, compute, store)


def correct(new, fine, after, before, level, offset, first, last):
    def body(index):
        coarse_row = first // 2 + index + offset
        row = first // 2 * 2 + 2 * index
        for field in range(FIELDS):
            change = tile(after, field, coarse_row, level + 1) - tile(before, field, coarse_row, level + 1)
            put(new, field, row, level, tile(fine, field, row, level) + change)
            put(new, field, row + 1, level, tile(fine, field, row + 1, level) + change)

    rows_loop(0, (last + 1) // 2 - first // 2, body)


SWEEP_BATCH = 4
COARSEN_BATCH = 2


def tables_kernel(where_ref, coeff_ref, ids_ref, tab0, tab1, tab2, tab3, mats, full):
    device, devices = where_ref[0], where_ref[1]
    regions = coeff_ref.shape[1]
    wide = 5 * 256
    exact = lax.Precision.HIGHEST
    region = lax.broadcasted_iota(jnp.int32, (regions, LANES), 0)
    coeff = coeff_ref[...]
    for chunk in range(10):
        ids = jnp.broadcast_to(ids_ref[chunk : chunk + 1, :], (regions, LANES)).astype(jnp.int32)
        chosen = (region == ids).astype(jnp.float32)
        mats[:, chunk * LANES : (chunk + 1) * LANES] = jnp.dot(
            coeff, chosen, precision=exact, preferred_element_type=jnp.float32
        )

    def averaged(lanes_in, lanes_out, span, source):
        into = lax.broadcasted_iota(jnp.int32, (lanes_in, lanes_out), 0)
        out = lax.broadcasted_iota(jnp.int32, (lanes_in, lanes_out), 1)
        same = (into // (SUB * span) == out // SUB) & ((into % SUB) == (out % SUB))
        average = jnp.where(same, 1.0 / span, 0.0).astype(jnp.float32)
        return jnp.dot(source, average, precision=exact, preferred_element_type=jnp.float32)

    def build(matrix, level, rows, own_first, out):
        lanes = rows * SUB
        weight = DIFFUSION / 4.0**level
        row = lax.broadcasted_iota(jnp.int32, (SUB, lanes), 1) // SUB
        own = OWN >> level
        whole = (row - own_first) + device * own
        inside = (whole >= 0) & (whole < devices * own)
        full[:, :lanes] = jnp.zeros((ENTRY_ROWS, lanes), jnp.float32)
        full[0:32, :lanes] = matrix
        entry = lambda e: jnp.broadcast_to(full[e : e + 1, :lanes], (SUB, lanes))
        block = [[entry(FIELDS * i + j) for j in range(FIELDS)] for i in range(FIELDS)]
        for i in range(FIELDS):
            block[i][i] = block[i][i] + 4.0 * weight
        for i in range(FIELDS):
            for j in range(FIELDS):
                e = MATRIX_AT + FIELDS * i + j
                full[e : e + 1, :lanes] = (block[i][j] * (1.0 / weight))[0:1]
        right = [[None] * FIELDS for _ in range(FIELDS)]
        for i in range(FIELDS):
            right[i][i] = jnp.ones((SUB, lanes), jnp.float32)
        for c in range(FIELDS):
            lead = 1.0 / block[c][c]
            for j in range(c + 1, FIELDS):
                block[c][j] = block[c][j] * lead
            for j in range(FIELDS):
                if right[c][j] is not None:
                    right[c][j] = right[c][j] * lead
            for i in range(FIELDS):
                if i == c:
                    continue
                factor = block[i][c]
                for j in range(c + 1, FIELDS):
                    block[i][j] = block[i][j] - factor * block[c][j]
                for j in range(FIELDS):
                    if right[c][j] is not None:
                        term = factor * right[c][j]
                        right[i][j] = -term if right[i][j] is None else right[i][j] - term
        for i in range(FIELDS):
            for j in range(FIELDS):
                e = FIELDS * i + j
                scaled = jnp.where(inside, right[i][j] * (RELAXATION * weight), 0.0)
                full[e : e + 1, :lanes] = scaled[0:1]
        block_of = lax.broadcasted_iota(jnp.int32, (SUB, LANES), 1) // SPREAD

        def widen(place):
            lane_of = place * SUB + block_of
            for start in range(0, rows, LANES // SUB):

                def one():
                    chunk = start * SUB
                    for entry in range(0, ENTRY_ROWS, SUB):
                        out[start + place, entry : entry + SUB, :] = jnp.take_along_axis(
                            full[entry : entry + SUB, chunk : chunk + LANES], lane_of, axis=1
                        )

                if start + LANES // SUB <= rows:
                    one()
                else:
                    pl.when(start + place < rows)(one)

        rows_loop(0, LANES // SUB, widen)

    fine = mats[:, 6 * SUB * 8 : (6 * 8 + T0) * SUB]
    build(fine, 0, T0, O0, tab0)
    build(averaged(T0 * SUB, T1 * SUB, 2, fine), 1, T1, O1, tab1)
    second = averaged(wide, 3 * LANES, 4, mats[...])
    build(second[:, : T2 * SUB], 2, T2, O2, tab2)
    build(averaged(3 * LANES, 2 * LANES, 2, second)[:, : T3 * SUB], 3, T3, O3, tab3)


def turn(inward):
    into = lax.broadcasted_iota(jnp.int32, (LANES, LANES), 0 if inward else 1)
    out = lax.broadcasted_iota(jnp.int32, (LANES, LANES), 1 if inward else 0)
    return ((into % SUB) * SPREAD + into // SUB == out).astype(jnp.float32)


def swap_chunks(tiles):
    chunk = lax.broadcasted_iota(jnp.int32, tiles[0].shape, 1) // SPREAD
    tiles = list(tiles)
    for bit in (1, 2, 4):
        shift = bit * SPREAD
        for i in range(SUB):
            if i & bit:
                continue
            low, high = tiles[i], tiles[i | bit]
            keep = (chunk & bit) == 0
            tiles[i] = jnp.where(keep, low, pltpu.roll(high, shift, 1))
            tiles[i | bit] = jnp.where(keep, pltpu.roll(low, LANES - shift, 1), high)
    return tiles


def reordered(value, matrix):
    return jnp.dot(value, matrix, precision=lax.Precision.HIGHEST, preferred_element_type=jnp.float32)


def split_kernel(where_ref, state_ref, forcing_ref, state_rows, forcing_rows, send_a, send_b):
    odd = where_ref[0] % 2
    matrix = turn(True)
    for source, target in ((state_ref, state_rows), (forcing_ref, forcing_rows)):
        for field in range(FIELDS):
            blocks = [
                reordered(source[field, :, b * LANES : (b + 1) * LANES], matrix) for b in range(SUB)
            ]
            for sub, value in enumerate(swap_chunks(blocks)):
                target[field, pl.ds(sub, OWN, stride=SUB), :] = value
    low, high = 0, (OWN - FINE_HALO) * SUB
    size = FINE_HALO * SUB
    for which, rows in enumerate((state_rows, forcing_rows)):
        for field in range(FIELDS):
            first = rows[field, low : low + size, :]
            last = rows[field, high : high + size, :]
            send_a[which * FIELDS + field] = jnp.where(odd == 1, first, last)
            send_b[which * FIELDS + field] = jnp.where(odd == 1, last, first)


def place_halo(where_ref, buffer, own_rows, got_a, got_b, first, padded):
    odd = where_ref[0] % 2
    row_a = jnp.where(odd == 1, O0 - FINE_HALO, O0 + OWN)
    row_b = jnp.where(odd == 1, O0 + OWN, O0 - FINE_HALO)

    def put_row(field, row, value):
        if padded:
            put(buffer, field, row, 0, value)
        else:
            buffer[field, row] = value

    def own(row):
        start = pl.multiple_of(row * SUB, SUB)
        for field in range(FIELDS):
            put_row(field, O0 + row, own_rows[field, pl.ds(start, SUB), :])

    def halo(row):
        start = pl.multiple_of(row * SUB, SUB)
        for field in range(FIELDS):
            put_row(field, row_a + row, got_a[first + field, pl.ds(start, SUB), :])
            put_row(field, row_b + row, got_b[first + field, pl.ds(start, SUB), :])

    rows_loop(0, OWN, own)
    rows_loop(0, FINE_HALO, halo)


def down_kernel(fresh, *refs):
    if fresh:
        where_ref, state, force, got_a, got_b, tab0, tab1, v0, v1, s1, c1, send, f0, tmp0, tmp1, q1 = refs
    else:
        where_ref, state, got_a, got_b, f0, tab0, tab1, v0, v1, s1, c1, send, tmp0, tmp1, q1 = refs
    place_halo(where_ref, v0, state, got_a, got_b, 0, True)
    if fresh:
        place_halo(where_ref, f0, force, got_a, got_b, FIELDS, False)
    fine_source = lambda field, row: f0[field, row]
    low, high = O0 - FINE_HALO, O0 + OWN + FINE_HALO
    sweep(fine_source, v0, tmp0, tab0, 0, low + 1, high - 1)
    sweep(fine_source, tmp0, v0, tab0, 0, low + 2, high - 2)

    half = OWN // 2
    descend(fine_source, v0, tab0, 0, c1, q1, tmp1, tab1, O1 - 4, O1 + half + 4)
    make_source(c1, q1, s1, tab1, 1, O1 - 3, O1 + half + 3)
    first_source = lambda field, row: s1[field, row]
    sweep(first_source, tmp1, v1, tab1, 1, O1 - 3, O1 + half + 3)

    sub = sub_iota()

    def to_second(index):
        coarse, rest = coarsen(first_source, v1, tab1, 1, index + O1 // 2)
        return coarse + rest

    def pack(index, values):
        group, place = index // GROUP, index % GROUP
        mine = (sub & (GROUP - 1)) == place
        for which in range(2 * FIELDS):
            send[group, which] = jnp.where(mine, values[which], send[group, which])

    send[...] = jnp.zeros_like(send)
    batches(0, OWN // 4, COARSEN_BATCH, to_second, pack)


def spread(source, index, which, place):
    take = lambda sub: jnp.broadcast_to(source[index, which, sub : sub + 1, :], (SUB, LANES))
    return jnp.where(sub_iota() < GROUP, take(place), take(GROUP + place))


def up_kernel(last, *refs):
    if last:
        (where_ref, own, got_a, got_b, got_a2, v0, f0, v1, s1, c1, tab0, tab1, tab2, tab3, out,
         tmp0, work0, tmp1, work1, c2, q2, s2, v2, tmp2, c3, q3, s3, v3, tmp3) = refs
    else:
        (where_ref, own, got_a, got_b, got_a2, v0, f0, v1, s1, c1, tab0, tab1, tab2, tab3, out,
         send_a, send_b, tmp0, work0, tmp1, work1, c2, q2, s2, v2, tmp2, c3, q3, s3, v3, tmp3) = refs
    odd = where_ref[0] % 2

    def unpack(source, index, group):
        for place in range(GROUP):
            row = group * GROUP + place
            coarse = [spread(source, index, f, place) for f in range(FIELDS)]
            rest = [spread(source, index, FIELDS + f, place) for f in range(FIELDS)]
            start = first_sweep(coarse, rest, tab2, row)
            for field in range(FIELDS):
                put(c2, field, row, 2, coarse[field])
                q2[field, row] = rest[field]
                put(tmp2, field, row, 2, start[field])

    pick = lambda a, b: jnp.where(odd == 1, b, a)
    rows_loop(0, 2, lambda i: unpack(own, i, 4 + i))
    rows_loop(0, 2, lambda i: unpack(got_a, i, pick(6, 2) + i))
    rows_loop(0, 3, lambda i: unpack(got_b, i, pick(1, 6) + i))
    rows_loop(0, 1, lambda i: unpack(got_a2, i, pick(8, 1) + i))

    quarter, eighth = OWN // 4, OWN // 8
    make_source(c2, q2, s2, tab2, 2, O2 - 11, O2 + quarter + 11)
    second_source = lambda field, row: s2[field, row]
    sweep(second_source, tmp2, v2, tab2, 2, O2 - 11, O2 + quarter + 11)

    descend(second_source, v2, tab2, 2, c3, q3, tmp3, tab3, O3 - 5, O3 + eighth + 5)
    make_source(c3, q3, s3, tab3, 3, O3 - 4, O3 + eighth + 4)
    third_source = lambda field, row: s3[field, row]
    sweep(third_source, tmp3, v3, tab3, 3, O3 - 4, O3 + eighth + 4)
    sweep(third_source, v3, tmp3, tab3, 3, O3 - 3, O3 + eighth + 3)
    sweep(third_source, tmp3, v3, tab3, 3, O3 - 2, O3 + eighth + 2)
    correct(v2, v2, v3, c3, 2, 0, O2 - 4, O2 + quarter + 4)
    sweep(second_source, v2, tmp2, tab2, 2, O2 - 3, O2 + quarter + 3)
    sweep(second_source, tmp2, v2, tab2, 2, O2 - 2, O2 + quarter + 2)

    half = OWN // 2
    first_source = lambda field, row: s1[field, row]
    correct(work1, v1, v2, c2, 1, O2 - O1 // 2, O1 - 3, O1 + half + 3)
    sweep(first_source, work1, tmp1, tab1, 1, O1 - 2, O1 + half + 2)
    sweep(first_source, tmp1, work1, tab1, 1, O1 - 1, O1 + half + 1)

    fine_source = lambda field, row: f0[field, row]
    correct(work0, v0, work1, c1, 0, 0, O0 - 2, O0 + OWN + 2)
    sweep(fine_source, work0, tmp0, tab0, 0, O0 - 1, O0 + OWN + 1)
    sweep(fine_source, tmp0, work0, tab0, 0, O0, O0 + OWN)

    if last:
        matrix = turn(False)
        for field in range(FIELDS):
            tiles = [
                work0[field, pl.ds(at(O0, 0) + sub, OWN, stride=stride_of(0)), :] for sub in range(SUB)
            ]
            for block, value in enumerate(swap_chunks(tiles)):
                out[field, :, block * LANES : (block + 1) * LANES] = reordered(value, matrix)
        return

    def leave(row):
        start = pl.multiple_of(row * SUB, SUB)
        for field in range(FIELDS):
            out[field, pl.ds(start, SUB), :] = tile(work0, field, O0 + row, 0)

    rows_loop(0, OWN, leave)
    from_a, from_b = pick(OWN - FINE_HALO, 0), pick(0, OWN - FINE_HALO)

    def edge(row):
        start = pl.multiple_of(row * SUB, SUB)
        for field in range(FIELDS):
            send_a[field, pl.ds(start, SUB), :] = tile(work0, field, O0 + from_a + row, 0)
            send_b[field, pl.ds(start, SUB), :] = tile(work0, field, O0 + from_b + row, 0)

    rows_loop(0, FINE_HALO, edge)


VMEM = pl.BlockSpec(memory_space=pltpu.VMEM)
SMEM = pl.BlockSpec(memory_space=pltpu.SMEM)


def f32(*shape):
    return jax.ShapeDtypeStruct(shape, jnp.float32)


def scratch(*shape):
    return pltpu.VMEM(shape, jnp.float32)


def padded(rows, level):
    return (FIELDS, padded_rows(rows, level), LANES)


def plain(rows):
    return (FIELDS, rows, SUB, LANES)


def call(kernel, name, outs, operands, scratches=()):
    return pl.pallas_call(
        kernel,
        out_shape=outs,
        in_specs=[SMEM] + [VMEM] * (len(operands) - 1),
        out_specs=[VMEM] * len(outs),
        scratch_shapes=list(scratches),
        name=name,
        compiler_params=pltpu.CompilerParams(vmem_limit_bytes=48 * 1024 * 1024),
    )(*operands)


def per_device(initial_state, forcing, coefficients, region_ids):
    size = lax.axis_size("axial")
    device = lax.axis_index("axial")
    assert initial_state.shape == (FIELDS, OWN, SUB * LANES)
    assert region_ids.shape == (OWN, SUB)
    where_ref = jnp.stack([device, jnp.int32(size)]).astype(jnp.int32)
    odd = device % 2
    pair_a = [(i, i ^ 1) for i in range(size)]
    pair_b = [(i, i + 1 if i % 2 else i - 1) for i in range(1, size - 1)]
    swap_a = lambda x: lax.ppermute(x, "axial", pair_a)
    swap_b = lambda x: lax.ppermute(x, "axial", pair_b)

    share = coefficients.shape[1]
    regions = share * size
    lanes = -(-regions // LANES) * LANES
    table = lax.dynamic_update_slice(
        jnp.zeros((32, lanes), jnp.float32),
        jnp.pad(coefficients, ((0, 32 - ENTRIES), (0, 0))),
        (0, device * share),
    )
    table = jnp.concatenate([table[:, i : i + LANES] for i in range(0, lanes, LANES)], axis=0)
    ids = lax.dynamic_update_slice(
        jnp.zeros((2 * size + 8, LANES), jnp.float32),
        region_ids.reshape(2, LANES).astype(jnp.float32),
        (2 * device + 4, 0),
    )
    gathered = jnp.concatenate([table, ids], axis=0)
    step = 1
    while step < size:
        swap = [(i, i ^ step) for i in range(size)]
        gathered = gathered + lax.ppermute(gathered, "axial", swap)
        step *= 2
    count = 32 * (lanes // LANES)
    table = jnp.concatenate([gathered[i : i + 32] for i in range(0, count, 32)], axis=1)
    near_ids = lax.dynamic_slice(gathered, (count + 2 * device, 0), (10, LANES))
    near_ids = jnp.pad(near_ids, ((0, 6), (0, 0)))

    state, force, send_a, send_b = call(
        split_kernel,
        "split",
        [f32(FIELDS, OWN * SUB, LANES)] * 2 + [f32(2 * FIELDS, FINE_HALO * SUB, LANES)] * 2,
        [where_ref, initial_state, forcing],
    )
    got_b, got_a = swap_b(send_b), swap_a(send_a)
    tables = call(
        tables_kernel,
        "tables",
        [f32(rows, ENTRY_ROWS, LANES) for rows in (T0, T1, T2, T3)],
        [where_ref, table, near_ids],
        [scratch(32, 5 * 256), scratch(ENTRY_ROWS, T0 * SUB)],
    )

    f0 = None
    for cycle in range(CYCLES):
        outs = [f32(*padded(T0, 0)), f32(*padded(T1, 1)), f32(*plain(T1)), f32(*padded(T1, 1)),
                f32(2, 2 * FIELDS, SUB, LANES)]
        temps = [scratch(*padded(T0, 0)), scratch(*padded(T1, 1)), scratch(*plain(T1))]
        if cycle == 0:
            v0, v1, s1, c1, own, f0 = call(
                functools.partial(down_kernel, True), "down_fresh", outs + [f32(*plain(T0))],
                [where_ref, state, force, got_a, got_b, tables[0], tables[1]], temps,
            )
        else:
            v0, v1, s1, c1, own = call(
                functools.partial(down_kernel, False), "down", outs,
                [where_ref, state, got_a, got_b, f0, tables[0], tables[1]], temps,
            )
        beside = swap_a(own)
        row = jnp.concatenate([beside[1:], own, beside[:1]], axis=0)
        far = swap_b(lax.dynamic_slice_in_dim(row, 1 - odd, 3, axis=0))
        last_one = swap_a(lax.dynamic_slice_in_dim(far, 2 - 2 * odd, 1, axis=0))
        operands = [where_ref, own, beside, far, last_one, v0, f0, v1, s1, c1, *tables]
        temps = [scratch(*padded(T0, 0))] * 2 + [scratch(*padded(T1, 1))] * 2
        temps += [scratch(*padded(T2, 2)), scratch(*plain(T2)), scratch(*plain(T2)), scratch(*padded(T2, 2)), scratch(*padded(T2, 2))]
        temps += [scratch(*padded(T3, 3)), scratch(*plain(T3)), scratch(*plain(T3)), scratch(*padded(T3, 3)), scratch(*padded(T3, 3))]
        if cycle == CYCLES - 1:
            return call(
                functools.partial(up_kernel, True), "up_last",
                [f32(FIELDS, OWN, SUB * LANES)], operands, temps,
            )[0]
        state, send_a, send_b = call(
            functools.partial(up_kernel, False), "up",
            [f32(FIELDS, OWN * SUB, LANES)] + [f32(FIELDS, FINE_HALO * SUB, LANES)] * 2,
            operands, temps,
        )
        got_b, got_a = swap_b(send_b), swap_a(send_a)


def solution(mesh):
    placed = (
        P("sample", "axial", None),
        P("sample", "axial", None),
        P("sample", "axial"),
        P("axial", None),
    )
    return jax.shard_map(
        per_device,
        mesh=mesh,
        in_specs=placed,
        out_specs=P("sample", "axial", None),
        check_vma=False,
    )
```

```python
import functools

import jax
import jax.numpy as jnp
from jax import lax
from jax.experimental import pallas as pl
from jax.experimental.pallas import tpu as pltpu
from jax.sharding import PartitionSpec as P

DIFFUSION = 1.0
RELAXATION = 0.8
SOURCE_GAIN = 0.05
CYCLES = 2

FIELDS = 5
ENTRIES = FIELDS * FIELDS
SUB, LANES = 8, 128

OWN = 32
FINE_HALO = 11
T0, O0 = 64, 16
T1, O1 = 32, 8
T2, O2 = 40, 16
T3, O3 = 20, 8
GROUP = 4
SPREAD = 16


def stride_of(level):
    return SUB + 2 * 2**level


def padded_rows(rows, level):
    return stride_of(level) * (rows + SUB)


def at(row, level):
    return stride_of(level) * row + 2**level


def lane_iota():
    return lax.broadcasted_iota(jnp.int32, (SUB, LANES), 1)


def sub_iota():
    return lax.broadcasted_iota(jnp.int32, (SUB, LANES), 0)


def tile(ref, field, row, level):
    return ref[field, pl.ds(at(row, level), SUB), :]


def put(ref, field, row, level, value):
    ref[field, pl.ds(at(row, level), SUB), :] = value


def edges(ref, level, first, last):
    width, stride, lane = 2**level, stride_of(level), lane_iota()
    for row in range(first, last, SUB):
        start = at(row, level)
        for field in range(FIELDS):
            rows = lambda sub: (field, pl.ds(start + sub, SUB, stride=stride), slice(None))
            before = jnp.where(lane == 0, 0.0, pltpu.roll(ref[rows(SUB - 1)], 1, 1))
            after = jnp.where(lane == LANES - 1, 0.0, pltpu.roll(ref[rows(0)], LANES - 1, 1))
            for i in range(width):
                ref[rows(i - width)] = before
                ref[rows(SUB + i)] = after


def rows_loop(first, last, body):
    def step(row, carry):
        body(row)
        return carry

    lax.fori_loop(first, last, step, 0)


def batches(first, last, batch, compute, store):
    def body(index):
        rows = [first + index * batch + i for i in range(batch)]
        results = [compute(row) for row in rows]
        for row, result in zip(rows, results):
            store(row, result)

    rows_loop(0, -(-(last - first) // batch), body)


def neighbours(ref, row, level):
    start, width, stride = at(row, level), 2**level, stride_of(level)
    sums, centres = [], []
    for field in range(FIELDS):
        load = lambda first: ref[field, pl.ds(first, SUB), :]
        radial = load(start - width) + load(start + width)
        sums.append(radial + (load(start - stride) + load(start + stride)))
        centres.append(load(start))
    return sums, centres


def block_times(table, level, row, first, vectors):
    row = TABLE_AT[level] + row
    out = []
    for i in range(FIELDS):
        total = None
        for j in range(FIELDS):
            entry = first + FIELDS * i + j
            term = jnp.broadcast_to(table[entry, pl.ds(row, 1), :], (SUB, LANES)) * vectors[j]
            total = term if total is None else total + term
        out.append(total)
    return out


MATRIX_AT = ENTRIES
TABLE_AT = (0, T0, T0 + T1, T0 + T1 + T2)
TABLE_ROWS = 160
NEAR = 5


def gain_of(level):
    return SOURCE_GAIN * 4.0**level / DIFFUSION


def sweep(source_of, old, new, table, level, first, last, more=True):
    gain = gain_of(level)

    def compute(row):
        sums, centres = neighbours(old, row, level)
        rest = [
            (source_of(field, row) + sums[field]) - gain * jnp.tanh(centres[field])
            for field in range(FIELDS)
        ]
        moved = block_times(table, level, row, 0, rest)
        return [(1.0 - RELAXATION) * centres[f] + moved[f] for f in range(FIELDS)]

    def store(row, values):
        for field in range(FIELDS):
            put(new, field, row, level, values[field])

    batches(first, last, SWEEP_BATCH, compute, store)
    if more:
        edges(new, level, first, last)


def residual(source_of, values, table, level, row):
    gain = gain_of(level)
    sums, centres = neighbours(values, row, level)
    applied = block_times(table, level, row, MATRIX_AT, centres)
    left = [
        ((source_of(field, row) + sums[field]) - gain * jnp.tanh(centres[field])) - applied[field]
        for field in range(FIELDS)
    ]
    return left, centres


def pair_sum(value, level):
    width = 2**level
    other = pltpu.roll(value, SUB - width, 0)
    if 2 * width != SUB:
        other = jnp.where((sub_iota() & width) == 0, other, pltpu.roll(value, width, 0))
    return value + other


def coarsen(source_of, values, table, level, row):
    upper_r, upper_v = residual(source_of, values, table, level, 2 * row)
    lower_r, lower_v = residual(source_of, values, table, level, 2 * row + 1)
    coarse = [0.25 * pair_sum(upper_v[f] + lower_v[f], level) for f in range(FIELDS)]
    rest = [pair_sum(upper_r[f] + lower_r[f], level) for f in range(FIELDS)]
    return coarse, rest


def first_sweep(coarse, rest, table, level, row):
    moved = block_times(table, level, row, 0, rest)
    return [coarse[f] + moved[f] for f in range(FIELDS)]


def descend(source_of, values, table, level, c, q, first_values, first, last):
    def compute(row):
        coarse, rest = coarsen(source_of, values, table, level, row)
        return coarse, rest, first_sweep(coarse, rest, table, level + 1, row)

    def store(row, results):
        for field in range(FIELDS):
            put(c, field, row, level + 1, results[0][field])
            q[field, row] = results[1][field]
            put(first_values, field, row, level + 1, results[2][field])

    batches(first, last, COARSEN_BATCH, compute, store)
    edges(c, level + 1, first, last)
    edges(first_values, level + 1, first, last)


def make_source(coarse, rest, source, table, level, first, last):
    gain = gain_of(level)

    def compute(row):
        sums, centres = neighbours(coarse, row, level)
        applied = block_times(table, level, row, MATRIX_AT, centres)
        return [
            (applied[f] - sums[f]) + (gain * jnp.tanh(centres[f]) + rest[f, row])
            for f in range(FIELDS)
        ]

    def store(row, values):
        for field in range(FIELDS):
            source[field, row] = values[field]

    batches(first, last, SWEEP_BATCH, compute, store)


def correct(new, fine, after, before, level, offset, first, last):
    def body(index):
        coarse_row = first // 2 + index + offset
        row = first // 2 * 2 + 2 * index
        for field in range(FIELDS):
            change = tile(after, field, coarse_row, level + 1) - tile(before, field, coarse_row, level + 1)
            put(new, field, row, level, tile(fine, field, row, level) + change)
            put(new, field, row + 1, level, tile(fine, field, row + 1, level) + change)

    rows_loop(0, (last + 1) // 2 - first // 2, body)
    edges(new, level, first, last)


SWEEP_BATCH = 4
COARSEN_BATCH = 2


def three_parts(value):
    high = value.astype(jnp.bfloat16)
    rest = value - high.astype(jnp.float32)
    middle = rest.astype(jnp.bfloat16)
    low = (rest - middle.astype(jnp.float32)).astype(jnp.bfloat16)
    return high, middle, low


def dot(left, right):
    return jnp.dot(left, right, preferred_element_type=jnp.float32)


def tables_kernel(regions, where_ref, regions_ref, table, mats, parts):
    device, devices = where_ref[0], where_ref[1]
    wide = 2 * LANES
    lane = lane_iota()
    ids = [jnp.full((SUB, LANES), -1.0, jnp.float32)] * 2
    per_tile = LANES // OWN
    for i in range(NEAR):
        owner = jnp.clip(device + (i - NEAR // 2), 0, devices - 1)
        start = pl.multiple_of(regions + owner // per_tile * SUB, SUB)
        held = regions_ref[pl.ds(start, SUB), :]
        turned = pltpu.roll(held, ((i % per_tile) - owner % per_tile + per_tile) % per_tile * OWN, 1)
        place = i // per_tile
        ids[place] = jnp.where(lane // OWN == i % per_tile, turned, ids[place])
    ids = jnp.concatenate(ids, axis=1).astype(jnp.int32)

    coefficients = jnp.transpose(regions_ref[0:regions, :])[0:32]
    coefficients = jnp.concatenate(three_parts(coefficients), axis=0)
    region = lax.broadcasted_iota(jnp.int32, (regions, wide), 0)
    for block in range(SUB):
        chosen = region == jnp.broadcast_to(ids[block : block + 1], (regions, wide))
        found = dot(coefficients, chosen.astype(jnp.float32).astype(jnp.bfloat16))
        found = (found[0:32] + found[32:64]) + found[64:96]
        for half in range(2):
            mats[half, pl.ds(block, 32, stride=SUB), :] = found[:, half * LANES : (half + 1) * LANES]

    fine = lax.broadcasted_iota(jnp.int32, (wide, wide), 0)
    out = lax.broadcasted_iota(jnp.int32, (wide, wide), 1)
    average = jnp.zeros((wide, wide), jnp.float32)
    own_at = NEAR // 2 * OWN
    for level, (first_own, rows) in enumerate(((O0, T0), (O1, T1), (O2, T2), (O3, T3))):
        span = 2**level
        row = out - TABLE_AT[level]
        same = (row >= 0) & (row < rows) & (fine // span == row + (own_at // span - first_own))
        average = jnp.where(same, 1.0 / span, average)
    average = average.astype(jnp.bfloat16)
    used = SUB * ENTRIES
    high, middle, low = three_parts(jnp.concatenate([mats[0, 0:used], mats[1, 0:used]], axis=1))
    levels = (dot(high, average) + dot(middle, average)) + dot(low, average)

    row = lax.broadcasted_iota(jnp.int32, (SUB, wide), 1)
    weight = jnp.zeros((SUB, wide), jnp.float32) + DIFFUSION
    whole = jnp.zeros((SUB, wide), jnp.int32)
    limit = jnp.zeros((SUB, wide), jnp.int32)
    for level, first_own in enumerate((O0, O1, O2, O3)):
        here = row >= TABLE_AT[level]
        weight = jnp.where(here, DIFFUSION / 4.0**level, weight)
        whole = jnp.where(here, row - TABLE_AT[level] - first_own + device * (OWN >> level), whole)
        limit = jnp.where(here, devices * (OWN >> level), limit)
    inside = (whole >= 0) & (whole < limit)
    scale = jnp.where(inside, RELAXATION * weight, 0.0)
    unscale = 1.0 / weight

    n = FIELDS
    block = [[levels[SUB * (n * i + j) : SUB * (n * i + j + 1)] for j in range(n)] for i in range(n)]
    for i in range(n):
        block[i][i] = block[i][i] + 4.0 * weight
    entries = [block[i][j] * unscale for i in range(n) for j in range(n)]
    right = [[None] * n for _ in range(n)]
    for i in range(n):
        right[i][i] = jnp.ones((SUB, wide), jnp.float32)
    for c in range(n):
        lead = 1.0 / block[c][c]
        for j in range(c + 1, n):
            block[c][j] = block[c][j] * lead
        for j in range(n):
            if right[c][j] is not None:
                right[c][j] = right[c][j] * lead
        for i in range(n):
            if i == c:
                continue
            factor = block[i][c]
            for j in range(c + 1, n):
                block[i][j] = block[i][j] - factor * block[c][j]
            for j in range(n):
                if right[c][j] is not None:
                    term = factor * right[c][j]
                    right[i][j] = -term if right[i][j] is None else right[i][j] - term
    entries = [right[i][j] * scale for i in range(n) for j in range(n)] + entries

    group = FIELDS
    into = lax.broadcasted_iota(jnp.int32, (LANES, group * LANES), 0)
    out = lax.broadcasted_iota(jnp.int32, (LANES, group * LANES), 1)
    same = (into // (3 * SUB) == out // LANES) & (into % SUB == out % LANES // SPREAD)
    widen = same.astype(jnp.float32).astype(jnp.bfloat16)
    parts[...] = jnp.zeros_like(parts)
    for first in range(0, len(entries), group):
        for i in range(group):
            for p, part in enumerate(three_parts(entries[first + i])):
                start = (3 * i + p) * SUB
                parts[start : start + SUB, :] = part.astype(jnp.float32)
        turned = jnp.transpose(parts[...])[0:TABLE_ROWS].astype(jnp.bfloat16)
        wide_rows = dot(turned, widen)
        for i in range(group):
            table[first + i] = wide_rows[:, i * LANES : (i + 1) * LANES]


def turn(first_sub, inward):
    shape = (SUB * LANES, 2 * LANES)
    into = lax.broadcasted_iota(jnp.int32, shape, 0)
    out = lax.broadcasted_iota(jnp.int32, shape, 1)
    if inward:
        wanted = (out % LANES) * SUB + first_sub + out // LANES
    else:
        cell = out + first_sub * LANES
        wanted = (cell % SUB) * LANES + cell // SUB
    return (into == wanted).astype(jnp.float32).astype(jnp.bfloat16)


def split_kernel(where_ref, state_ref, forcing_ref, state_rows, forcing_rows, send_a, send_b, parts):
    odd = where_ref[0] % 2
    held = 2 * FIELDS * OWN
    for which, source in enumerate((state_ref, forcing_ref)):
        for field in range(FIELDS):
            for p, part in enumerate(three_parts(source[field])):
                start = p * held + (which * FIELDS + field) * OWN
                parts[start : start + OWN, :] = part

    def two_subs(index):
        values = dot(parts[...], turn(2 * index, True))
        values = (values[:held] + values[held : 2 * held]) + values[2 * held :]
        for which, target in enumerate((state_rows, forcing_rows)):
            for field in range(FIELDS):
                start = (which * FIELDS + field) * OWN
                for half in range(2):
                    target[field, pl.ds(2 * index + half, OWN, stride=SUB), :] = values[
                        start : start + OWN, half * LANES : (half + 1) * LANES
                    ]

    rows_loop(0, SUB // 2, two_subs)
    low, high = 0, (OWN - FINE_HALO) * SUB
    size = FINE_HALO * SUB
    for which, rows in enumerate((state_rows, forcing_rows)):
        for field in range(FIELDS):
            first = rows[field, low : low + size, :]
            last = rows[field, high : high + size, :]
            send_a[which * FIELDS + field] = jnp.where(odd == 1, first, last)
            send_b[which * FIELDS + field] = jnp.where(odd == 1, last, first)


def place_halo(where_ref, buffer, own_rows, got_a, got_b, first, padded):
    odd = where_ref[0] % 2
    row_a = jnp.where(odd == 1, O0 - FINE_HALO, O0 + OWN)
    row_b = jnp.where(odd == 1, O0 + OWN, O0 - FINE_HALO)

    def put_row(field, row, value):
        if padded:
            put(buffer, field, row, 0, value)
        else:
            buffer[field, row] = value

    def own(row):
        start = pl.multiple_of(row * SUB, SUB)
        for field in range(FIELDS):
            put_row(field, O0 + row, own_rows[field, pl.ds(start, SUB), :])

    def halo(row):
        start = pl.multiple_of(row * SUB, SUB)
        for field in range(FIELDS):
            put_row(field, row_a + row, got_a[first + field, pl.ds(start, SUB), :])
            put_row(field, row_b + row, got_b[first + field, pl.ds(start, SUB), :])

    rows_loop(0, OWN, own)
    rows_loop(0, FINE_HALO, halo)


def down_kernel(fresh, *refs):
    if fresh:
        where_ref, state, force, got_a, got_b, table, v0, v1, s1, c1, send, f0, tmp0, tmp1, q1 = refs
    else:
        where_ref, state, got_a, got_b, f0, table, v0, v1, s1, c1, send, tmp0, tmp1, q1 = refs
    place_halo(where_ref, v0, state, got_a, got_b, 0, True)
    edges(v0, 0, O0 - FINE_HALO, O0 + OWN + FINE_HALO)
    if fresh:
        place_halo(where_ref, f0, force, got_a, got_b, FIELDS, False)
    fine_source = lambda field, row: f0[field, row]
    low, high = O0 - FINE_HALO, O0 + OWN + FINE_HALO
    sweep(fine_source, v0, tmp0, table, 0, low + 1, high - 1)
    sweep(fine_source, tmp0, v0, table, 0, low + 2, high - 2)

    half = OWN // 2
    descend(fine_source, v0, table, 0, c1, q1, tmp1, O1 - 4, O1 + half + 4)
    make_source(c1, q1, s1, table, 1, O1 - 3, O1 + half + 3)
    first_source = lambda field, row: s1[field, row]
    sweep(first_source, tmp1, v1, table, 1, O1 - 3, O1 + half + 3)

    sub = sub_iota()

    def to_second(index):
        coarse, rest = coarsen(first_source, v1, table, 1, index + O1 // 2)
        return coarse + rest

    def pack(index, values):
        group, place = index // GROUP, index % GROUP
        mine = (sub & (GROUP - 1)) == place
        for which in range(2 * FIELDS):
            send[group, which] = jnp.where(mine, values[which], send[group, which])

    send[...] = jnp.zeros_like(send)
    batches(0, OWN // 4, COARSEN_BATCH, to_second, pack)


def spread(source, index, which, place):
    take = lambda sub: jnp.broadcast_to(source[index, which, sub : sub + 1, :], (SUB, LANES))
    return jnp.where(sub_iota() < GROUP, take(place), take(GROUP + place))


def up_kernel(last, *refs):
    if last:
        (where_ref, own, got_a, got_b, got_a2, v0, f0, v1, s1, c1, table, out,
         parts, tmp0, work0, tmp1, work1, c2, q2, s2, v2, tmp2, c3, q3, s3, v3, tmp3) = refs
    else:
        (where_ref, own, got_a, got_b, got_a2, v0, f0, v1, s1, c1, table, out,
         send_a, send_b, tmp0, work0, tmp1, work1, c2, q2, s2, v2, tmp2, c3, q3, s3, v3, tmp3) = refs
    odd = where_ref[0] % 2

    def unpack(source, index, group):
        for place in range(GROUP):
            row = group * GROUP + place
            coarse = [spread(source, index, f, place) for f in range(FIELDS)]
            rest = [spread(source, index, FIELDS + f, place) for f in range(FIELDS)]
            start = first_sweep(coarse, rest, table, 2, row)
            for field in range(FIELDS):
                put(c2, field, row, 2, coarse[field])
                q2[field, row] = rest[field]
                put(tmp2, field, row, 2, start[field])

    pick = lambda a, b: jnp.where(odd == 1, b, a)
    rows_loop(0, 2, lambda i: unpack(own, i, 4 + i))
    rows_loop(0, 2, lambda i: unpack(got_a, i, pick(6, 2) + i))
    rows_loop(0, 3, lambda i: unpack(got_b, i, pick(1, 6) + i))
    rows_loop(0, 1, lambda i: unpack(got_a2, pick(0, 2) + i, pick(8, 1) + i))

    quarter, eighth = OWN // 4, OWN // 8
    for ref in (c2, tmp2):
        edges(ref, 2, O2 - 12, O2 + quarter + 12)
    make_source(c2, q2, s2, table, 2, O2 - 11, O2 + quarter + 11)
    second_source = lambda field, row: s2[field, row]
    sweep(second_source, tmp2, v2, table, 2, O2 - 11, O2 + quarter + 11)

    descend(second_source, v2, table, 2, c3, q3, tmp3, O3 - 5, O3 + eighth + 5)
    make_source(c3, q3, s3, table, 3, O3 - 4, O3 + eighth + 4)
    third_source = lambda field, row: s3[field, row]
    sweep(third_source, tmp3, v3, table, 3, O3 - 4, O3 + eighth + 4)
    sweep(third_source, v3, tmp3, table, 3, O3 - 3, O3 + eighth + 3)
    sweep(third_source, tmp3, v3, table, 3, O3 - 2, O3 + eighth + 2, False)
    correct(v2, v2, v3, c3, 2, 0, O2 - 4, O2 + quarter + 4)
    sweep(second_source, v2, tmp2, table, 2, O2 - 3, O2 + quarter + 3)
    sweep(second_source, tmp2, v2, table, 2, O2 - 2, O2 + quarter + 2, False)

    half = OWN // 2
    first_source = lambda field, row: s1[field, row]
    correct(work1, v1, v2, c2, 1, O2 - O1 // 2, O1 - 3, O1 + half + 3)
    sweep(first_source, work1, tmp1, table, 1, O1 - 2, O1 + half + 2)
    sweep(first_source, tmp1, work1, table, 1, O1 - 1, O1 + half + 1, False)

    fine_source = lambda field, row: f0[field, row]
    correct(work0, v0, work1, c1, 0, 0, O0 - 2, O0 + OWN + 2)
    sweep(fine_source, work0, tmp0, table, 0, O0 - 1, O0 + OWN + 1)
    sweep(fine_source, tmp0, work0, table, 0, O0, O0 + OWN, False)

    if last:
        held = FIELDS * OWN
        for field in range(FIELDS):
            for sub in range(SUB):
                value = work0[field, pl.ds(at(O0, 0) + sub, OWN, stride=stride_of(0)), :]
                for p, part in enumerate(three_parts(value)):
                    start = p * held + field * OWN
                    parts[start : start + OWN, sub * LANES : (sub + 1) * LANES] = part

        def columns_out(index):
            values = dot(parts[...], turn(2 * index, False))
            values = (values[:held] + values[held : 2 * held]) + values[2 * held :]
            cells = pl.ds(pl.multiple_of(index * 2 * LANES, 2 * LANES), 2 * LANES)
            for field in range(FIELDS):
                out[field, :, cells] = values[field * OWN : (field + 1) * OWN]

        rows_loop(0, SUB // 2, columns_out)
        return

    def leave(row):
        start = pl.multiple_of(row * SUB, SUB)
        for field in range(FIELDS):
            out[field, pl.ds(start, SUB), :] = tile(work0, field, O0 + row, 0)

    rows_loop(0, OWN, leave)
    from_a, from_b = pick(OWN - FINE_HALO, 0), pick(0, OWN - FINE_HALO)

    def edge(row):
        start = pl.multiple_of(row * SUB, SUB)
        for field in range(FIELDS):
            send_a[field, pl.ds(start, SUB), :] = tile(work0, field, O0 + from_a + row, 0)
            send_b[field, pl.ds(start, SUB), :] = tile(work0, field, O0 + from_b + row, 0)

    rows_loop(0, FINE_HALO, edge)


VMEM = pl.BlockSpec(memory_space=pltpu.VMEM)
SMEM = pl.BlockSpec(memory_space=pltpu.SMEM)


def f32(*shape):
    return jax.ShapeDtypeStruct(shape, jnp.float32)


def scratch(*shape):
    return pltpu.VMEM(shape, jnp.float32)


def padded(rows, level):
    return (FIELDS, padded_rows(rows, level), LANES)


def plain(rows):
    return (FIELDS, rows, SUB, LANES)


def call(kernel, name, outs, operands, scratches=()):
    return pl.pallas_call(
        kernel,
        out_shape=outs,
        in_specs=[SMEM] + [VMEM] * (len(operands) - 1),
        out_specs=[VMEM] * len(outs),
        scratch_shapes=list(scratches),
        name=name,
        compiler_params=pltpu.CompilerParams(vmem_limit_bytes=28 * 1024 * 1024),
    )(*operands)


def per_device(initial_state, forcing, coefficients, region_ids):
    size = lax.axis_size("axial")
    device = lax.axis_index("axial")
    assert initial_state.shape == (FIELDS, OWN, SUB * LANES)
    assert region_ids.shape == (OWN, SUB)
    where_ref = jnp.stack([device, jnp.int32(size)]).astype(jnp.int32)
    odd = device % 2
    pair_a = [(i, i ^ 1) for i in range(size)]
    pair_b = [(i, i + 1 if i % 2 else i - 1) for i in range(1, size - 1)]
    swap_a = lambda x: lax.ppermute(x, "axial", pair_a)
    swap_b = lambda x: lax.ppermute(x, "axial", pair_b)

    share = coefficients.shape[1]
    regions = share * size
    per_tile = LANES // OWN
    gathered = jnp.zeros((regions + SUB * -(-size // per_tile), LANES), jnp.float32)
    gathered = lax.dynamic_update_slice(gathered, coefficients.T, (device * share, 0))
    gathered = lax.dynamic_update_slice(
        gathered,
        region_ids.T.astype(jnp.float32),
        (regions + device // per_tile * SUB, device % per_tile * OWN),
    )
    step = 1
    while step < size:
        swap = [(i, i ^ step) for i in range(size)]
        gathered = gathered + lax.ppermute(gathered, "axial", swap)
        step *= 2

    state, force, send_a, send_b = call(
        split_kernel,
        "split",
        [f32(FIELDS, OWN * SUB, LANES)] * 2 + [f32(2 * FIELDS, FINE_HALO * SUB, LANES)] * 2,
        [where_ref, initial_state, forcing],
        [pltpu.VMEM((3 * 2 * FIELDS * OWN, SUB * LANES), jnp.bfloat16)],
    )
    send_a, send_b, gathered = lax.optimization_barrier((send_a, send_b, gathered))
    got_b, got_a = swap_b(send_b), swap_a(send_a)
    (table,) = call(
        functools.partial(tables_kernel, regions),
        "tables",
        [f32(2 * ENTRIES, TABLE_ROWS, LANES)],
        [where_ref, gathered],
        [scratch(2, 32 * SUB, LANES), scratch(LANES, 2 * LANES)],
    )

    f0 = None
    for cycle in range(CYCLES):
        outs = [f32(*padded(T0, 0)), f32(*padded(T1, 1)), f32(*plain(T1)), f32(*padded(T1, 1)),
                f32(2, 2 * FIELDS, SUB, LANES)]
        temps = [scratch(*padded(T0, 0)), scratch(*padded(T1, 1)), scratch(*plain(T1))]
        if cycle == 0:
            v0, v1, s1, c1, own, f0 = call(
                functools.partial(down_kernel, True), "down_fresh", outs + [f32(*plain(T0))],
                [where_ref, state, force, got_a, got_b, table], temps,
            )
        else:
            v0, v1, s1, c1, own = call(
                functools.partial(down_kernel, False), "down", outs,
                [where_ref, state, got_a, got_b, f0, table], temps,
            )
        beside = swap_a(own)
        row = jnp.concatenate([beside[1:], own, beside[:1]], axis=0)
        far = swap_b(lax.dynamic_slice_in_dim(row, 1 - odd, 3, axis=0))
        beyond = swap_a(far)
        operands = [where_ref, own, beside, far, beyond, v0, f0, v1, s1, c1, table]
        temps = [scratch(*padded(T0, 0))] * 2 + [scratch(*padded(T1, 1))] * 2
        temps += [scratch(*padded(T2, 2)), scratch(*plain(T2)), scratch(*plain(T2)), scratch(*padded(T2, 2)), scratch(*padded(T2, 2))]
        temps += [scratch(*padded(T3, 3)), scratch(*plain(T3)), scratch(*plain(T3)), scratch(*padded(T3, 3)), scratch(*padded(T3, 3))]
        if cycle == CYCLES - 1:
            return call(
                functools.partial(up_kernel, True), "up_last",
                [f32(FIELDS, OWN, SUB * LANES)], operands,
                [pltpu.VMEM((3 * FIELDS * OWN, SUB * LANES), jnp.bfloat16)] + temps,
            )[0]
        state, send_a, send_b = call(
            functools.partial(up_kernel, False), "up",
            [f32(FIELDS, OWN * SUB, LANES)] + [f32(FIELDS, FINE_HALO * SUB, LANES)] * 2,
            operands, temps,
        )
        got_b, got_a = swap_b(send_b), swap_a(send_a)


def solution(mesh):
    placed = (
        P("sample", "axial", None),
        P("sample", "axial", None),
        P("sample", "axial"),
        P("axial", None),
    )
    return jax.shard_map(
        per_device,
        mesh=mesh,
        in_specs=placed,
        out_specs=P("sample", "axial", None),
        check_vma=False,
    )
```

```python
import functools

import jax
import jax.numpy as jnp
from jax import lax
from jax.experimental import pallas as pl
from jax.experimental.pallas import tpu as pltpu
from jax.sharding import PartitionSpec as P

DIFFUSION = 1.0
RELAXATION = 0.8
SOURCE_GAIN = 0.05
CYCLES = 2

FIELDS = 5
ENTRIES = FIELDS * FIELDS
SUB, LANES = 8, 128

OWN = 32
FINE_HALO = 11
T0, O0 = 64, 16
T1, O1 = 32, 8
T2, O2 = 40, 16
T3, O3 = 20, 8
GROUP = 4
SPREAD = 16


def stride_of(level):
    return SUB + 2 * 2**level


def padded_rows(rows, level):
    return stride_of(level) * (rows + SUB)


def at(row, level):
    return stride_of(level) * row + 2**level


def lane_iota():
    return lax.broadcasted_iota(jnp.int32, (SUB, LANES), 1)


def sub_iota():
    return lax.broadcasted_iota(jnp.int32, (SUB, LANES), 0)


def tile(ref, field, row, level):
    return ref[field, pl.ds(at(row, level), SUB), :]


def put(ref, field, row, level, value):
    ref[field, pl.ds(at(row, level), SUB), :] = value


def edges(ref, level, first, last):
    width, stride, lane = 2**level, stride_of(level), lane_iota()
    for row in range(first, last, SUB):
        start = at(row, level)
        for field in range(FIELDS):
            rows = lambda sub: (field, pl.ds(start + sub, SUB, stride=stride), slice(None))
            before = jnp.where(lane == 0, 0.0, pltpu.roll(ref[rows(SUB - 1)], 1, 1))
            after = jnp.where(lane == LANES - 1, 0.0, pltpu.roll(ref[rows(0)], LANES - 1, 1))
            for i in range(width):
                ref[rows(i - width)] = before
                ref[rows(SUB + i)] = after


def rows_loop(first, last, body):
    def step(row, carry):
        body(row)
        return carry

    lax.fori_loop(first, last, step, 0)


def batches(first, last, batch, compute, store):
    def body(index):
        rows = [first + index * batch + i for i in range(batch)]
        results = [compute(row) for row in rows]
        for row, result in zip(rows, results):
            store(row, result)

    rows_loop(0, -(-(last - first) // batch), body)


def neighbours(ref, row, level):
    start, width, stride = at(row, level), 2**level, stride_of(level)
    sums, centres = [], []
    for field in range(FIELDS):
        load = lambda first: ref[field, pl.ds(first, SUB), :]
        radial = load(start - width) + load(start + width)
        sums.append(radial + (load(start - stride) + load(start + stride)))
        centres.append(load(start))
    return sums, centres


def block_times(table, level, row, first, vectors):
    row = TABLE_AT[level] + row
    out = []
    for i in range(FIELDS):
        total = None
        for j in range(FIELDS):
            entry = first + FIELDS * i + j
            term = jnp.broadcast_to(table[entry, pl.ds(row, 1), :], (SUB, LANES)) * vectors[j]
            total = term if total is None else total + term
        out.append(total)
    return out


MATRIX_AT = ENTRIES
TABLE_AT = (0, T0, T0 + T1, T0 + T1 + T2)
TABLE_ROWS = 160
NEAR = 5


def gain_of(level):
    return SOURCE_GAIN * 4.0**level / DIFFUSION


def sweep(source_of, old, new, table, level, first, last, more=True):
    gain = gain_of(level)

    def compute(row):
        sums, centres = neighbours(old, row, level)
        rest = [
            (source_of(field, row) + sums[field]) - gain * jnp.tanh(centres[field])
            for field in range(FIELDS)
        ]
        moved = block_times(table, level, row, 0, rest)
        return [(1.0 - RELAXATION) * centres[f] + moved[f] for f in range(FIELDS)]

    def store(row, values):
        for field in range(FIELDS):
            put(new, field, row, level, values[field])

    batches(first, last, SWEEP_BATCH, compute, store)
    if more:
        edges(new, level, first, last)


def residual(source_of, values, table, level, row):
    gain = gain_of(level)
    sums, centres = neighbours(values, row, level)
    applied = block_times(table, level, row, MATRIX_AT, centres)
    left = [
        ((source_of(field, row) + sums[field]) - gain * jnp.tanh(centres[field])) - applied[field]
        for field in range(FIELDS)
    ]
    return left, centres


def pair_sum(value, level):
    width = 2**level
    other = pltpu.roll(value, SUB - width, 0)
    if 2 * width != SUB:
        other = jnp.where((sub_iota() & width) == 0, other, pltpu.roll(value, width, 0))
    return value + other


def coarsen(source_of, values, table, level, row):
    upper_r, upper_v = residual(source_of, values, table, level, 2 * row)
    lower_r, lower_v = residual(source_of, values, table, level, 2 * row + 1)
    coarse = [0.25 * pair_sum(upper_v[f] + lower_v[f], level) for f in range(FIELDS)]
    rest = [pair_sum(upper_r[f] + lower_r[f], level) for f in range(FIELDS)]
    return coarse, rest


def first_sweep(coarse, rest, table, level, row):
    moved = block_times(table, level, row, 0, rest)
    return [coarse[f] + moved[f] for f in range(FIELDS)]


def descend(source_of, values, table, level, c, q, first_values, first, last):
    def compute(row):
        coarse, rest = coarsen(source_of, values, table, level, row)
        return coarse, rest, first_sweep(coarse, rest, table, level + 1, row)

    def store(row, results):
        for field in range(FIELDS):
            put(c, field, row, level + 1, results[0][field])
            q[field, row] = results[1][field]
            put(first_values, field, row, level + 1, results[2][field])

    batches(first, last, COARSEN_BATCH, compute, store)
    edges(c, level + 1, first, last)
    edges(first_values, level + 1, first, last)


def make_source(coarse, rest, source, table, level, first, last):
    gain = gain_of(level)

    def compute(row):
        sums, centres = neighbours(coarse, row, level)
        applied = block_times(table, level, row, MATRIX_AT, centres)
        return [
            (applied[f] - sums[f]) + (gain * jnp.tanh(centres[f]) + rest[f, row])
            for f in range(FIELDS)
        ]

    def store(row, values):
        for field in range(FIELDS):
            source[field, row] = values[field]

    batches(first, last, SWEEP_BATCH, compute, store)


def correct(new, fine, after, before, level, offset, first, last):
    def body(index):
        coarse_row = first // 2 + index + offset
        row = first // 2 * 2 + 2 * index
        for field in range(FIELDS):
            change = tile(after, field, coarse_row, level + 1) - tile(before, field, coarse_row, level + 1)
            put(new, field, row, level, tile(fine, field, row, level) + change)
            put(new, field, row + 1, level, tile(fine, field, row + 1, level) + change)

    rows_loop(0, (last + 1) // 2 - first // 2, body)
    edges(new, level, first, last)


SWEEP_BATCH = 4
COARSEN_BATCH = 2


def three_parts(value):
    high = value.astype(jnp.bfloat16)
    rest = value - high.astype(jnp.float32)
    middle = rest.astype(jnp.bfloat16)
    low = (rest - middle.astype(jnp.float32)).astype(jnp.bfloat16)
    return high, middle, low


def dot(left, right):
    return jnp.dot(left, right, preferred_element_type=jnp.float32)


def prep_kernel(share, where_ref, coefficients_ref, ids_ref, out, own_coefficients, own_ids, sems):
    device, devices = where_ref[0], where_ref[1]
    copies = [
        pltpu.make_async_copy(coefficients_ref, own_coefficients, sems.at[0]),
        pltpu.make_async_copy(ids_ref, own_ids, sems.at[1]),
    ]
    for copy in copies:
        copy.start()
    out[...] = jnp.zeros_like(out)
    for copy in copies:
        copy.wait()
    for i in range(share):
        out[pl.ds(device * share + i, 1), 0:ENTRIES] = own_coefficients[i : i + 1, :]
    ids = own_ids[...].astype(jnp.float32)
    per_tile = LANES // OWN
    start = pl.multiple_of(devices * share + device // per_tile * SUB, SUB)
    for place in range(per_tile):

        @pl.when(device % per_tile == place)
        def _():
            out[pl.ds(start, SUB), place * OWN : (place + 1) * OWN] = ids


def tables_kernel(regions, where_ref, regions_ref, table, mats, parts):
    device, devices = where_ref[0], where_ref[1]
    wide = 2 * LANES
    lane = lane_iota()
    ids = [jnp.full((SUB, LANES), -1.0, jnp.float32)] * 2
    per_tile = LANES // OWN
    for i in range(NEAR):
        owner = jnp.clip(device + (i - NEAR // 2), 0, devices - 1)
        start = pl.multiple_of(regions + owner // per_tile * SUB, SUB)
        held = regions_ref[pl.ds(start, SUB), :]
        turned = pltpu.roll(held, ((i % per_tile) - owner % per_tile + per_tile) % per_tile * OWN, 1)
        place = i // per_tile
        ids[place] = jnp.where(lane // OWN == i % per_tile, turned, ids[place])
    ids = jnp.concatenate(ids, axis=1).astype(jnp.int32)

    coefficients = jnp.transpose(regions_ref[0:regions, :])[0:32]
    coefficients = jnp.concatenate(three_parts(coefficients), axis=0)
    region = lax.broadcasted_iota(jnp.int32, (regions, wide), 0)
    for block in range(SUB):
        chosen = region == jnp.broadcast_to(ids[block : block + 1], (regions, wide))
        found = dot(coefficients, chosen.astype(jnp.float32).astype(jnp.bfloat16))
        found = (found[0:32] + found[32:64]) + found[64:96]
        for half in range(2):
            mats[half, pl.ds(block, 32, stride=SUB), :] = found[:, half * LANES : (half + 1) * LANES]

    fine = lax.broadcasted_iota(jnp.int32, (wide, wide), 0)
    out = lax.broadcasted_iota(jnp.int32, (wide, wide), 1)
    average = jnp.zeros((wide, wide), jnp.float32)
    own_at = NEAR // 2 * OWN
    for level, (first_own, rows) in enumerate(((O0, T0), (O1, T1), (O2, T2), (O3, T3))):
        span = 2**level
        row = out - TABLE_AT[level]
        same = (row >= 0) & (row < rows) & (fine // span == row + (own_at // span - first_own))
        average = jnp.where(same, 1.0 / span, average)
    average = average.astype(jnp.bfloat16)
    used = SUB * ENTRIES
    high, middle, low = three_parts(jnp.concatenate([mats[0, 0:used], mats[1, 0:used]], axis=1))
    levels = (dot(high, average) + dot(middle, average)) + dot(low, average)

    row = lax.broadcasted_iota(jnp.int32, (SUB, wide), 1)
    weight = jnp.zeros((SUB, wide), jnp.float32) + DIFFUSION
    whole = jnp.zeros((SUB, wide), jnp.int32)
    limit = jnp.zeros((SUB, wide), jnp.int32)
    for level, first_own in enumerate((O0, O1, O2, O3)):
        here = row >= TABLE_AT[level]
        weight = jnp.where(here, DIFFUSION / 4.0**level, weight)
        whole = jnp.where(here, row - TABLE_AT[level] - first_own + device * (OWN >> level), whole)
        limit = jnp.where(here, devices * (OWN >> level), limit)
    inside = (whole >= 0) & (whole < limit)
    scale = jnp.where(inside, RELAXATION * weight, 0.0)
    unscale = 1.0 / weight

    n = FIELDS
    block = [[levels[SUB * (n * i + j) : SUB * (n * i + j + 1)] for j in range(n)] for i in range(n)]
    for i in range(n):
        block[i][i] = block[i][i] + 4.0 * weight
    entries = [block[i][j] * unscale for i in range(n) for j in range(n)]
    right = [[None] * n for _ in range(n)]
    for i in range(n):
        right[i][i] = jnp.ones((SUB, wide), jnp.float32)
    for c in range(n):
        lead = 1.0 / block[c][c]
        for j in range(c + 1, n):
            block[c][j] = block[c][j] * lead
        for j in range(n):
            if right[c][j] is not None:
                right[c][j] = right[c][j] * lead
        for i in range(n):
            if i == c:
                continue
            factor = block[i][c]
            for j in range(c + 1, n):
                block[i][j] = block[i][j] - factor * block[c][j]
            for j in range(n):
                if right[c][j] is not None:
                    term = factor * right[c][j]
                    right[i][j] = -term if right[i][j] is None else right[i][j] - term
    entries = [right[i][j] * scale for i in range(n) for j in range(n)] + entries

    group = FIELDS
    into = lax.broadcasted_iota(jnp.int32, (LANES, group * LANES), 0)
    out = lax.broadcasted_iota(jnp.int32, (LANES, group * LANES), 1)
    same = (into // (3 * SUB) == out // LANES) & (into % SUB == out % LANES // SPREAD)
    widen = same.astype(jnp.float32).astype(jnp.bfloat16)
    parts[...] = jnp.zeros_like(parts)
    for first in range(0, len(entries), group):
        for i in range(group):
            for p, part in enumerate(three_parts(entries[first + i])):
                start = (3 * i + p) * SUB
                parts[start : start + SUB, :] = part.astype(jnp.float32)
        turned = jnp.transpose(parts[...])[0:TABLE_ROWS].astype(jnp.bfloat16)
        wide_rows = dot(turned, widen)
        for i in range(group):
            table[first + i] = wide_rows[:, i * LANES : (i + 1) * LANES]


def turn(first_sub, inward):
    shape = (SUB * LANES, 2 * LANES)
    into = lax.broadcasted_iota(jnp.int32, shape, 0)
    out = lax.broadcasted_iota(jnp.int32, shape, 1)
    if inward:
        wanted = (out % LANES) * SUB + first_sub + out // LANES
    else:
        cell = out + first_sub * LANES
        wanted = (cell % SUB) * LANES + cell // SUB
    return (into == wanted).astype(jnp.float32).astype(jnp.bfloat16)


def split_kernel(where_ref, state_ref, forcing_ref, state_rows, forcing_rows, send_a, send_b, parts, held_in, sems):
    copies = [
        pltpu.make_async_copy(source, held_in.at[i], sems.at[i])
        for i, source in enumerate((state_ref, forcing_ref))
    ]
    for copy in copies:
        copy.start()
    odd = where_ref[0] % 2
    held = 2 * FIELDS * OWN
    for which, copy in enumerate(copies):
        copy.wait()
        for field in range(FIELDS):
            for p, part in enumerate(three_parts(held_in[which, field])):
                start = p * held + (which * FIELDS + field) * OWN
                parts[start : start + OWN, :] = part

    def two_subs(index):
        values = dot(parts[...], turn(2 * index, True))
        values = (values[:held] + values[held : 2 * held]) + values[2 * held :]
        for which, target in enumerate((state_rows, forcing_rows)):
            for field in range(FIELDS):
                start = (which * FIELDS + field) * OWN
                for half in range(2):
                    target[field, pl.ds(2 * index + half, OWN, stride=SUB), :] = values[
                        start : start + OWN, half * LANES : (half + 1) * LANES
                    ]

    rows_loop(0, SUB // 2, two_subs)
    low, high = 0, (OWN - FINE_HALO) * SUB
    size = FINE_HALO * SUB
    for which, rows in enumerate((state_rows, forcing_rows)):
        for field in range(FIELDS):
            first = rows[field, low : low + size, :]
            last = rows[field, high : high + size, :]
            send_a[which * FIELDS + field] = jnp.where(odd == 1, first, last)
            send_b[which * FIELDS + field] = jnp.where(odd == 1, last, first)


def place_halo(where_ref, buffer, own_rows, got_a, got_b, first, padded):
    odd = where_ref[0] % 2
    row_a = jnp.where(odd == 1, O0 - FINE_HALO, O0 + OWN)
    row_b = jnp.where(odd == 1, O0 + OWN, O0 - FINE_HALO)

    def put_row(field, row, value):
        if padded:
            put(buffer, field, row, 0, value)
        else:
            buffer[field, row] = value

    def own(row):
        start = pl.multiple_of(row * SUB, SUB)
        for field in range(FIELDS):
            put_row(field, O0 + row, own_rows[field, pl.ds(start, SUB), :])

    def halo(row):
        start = pl.multiple_of(row * SUB, SUB)
        for field in range(FIELDS):
            put_row(field, row_a + row, got_a[first + field, pl.ds(start, SUB), :])
            put_row(field, row_b + row, got_b[first + field, pl.ds(start, SUB), :])

    rows_loop(0, OWN, own)
    rows_loop(0, FINE_HALO, halo)


def down_kernel(fresh, *refs):
    if fresh:
        where_ref, state, force, got_a, got_b, table, v0, v1, s1, c1, send, f0, tmp0, tmp1, q1 = refs
    else:
        where_ref, state, got_a, got_b, f0, table, v0, v1, s1, c1, send, tmp0, tmp1, q1 = refs
    place_halo(where_ref, v0, state, got_a, got_b, 0, True)
    edges(v0, 0, O0 - FINE_HALO, O0 + OWN + FINE_HALO)
    if fresh:
        place_halo(where_ref, f0, force, got_a, got_b, FIELDS, False)
    fine_source = lambda field, row: f0[field, row]
    low, high = O0 - FINE_HALO, O0 + OWN + FINE_HALO
    sweep(fine_source, v0, tmp0, table, 0, low + 1, high - 1)
    sweep(fine_source, tmp0, v0, table, 0, low + 2, high - 2)

    half = OWN // 2
    descend(fine_source, v0, table, 0, c1, q1, tmp1, O1 - 4, O1 + half + 4)
    make_source(c1, q1, s1, table, 1, O1 - 3, O1 + half + 3)
    first_source = lambda field, row: s1[field, row]
    sweep(first_source, tmp1, v1, table, 1, O1 - 3, O1 + half + 3)

    sub = sub_iota()

    def to_second(index):
        coarse, rest = coarsen(first_source, v1, table, 1, index + O1 // 2)
        return coarse + rest

    def pack(index, values):
        group, place = index // GROUP, index % GROUP
        mine = (sub & (GROUP - 1)) == place
        for which in range(2 * FIELDS):
            send[group, which] = jnp.where(mine, values[which], send[group, which])

    send[...] = jnp.zeros_like(send)
    batches(0, OWN // 4, COARSEN_BATCH, to_second, pack)


def spread(source, index, which, place):
    take = lambda sub: jnp.broadcast_to(source[index, which, sub : sub + 1, :], (SUB, LANES))
    return jnp.where(sub_iota() < GROUP, take(place), take(GROUP + place))


def up_kernel(last, *refs):
    if last:
        (where_ref, own, got_a, got_b, got_a2, v0, f0, v1, s1, c1, table, out,
         parts, tmp0, work0, tmp1, work1, c2, q2, s2, v2, tmp2, c3, q3, s3, v3, tmp3) = refs
    else:
        (where_ref, own, got_a, got_b, got_a2, v0, f0, v1, s1, c1, table, out,
         send_a, send_b, tmp0, work0, tmp1, work1, c2, q2, s2, v2, tmp2, c3, q3, s3, v3, tmp3) = refs
    odd = where_ref[0] % 2

    def unpack(source, index, group):
        for place in range(GROUP):
            row = group * GROUP + place
            coarse = [spread(source, index, f, place) for f in range(FIELDS)]
            rest = [spread(source, index, FIELDS + f, place) for f in range(FIELDS)]
            start = first_sweep(coarse, rest, table, 2, row)
            for field in range(FIELDS):
                put(c2, field, row, 2, coarse[field])
                q2[field, row] = rest[field]
                put(tmp2, field, row, 2, start[field])

    pick = lambda a, b: jnp.where(odd == 1, b, a)
    rows_loop(0, 2, lambda i: unpack(own, i, 4 + i))
    rows_loop(0, 2, lambda i: unpack(got_a, i, pick(6, 2) + i))
    rows_loop(0, 3, lambda i: unpack(got_b, i, pick(1, 6) + i))
    rows_loop(0, 1, lambda i: unpack(got_a2, pick(0, 2) + i, pick(8, 1) + i))

    quarter, eighth = OWN // 4, OWN // 8
    for ref in (c2, tmp2):
        edges(ref, 2, O2 - 12, O2 + quarter + 12)
    make_source(c2, q2, s2, table, 2, O2 - 11, O2 + quarter + 11)
    second_source = lambda field, row: s2[field, row]
    sweep(second_source, tmp2, v2, table, 2, O2 - 11, O2 + quarter + 11)

    descend(second_source, v2, table, 2, c3, q3, tmp3, O3 - 5, O3 + eighth + 5)
    make_source(c3, q3, s3, table, 3, O3 - 4, O3 + eighth + 4)
    third_source = lambda field, row: s3[field, row]
    sweep(third_source, tmp3, v3, table, 3, O3 - 4, O3 + eighth + 4)
    sweep(third_source, v3, tmp3, table, 3, O3 - 3, O3 + eighth + 3)
    sweep(third_source, tmp3, v3, table, 3, O3 - 2, O3 + eighth + 2, False)
    correct(v2, v2, v3, c3, 2, 0, O2 - 4, O2 + quarter + 4)
    sweep(second_source, v2, tmp2, table, 2, O2 - 3, O2 + quarter + 3)
    sweep(second_source, tmp2, v2, table, 2, O2 - 2, O2 + quarter + 2, False)

    half = OWN // 2
    first_source = lambda field, row: s1[field, row]
    correct(work1, v1, v2, c2, 1, O2 - O1 // 2, O1 - 3, O1 + half + 3)
    sweep(first_source, work1, tmp1, table, 1, O1 - 2, O1 + half + 2)
    sweep(first_source, tmp1, work1, table, 1, O1 - 1, O1 + half + 1, False)

    fine_source = lambda field, row: f0[field, row]
    correct(work0, v0, work1, c1, 0, 0, O0 - 2, O0 + OWN + 2)
    sweep(fine_source, work0, tmp0, table, 0, O0 - 1, O0 + OWN + 1)
    sweep(fine_source, tmp0, work0, table, 0, O0, O0 + OWN, False)

    if last:
        held = FIELDS * OWN
        for field in range(FIELDS):
            for sub in range(SUB):
                value = work0[field, pl.ds(at(O0, 0) + sub, OWN, stride=stride_of(0)), :]
                for p, part in enumerate(three_parts(value)):
                    start = p * held + field * OWN
                    parts[start : start + OWN, sub * LANES : (sub + 1) * LANES] = part

        def columns_out(index):
            values = dot(parts[...], turn(2 * index, False))
            values = (values[:held] + values[held : 2 * held]) + values[2 * held :]
            cells = pl.ds(pl.multiple_of(index * 2 * LANES, 2 * LANES), 2 * LANES)
            for field in range(FIELDS):
                out[field, :, cells] = values[field * OWN : (field + 1) * OWN]

        rows_loop(0, SUB // 2, columns_out)
        return

    def leave(row):
        start = pl.multiple_of(row * SUB, SUB)
        for field in range(FIELDS):
            out[field, pl.ds(start, SUB), :] = tile(work0, field, O0 + row, 0)

    rows_loop(0, OWN, leave)
    from_a, from_b = pick(OWN - FINE_HALO, 0), pick(0, OWN - FINE_HALO)

    def edge(row):
        start = pl.multiple_of(row * SUB, SUB)
        for field in range(FIELDS):
            send_a[field, pl.ds(start, SUB), :] = tile(work0, field, O0 + from_a + row, 0)
            send_b[field, pl.ds(start, SUB), :] = tile(work0, field, O0 + from_b + row, 0)

    rows_loop(0, FINE_HALO, edge)


def relay_kernel(where_ref, own, beside, row):
    odd = where_ref[0] % 2
    row[odd] = own[0]
    row[odd + 1] = own[1]
    row[2 - 2 * odd] = beside[odd]


VMEM = pl.BlockSpec(memory_space=pltpu.VMEM)
SMEM = pl.BlockSpec(memory_space=pltpu.SMEM)
ANY = pl.BlockSpec(memory_space=pltpu.HBM)


def f32(*shape):
    return jax.ShapeDtypeStruct(shape, jnp.float32)


def scratch(*shape):
    return pltpu.VMEM(shape, jnp.float32)


def padded(rows, level):
    return (FIELDS, padded_rows(rows, level), LANES)


def plain(rows):
    return (FIELDS, rows, SUB, LANES)


def call(kernel, name, grant, outs, operands, scratches=(), raw=False):
    return pl.pallas_call(
        kernel,
        out_shape=outs,
        in_specs=[SMEM] + [ANY if raw else VMEM] * (len(operands) - 1),
        out_specs=[VMEM] * len(outs),
        scratch_shapes=list(scratches),
        name=name,
        compiler_params=pltpu.CompilerParams(vmem_limit_bytes=grant * 1024 * 1024),
    )(*operands)


def per_device(initial_state, forcing, coefficients, region_ids):
    size = lax.axis_size("axial")
    device = lax.axis_index("axial")
    assert initial_state.shape == (FIELDS, OWN, SUB * LANES)
    assert region_ids.shape == (OWN, SUB)
    where_ref = jnp.stack([device, jnp.int32(size)]).astype(jnp.int32)
    odd = device % 2
    pair_a = [(i, i ^ 1) for i in range(size)]
    pair_b = [(i, i + 1 if i % 2 else i - 1) for i in range(1, size - 1)]
    swap_a = lambda x: lax.ppermute(x, "axial", pair_a)
    swap_b = lambda x: lax.ppermute(x, "axial", pair_b)

    share = coefficients.shape[1]
    regions = share * size
    per_tile = LANES // OWN
    (gathered,) = call(
        functools.partial(prep_kernel, share),
        "prep",
        4,
        [f32(regions + SUB * -(-size // per_tile), LANES)],
        [where_ref, coefficients.T, region_ids.T],
        [
            scratch(share, ENTRIES),
            pltpu.VMEM((SUB, OWN), jnp.int32),
            pltpu.SemaphoreType.DMA((2,)),
        ],
        True,
    )

    def doubled(held, step):
        return held + lax.ppermute(held, "axial", [(i, i ^ step) for i in range(size)])

    state, force, send_a, send_b = call(
        split_kernel,
        "split", 12,
        [f32(FIELDS, OWN * SUB, LANES)] * 2 + [f32(2 * FIELDS, FINE_HALO * SUB, LANES)] * 2,
        [where_ref, initial_state, forcing],
        [
            pltpu.VMEM((3 * 2 * FIELDS * OWN, SUB * LANES), jnp.bfloat16),
            scratch(2, FIELDS, OWN, SUB * LANES),
            pltpu.SemaphoreType.DMA((2,)),
        ],
        True,
    )
    step = 1
    while step < min(size, 4):
        gathered = doubled(gathered, step)
        step *= 2
    gathered, send_a, send_b = lax.optimization_barrier((gathered, send_a, send_b))
    got_b, got_a = swap_b(send_b), swap_a(send_a)
    while step < size:
        gathered = doubled(gathered, step)
        step *= 2
    (table,) = call(
        functools.partial(tables_kernel, regions),
        "tables", 12,
        [f32(2 * ENTRIES, TABLE_ROWS, LANES)],
        [where_ref, gathered],
        [scratch(2, 32 * SUB, LANES), scratch(LANES, 2 * LANES)],
    )

    f0 = None
    for cycle in range(CYCLES):
        outs = [f32(*padded(T0, 0)), f32(*padded(T1, 1)), f32(*plain(T1)), f32(*padded(T1, 1)),
                f32(2, 2 * FIELDS, SUB, LANES)]
        temps = [scratch(*padded(T0, 0)), scratch(*padded(T1, 1)), scratch(*plain(T1))]
        if cycle == 0:
            v0, v1, s1, c1, own, f0 = call(
                functools.partial(down_kernel, True), "down_fresh", 14, outs + [f32(*plain(T0))],
                [where_ref, state, force, got_a, got_b, table], temps,
            )
        else:
            v0, v1, s1, c1, own = call(
                functools.partial(down_kernel, False), "down", 14, outs,
                [where_ref, state, got_a, got_b, f0, table], temps,
            )
        beside = swap_a(own)
        (row,) = call(
            relay_kernel, "relay", 2, [f32(3, 2 * FIELDS, SUB, LANES)], [where_ref, own, beside]
        )
        far = swap_b(row)
        beyond = swap_a(far)
        operands = [where_ref, own, beside, far, beyond, v0, f0, v1, s1, c1, table]
        temps = [scratch(*padded(T0, 0))] * 2 + [scratch(*padded(T1, 1))] * 2
        temps += [scratch(*padded(T2, 2)), scratch(*plain(T2)), scratch(*plain(T2)), scratch(*padded(T2, 2)), scratch(*padded(T2, 2))]
        temps += [scratch(*padded(T3, 3)), scratch(*plain(T3)), scratch(*plain(T3)), scratch(*padded(T3, 3)), scratch(*padded(T3, 3))]
        if cycle == CYCLES - 1:
            return call(
                functools.partial(up_kernel, True), "up_last", 26,
                [f32(FIELDS, OWN, SUB * LANES)], operands,
                [pltpu.VMEM((3 * FIELDS * OWN, SUB * LANES), jnp.bfloat16)] + temps,
            )[0]
        state, send_a, send_b = call(
            functools.partial(up_kernel, False), "up", 26,
            [f32(FIELDS, OWN * SUB, LANES)] + [f32(FIELDS, FINE_HALO * SUB, LANES)] * 2,
            operands, temps,
        )
        got_b, got_a = swap_b(send_b), swap_a(send_a)


def solution(mesh):
    placed = (
        P("sample", "axial", None),
        P("sample", "axial", None),
        P("sample", "axial"),
        P("axial", None),
    )
    return jax.shard_map(
        per_device,
        mesh=mesh,
        in_specs=placed,
        out_specs=P("sample", "axial", None),
        check_vma=False,
    )
```

```python
import functools

import jax
import jax.numpy as jnp
from jax import lax
from jax.experimental import pallas as pl
from jax.experimental.pallas import tpu as pltpu
from jax.sharding import PartitionSpec as P

DIFFUSION = 1.0
RELAXATION = 0.8
SOURCE_GAIN = 0.05
CYCLES = 2

FIELDS = 5
ENTRIES = FIELDS * FIELDS
SUB, LANES = 8, 128

OWN = 32
FINE_HALO = 11
T0, O0 = 64, 16
T1, O1 = 32, 8
T2, O2 = 40, 16
T3, O3 = 20, 8
GROUP = 4
SPREAD = 16


def stride_of(level):
    return SUB + 2 * 2**level


def padded_rows(rows, level):
    return stride_of(level) * (rows + SUB)


def at(row, level):
    return stride_of(level) * row + 2**level


def lane_iota():
    return lax.broadcasted_iota(jnp.int32, (SUB, LANES), 1)


def sub_iota():
    return lax.broadcasted_iota(jnp.int32, (SUB, LANES), 0)


def tile(ref, field, row, level):
    return ref[field, pl.ds(at(row, level), SUB), :]


def put(ref, field, row, level, value):
    ref[field, pl.ds(at(row, level), SUB), :] = value


def edges(ref, level, first, last):
    width, stride, lane = 2**level, stride_of(level), lane_iota()
    for row in range(first, last, SUB):
        start = at(row, level)
        for field in range(FIELDS):
            rows = lambda sub: (field, pl.ds(start + sub, SUB, stride=stride), slice(None))
            before = jnp.where(lane == 0, 0.0, pltpu.roll(ref[rows(SUB - 1)], 1, 1))
            after = jnp.where(lane == LANES - 1, 0.0, pltpu.roll(ref[rows(0)], LANES - 1, 1))
            for i in range(width):
                ref[rows(i - width)] = before
                ref[rows(SUB + i)] = after


def rows_loop(first, last, body):
    def step(row, carry):
        body(row)
        return carry

    lax.fori_loop(first, last, step, 0)


def batches(first, last, batch, compute, store):
    def body(index):
        rows = [first + index * batch + i for i in range(batch)]
        results = [compute(row) for row in rows]
        for row, result in zip(rows, results):
            store(row, result)

    rows_loop(0, -(-(last - first) // batch), body)


def neighbours(ref, row, level):
    start, width, stride = at(row, level), 2**level, stride_of(level)
    sums, centres = [], []
    for field in range(FIELDS):
        load = lambda first: ref[field, pl.ds(first, SUB), :]
        radial = load(start - width) + load(start + width)
        sums.append(radial + (load(start - stride) + load(start + stride)))
        centres.append(load(start))
    return sums, centres


def block_times(table, level, row, first, vectors):
    row = TABLE_AT[level] + row
    out = []
    for i in range(FIELDS):
        total = None
        for j in range(FIELDS):
            entry = first + FIELDS * i + j
            term = jnp.broadcast_to(table[entry, pl.ds(row, 1), :], (SUB, LANES)) * vectors[j]
            total = term if total is None else total + term
        out.append(total)
    return out


MATRIX_AT = ENTRIES
TABLE_AT = (0, T0, T0 + T1, T0 + T1 + T2)
TABLE_ROWS = 160
NEAR = 5


def gain_of(level):
    return SOURCE_GAIN * 4.0**level / DIFFUSION


def sweep(source_of, old, new, table, level, first, last, more=True, batch=None):
    gain = gain_of(level)

    def compute(row):
        sums, centres = neighbours(old, row, level)
        rest = [
            (source_of(field, row) + sums[field]) - gain * jnp.tanh(centres[field])
            for field in range(FIELDS)
        ]
        moved = block_times(table, level, row, 0, rest)
        return [(1.0 - RELAXATION) * centres[f] + moved[f] for f in range(FIELDS)]

    def store(row, values):
        for field in range(FIELDS):
            put(new, field, row, level, values[field])

    batches(first, last, batch or SWEEP_BATCH, compute, store)
    if more:
        edges(new, level, first, last)


def residual(source_of, values, table, level, row):
    gain = gain_of(level)
    sums, centres = neighbours(values, row, level)
    applied = block_times(table, level, row, MATRIX_AT, centres)
    left = [
        ((source_of(field, row) + sums[field]) - gain * jnp.tanh(centres[field])) - applied[field]
        for field in range(FIELDS)
    ]
    return left, centres


def pair_sum(value, level):
    width = 2**level
    other = pltpu.roll(value, SUB - width, 0)
    if 2 * width != SUB:
        other = jnp.where((sub_iota() & width) == 0, other, pltpu.roll(value, width, 0))
    return value + other


def coarsen(source_of, values, table, level, row):
    upper_r, upper_v = residual(source_of, values, table, level, 2 * row)
    lower_r, lower_v = residual(source_of, values, table, level, 2 * row + 1)
    coarse = [0.25 * pair_sum(upper_v[f] + lower_v[f], level) for f in range(FIELDS)]
    rest = [pair_sum(upper_r[f] + lower_r[f], level) for f in range(FIELDS)]
    return coarse, rest


def first_sweep(coarse, rest, table, level, row):
    moved = block_times(table, level, row, 0, rest)
    return [coarse[f] + moved[f] for f in range(FIELDS)]


def descend(source_of, values, table, level, c, q, first_values, first, last):
    def compute(row):
        coarse, rest = coarsen(source_of, values, table, level, row)
        return coarse, rest, first_sweep(coarse, rest, table, level + 1, row)

    def store(row, results):
        for field in range(FIELDS):
            put(c, field, row, level + 1, results[0][field])
            q[field, row] = results[1][field]
            put(first_values, field, row, level + 1, results[2][field])

    batches(first, last, COARSEN_BATCH, compute, store)
    edges(c, level + 1, first, last)
    edges(first_values, level + 1, first, last)


def make_source(coarse, rest, source, table, level, first, last):
    gain = gain_of(level)

    def compute(row):
        sums, centres = neighbours(coarse, row, level)
        applied = block_times(table, level, row, MATRIX_AT, centres)
        return [
            (applied[f] - sums[f]) + (gain * jnp.tanh(centres[f]) + rest[f, row])
            for f in range(FIELDS)
        ]

    def store(row, values):
        for field in range(FIELDS):
            source[field, row] = values[field]

    batches(first, last, SWEEP_BATCH, compute, store)


def correct(new, fine, after, before, level, offset, first, last):
    def body(index):
        coarse_row = first // 2 + index + offset
        row = first // 2 * 2 + 2 * index
        for field in range(FIELDS):
            change = tile(after, field, coarse_row, level + 1) - tile(before, field, coarse_row, level + 1)
            put(new, field, row, level, tile(fine, field, row, level) + change)
            put(new, field, row + 1, level, tile(fine, field, row + 1, level) + change)

    rows_loop(0, (last + 1) // 2 - first // 2, body)
    edges(new, level, first, last)


SWEEP_BATCH = 4
INNER = 2
COARSEN_BATCH = 2


def three_parts(value):
    high = value.astype(jnp.bfloat16)
    rest = value - high.astype(jnp.float32)
    middle = rest.astype(jnp.bfloat16)
    low = (rest - middle.astype(jnp.float32)).astype(jnp.bfloat16)
    return high, middle, low


def dot(left, right):
    return jnp.dot(left, right, preferred_element_type=jnp.float32)


def prep_kernel(share, where_ref, coefficients_ref, ids_ref, out, own_coefficients, own_ids, sems):
    device, devices = where_ref[0], where_ref[1]
    copies = [
        pltpu.make_async_copy(coefficients_ref, own_coefficients, sems.at[0]),
        pltpu.make_async_copy(ids_ref, own_ids, sems.at[1]),
    ]
    for copy in copies:
        copy.start()
    out[...] = jnp.zeros_like(out)
    for copy in copies:
        copy.wait()
    for i in range(share):
        out[pl.ds(device * share + i, 1), 0:ENTRIES] = own_coefficients[i : i + 1, :]
    ids = own_ids[...].astype(jnp.float32)
    per_tile = LANES // OWN
    start = pl.multiple_of(devices * share + device // per_tile * SUB, SUB)
    for place in range(per_tile):

        @pl.when(device % per_tile == place)
        def _():
            out[pl.ds(start, SUB), place * OWN : (place + 1) * OWN] = ids


def tables_kernel(regions, where_ref, regions_ref, table, mats, parts):
    device, devices = where_ref[0], where_ref[1]
    wide = 2 * LANES
    lane = lane_iota()
    ids = [jnp.full((SUB, LANES), -1.0, jnp.float32)] * 2
    per_tile = LANES // OWN
    for i in range(NEAR):
        owner = jnp.clip(device + (i - NEAR // 2), 0, devices - 1)
        start = pl.multiple_of(regions + owner // per_tile * SUB, SUB)
        held = regions_ref[pl.ds(start, SUB), :]
        turned = pltpu.roll(held, ((i % per_tile) - owner % per_tile + per_tile) % per_tile * OWN, 1)
        place = i // per_tile
        ids[place] = jnp.where(lane // OWN == i % per_tile, turned, ids[place])
    ids = jnp.concatenate(ids, axis=1).astype(jnp.int32)

    coefficients = jnp.transpose(regions_ref[0:regions, :])[0:32]
    coefficients = jnp.concatenate(three_parts(coefficients), axis=0)
    region = lax.broadcasted_iota(jnp.int32, (regions, wide), 0)
    for block in range(SUB):
        chosen = region == jnp.broadcast_to(ids[block : block + 1], (regions, wide))
        found = dot(coefficients, chosen.astype(jnp.float32).astype(jnp.bfloat16))
        found = (found[0:32] + found[32:64]) + found[64:96]
        for half in range(2):
            mats[half, pl.ds(block, 32, stride=SUB), :] = found[:, half * LANES : (half + 1) * LANES]

    fine = lax.broadcasted_iota(jnp.int32, (wide, wide), 0)
    out = lax.broadcasted_iota(jnp.int32, (wide, wide), 1)
    average = jnp.zeros((wide, wide), jnp.float32)
    own_at = NEAR // 2 * OWN
    for level, (first_own, rows) in enumerate(((O0, T0), (O1, T1), (O2, T2), (O3, T3))):
        span = 2**level
        row = out - TABLE_AT[level]
        same = (row >= 0) & (row < rows) & (fine // span == row + (own_at // span - first_own))
        average = jnp.where(same, 1.0 / span, average)
    average = average.astype(jnp.bfloat16)
    used = SUB * ENTRIES
    high, middle, low = three_parts(jnp.concatenate([mats[0, 0:used], mats[1, 0:used]], axis=1))
    levels = (dot(high, average) + dot(middle, average)) + dot(low, average)

    row = lax.broadcasted_iota(jnp.int32, (SUB, wide), 1)
    weight = jnp.zeros((SUB, wide), jnp.float32) + DIFFUSION
    whole = jnp.zeros((SUB, wide), jnp.int32)
    limit = jnp.zeros((SUB, wide), jnp.int32)
    for level, first_own in enumerate((O0, O1, O2, O3)):
        here = row >= TABLE_AT[level]
        weight = jnp.where(here, DIFFUSION / 4.0**level, weight)
        whole = jnp.where(here, row - TABLE_AT[level] - first_own + device * (OWN >> level), whole)
        limit = jnp.where(here, devices * (OWN >> level), limit)
    inside = (whole >= 0) & (whole < limit)
    scale = jnp.where(inside, RELAXATION * weight, 0.0)
    unscale = 1.0 / weight

    n = FIELDS
    block = [[levels[SUB * (n * i + j) : SUB * (n * i + j + 1)] for j in range(n)] for i in range(n)]
    for i in range(n):
        block[i][i] = block[i][i] + 4.0 * weight
    entries = [block[i][j] * unscale for i in range(n) for j in range(n)]
    right = [[None] * n for _ in range(n)]
    for i in range(n):
        right[i][i] = jnp.ones((SUB, wide), jnp.float32)
    for c in range(n):
        lead = 1.0 / block[c][c]
        for j in range(c + 1, n):
            block[c][j] = block[c][j] * lead
        for j in range(n):
            if right[c][j] is not None:
                right[c][j] = right[c][j] * lead
        for i in range(n):
            if i == c:
                continue
            factor = block[i][c]
            for j in range(c + 1, n):
                block[i][j] = block[i][j] - factor * block[c][j]
            for j in range(n):
                if right[c][j] is not None:
                    term = factor * right[c][j]
                    right[i][j] = -term if right[i][j] is None else right[i][j] - term
    entries = [right[i][j] * scale for i in range(n) for j in range(n)] + entries

    group = FIELDS
    into = lax.broadcasted_iota(jnp.int32, (LANES, group * LANES), 0)
    out = lax.broadcasted_iota(jnp.int32, (LANES, group * LANES), 1)
    same = (into // (3 * SUB) == out // LANES) & (into % SUB == out % LANES // SPREAD)
    widen = same.astype(jnp.float32).astype(jnp.bfloat16)
    parts[...] = jnp.zeros_like(parts)
    for first in range(0, len(entries), group):
        for i in range(group):
            for p, part in enumerate(three_parts(entries[first + i])):
                start = (3 * i + p) * SUB
                parts[start : start + SUB, :] = part.astype(jnp.float32)
        turned = jnp.transpose(parts[...])[0:TABLE_ROWS].astype(jnp.bfloat16)
        wide_rows = dot(turned, widen)
        for i in range(group):
            table[first + i] = wide_rows[:, i * LANES : (i + 1) * LANES]


def turn(first_sub, inward):
    into = lax.broadcasted_iota(jnp.int32, (SUB * LANES, 2 * LANES), 0)
    out = lax.broadcasted_iota(jnp.int32, (1, 2 * LANES), 1)
    if inward:
        wanted = (out % LANES) * SUB + first_sub + out // LANES
    else:
        cell = out + first_sub * LANES
        wanted = (cell % SUB) * LANES + cell // SUB
    return (into == wanted).astype(jnp.float32).astype(jnp.bfloat16)


def split_kernel(where_ref, state_ref, forcing_ref, state_rows, forcing_rows, send_a, send_b, parts, held_in, sems):
    copies = [
        pltpu.make_async_copy(source, held_in.at[i], sems.at[i])
        for i, source in enumerate((state_ref, forcing_ref))
    ]
    for copy in copies:
        copy.start()
    odd = where_ref[0] % 2
    held = 2 * FIELDS * OWN
    for which, copy in enumerate(copies):
        copy.wait()
        for field in range(FIELDS):
            for p, part in enumerate(three_parts(held_in[which, field])):
                start = p * held + (which * FIELDS + field) * OWN
                parts[start : start + OWN, :] = part

    def two_subs(index):
        values = dot(parts[...], turn(2 * index, True))
        values = (values[:held] + values[held : 2 * held]) + values[2 * held :]
        for which, target in enumerate((state_rows, forcing_rows)):
            for field in range(FIELDS):
                start = (which * FIELDS + field) * OWN
                for half in range(2):
                    target[field, pl.ds(2 * index + half, OWN, stride=SUB), :] = values[
                        start : start + OWN, half * LANES : (half + 1) * LANES
                    ]

    rows_loop(0, SUB // 2, two_subs)
    low, high = 0, (OWN - FINE_HALO) * SUB
    size = FINE_HALO * SUB
    for which, rows in enumerate((state_rows, forcing_rows)):
        for field in range(FIELDS):
            first = rows[field, low : low + size, :]
            last = rows[field, high : high + size, :]
            send_a[which * FIELDS + field] = jnp.where(odd == 1, first, last)
            send_b[which * FIELDS + field] = jnp.where(odd == 1, last, first)


def place_halo(where_ref, buffer, own_rows, got_a, got_b, first, padded):
    odd = where_ref[0] % 2
    row_a = jnp.where(odd == 1, O0 - FINE_HALO, O0 + OWN)
    row_b = jnp.where(odd == 1, O0 + OWN, O0 - FINE_HALO)

    def put_row(field, row, value):
        if padded:
            put(buffer, field, row, 0, value)
        else:
            buffer[field, row] = value

    def own(row):
        start = pl.multiple_of(row * SUB, SUB)
        for field in range(FIELDS):
            put_row(field, O0 + row, own_rows[field, pl.ds(start, SUB), :])

    def halo(row):
        start = pl.multiple_of(row * SUB, SUB)
        for field in range(FIELDS):
            put_row(field, row_a + row, got_a[first + field, pl.ds(start, SUB), :])
            put_row(field, row_b + row, got_b[first + field, pl.ds(start, SUB), :])

    if own_rows is not None:
        rows_loop(0, OWN, own)
    rows_loop(0, FINE_HALO, halo)


def interior_kernel(fresh, where_ref, state, force, table, v0, tmp0, c1, q1, tmp1):
    def own(row):
        start = pl.multiple_of(row * SUB, SUB)
        for field in range(FIELDS):
            put(v0, field, O0 + row, 0, state[field, pl.ds(start, SUB), :])

    rows_loop(0, OWN, own)
    edges(v0, 0, O0, O0 + OWN)
    if fresh:
        source = lambda field, row: force[field, pl.ds(pl.multiple_of((row - O0) * SUB, SUB), SUB), :]
    else:
        source = lambda field, row: force[field, row]
    sweep(source, v0, tmp0, table, 0, O0 + 1, O0 + OWN - 1, batch=5)
    sweep(source, tmp0, v0, table, 0, O0 + 2, O0 + OWN - 2, batch=4)
    descend(source, v0, table, 0, c1, q1, tmp1, O1 + INNER, O1 + OWN // 2 - INNER)


def down_kernel(fresh, *refs):
    if fresh:
        (where_ref, v0_in, tmp0_in, c1_in, q1_in, tmp1_in, force, got_a, got_b, table,
         v0, v1, s1, c1, send, f0, tmp0, tmp1, q1) = refs
    else:
        (where_ref, v0_in, tmp0_in, c1_in, q1_in, tmp1_in, got_a, got_b, f0, table,
         v0, v1, s1, c1, send, tmp0, tmp1, q1) = refs
    half = OWN // 2

    def take(target, source, level, first, last):
        rows = slice(at(first, level) - 2**level, at(last, level) - 2**level)
        target[:, rows, :] = source[:, rows, :]

    take(v0, v0_in, 0, O0, O0 + OWN)
    take(tmp0, tmp0_in, 0, O0 + 1, O0 + 3)
    take(tmp0, tmp0_in, 0, O0 + OWN - 3, O0 + OWN - 1)
    inner = slice(O1 + INNER, O1 + half - INNER)
    take(c1, c1_in, 1, inner.start, inner.stop)
    take(tmp1, tmp1_in, 1, inner.start, inner.stop)
    q1[:, inner] = q1_in[:, inner]

    place_halo(where_ref, v0, None, got_a, got_b, 0, True)
    edges(v0, 0, O0 - FINE_HALO, O0)
    edges(v0, 0, O0 + OWN, O0 + OWN + FINE_HALO)
    if fresh:
        place_halo(where_ref, f0, force, got_a, got_b, FIELDS, False)
    fine_source = lambda field, row: f0[field, row]
    for swept, (old, new) in enumerate(((v0, tmp0), (tmp0, v0))):
        for first in (O0 - FINE_HALO + swept, O0 + OWN - 1 - swept):
            sweep(fine_source, old, new, table, 0, first, first + FINE_HALO + 1)
    for first in (O1 - 4, O1 + half - INNER):
        descend(fine_source, v0, table, 0, c1, q1, tmp1, first, first + 4 + INNER)
    make_source(c1, q1, s1, table, 1, O1 - 3, O1 + half + 3)
    first_source = lambda field, row: s1[field, row]
    sweep(first_source, tmp1, v1, table, 1, O1 - 3, O1 + half + 3)

    sub = sub_iota()

    def to_second(index):
        coarse, rest = coarsen(first_source, v1, table, 1, index + O1 // 2)
        return coarse + rest

    def pack(index, values):
        group, place = index // GROUP, index % GROUP
        mine = (sub & (GROUP - 1)) == place
        for which in range(2 * FIELDS):
            send[group, which] = jnp.where(mine, values[which], send[group, which])

    send[...] = jnp.zeros_like(send)
    batches(0, OWN // 4, COARSEN_BATCH, to_second, pack)


def spread(source, index, which, place):
    take = lambda sub: jnp.broadcast_to(source[index, which, sub : sub + 1, :], (SUB, LANES))
    return jnp.where(sub_iota() < GROUP, take(place), take(GROUP + place))


def up_kernel(last, *refs):
    if last:
        (where_ref, own, got_a, got_b, got_a2, v0, f0, v1, s1, c1, table, out,
         parts, tmp0, work0, tmp1, work1, c2, q2, s2, v2, tmp2, c3, q3, s3, v3, tmp3) = refs
    else:
        (where_ref, own, got_a, got_b, got_a2, v0, f0, v1, s1, c1, table, out,
         send_a, send_b, tmp0, work0, tmp1, work1, c2, q2, s2, v2, tmp2, c3, q3, s3, v3, tmp3) = refs
    odd = where_ref[0] % 2

    def unpack(source, index, group):
        for place in range(GROUP):
            row = group * GROUP + place
            coarse = [spread(source, index, f, place) for f in range(FIELDS)]
            rest = [spread(source, index, FIELDS + f, place) for f in range(FIELDS)]
            start = first_sweep(coarse, rest, table, 2, row)
            for field in range(FIELDS):
                put(c2, field, row, 2, coarse[field])
                q2[field, row] = rest[field]
                put(tmp2, field, row, 2, start[field])

    pick = lambda a, b: jnp.where(odd == 1, b, a)
    rows_loop(0, 2, lambda i: unpack(own, i, 4 + i))
    rows_loop(0, 2, lambda i: unpack(got_a, i, pick(6, 2) + i))
    rows_loop(0, 3, lambda i: unpack(got_b, i, pick(1, 6) + i))
    rows_loop(0, 1, lambda i: unpack(got_a2, pick(0, 2) + i, pick(8, 1) + i))

    quarter, eighth = OWN // 4, OWN // 8
    for ref in (c2, tmp2):
        edges(ref, 2, O2 - 12, O2 + quarter + 12)
    make_source(c2, q2, s2, table, 2, O2 - 11, O2 + quarter + 11)
    second_source = lambda field, row: s2[field, row]
    sweep(second_source, tmp2, v2, table, 2, O2 - 11, O2 + quarter + 11)

    descend(second_source, v2, table, 2, c3, q3, tmp3, O3 - 5, O3 + eighth + 5)
    make_source(c3, q3, s3, table, 3, O3 - 4, O3 + eighth + 4)
    third_source = lambda field, row: s3[field, row]
    sweep(third_source, tmp3, v3, table, 3, O3 - 4, O3 + eighth + 4)
    sweep(third_source, v3, tmp3, table, 3, O3 - 3, O3 + eighth + 3)
    sweep(third_source, tmp3, v3, table, 3, O3 - 2, O3 + eighth + 2, False)
    correct(v2, v2, v3, c3, 2, 0, O2 - 4, O2 + quarter + 4)
    sweep(second_source, v2, tmp2, table, 2, O2 - 3, O2 + quarter + 3)
    sweep(second_source, tmp2, v2, table, 2, O2 - 2, O2 + quarter + 2, False)

    half = OWN // 2
    first_source = lambda field, row: s1[field, row]
    correct(work1, v1, v2, c2, 1, O2 - O1 // 2, O1 - 3, O1 + half + 3)
    sweep(first_source, work1, tmp1, table, 1, O1 - 2, O1 + half + 2)
    sweep(first_source, tmp1, work1, table, 1, O1 - 1, O1 + half + 1, False)

    fine_source = lambda field, row: f0[field, row]
    correct(work0, v0, work1, c1, 0, 0, O0 - 2, O0 + OWN + 2)
    sweep(fine_source, work0, tmp0, table, 0, O0 - 1, O0 + OWN + 1)
    sweep(fine_source, tmp0, work0, table, 0, O0, O0 + OWN, False)

    if last:
        held = FIELDS * OWN
        for field in range(FIELDS):
            for sub in range(SUB):
                value = work0[field, pl.ds(at(O0, 0) + sub, OWN, stride=stride_of(0)), :]
                for p, part in enumerate(three_parts(value)):
                    start = p * held + field * OWN
                    parts[start : start + OWN, sub * LANES : (sub + 1) * LANES] = part

        def columns_out(index):
            values = dot(parts[...], turn(2 * index, False))
            values = (values[:held] + values[held : 2 * held]) + values[2 * held :]
            cells = pl.ds(pl.multiple_of(index * 2 * LANES, 2 * LANES), 2 * LANES)
            for field in range(FIELDS):
                out[field, :, cells] = values[field * OWN : (field + 1) * OWN]

        rows_loop(0, SUB // 2, columns_out)
        return

    def leave(row):
        start = pl.multiple_of(row * SUB, SUB)
        for field in range(FIELDS):
            out[field, pl.ds(start, SUB), :] = tile(work0, field, O0 + row, 0)

    rows_loop(0, OWN, leave)
    from_a, from_b = pick(OWN - FINE_HALO, 0), pick(0, OWN - FINE_HALO)

    def edge(row):
        start = pl.multiple_of(row * SUB, SUB)
        for field in range(FIELDS):
            send_a[field, pl.ds(start, SUB), :] = tile(work0, field, O0 + from_a + row, 0)
            send_b[field, pl.ds(start, SUB), :] = tile(work0, field, O0 + from_b + row, 0)

    rows_loop(0, FINE_HALO, edge)


def relay_kernel(where_ref, own, beside, row):
    odd = where_ref[0] % 2
    row[odd] = own[0]
    row[odd + 1] = own[1]
    row[2 - 2 * odd] = beside[odd]


VMEM = pl.BlockSpec(memory_space=pltpu.VMEM)
SMEM = pl.BlockSpec(memory_space=pltpu.SMEM)
ANY = pl.BlockSpec(memory_space=pltpu.HBM)


def f32(*shape):
    return jax.ShapeDtypeStruct(shape, jnp.float32)


def scratch(*shape):
    return pltpu.VMEM(shape, jnp.float32)


def padded(rows, level):
    return (FIELDS, padded_rows(rows, level), LANES)


def plain(rows):
    return (FIELDS, rows, SUB, LANES)


def call(kernel, name, grant, outs, operands, scratches=(), raw=False):
    return pl.pallas_call(
        kernel,
        out_shape=outs,
        in_specs=[SMEM] + [ANY if raw else VMEM] * (len(operands) - 1),
        out_specs=[VMEM] * len(outs),
        scratch_shapes=list(scratches),
        name=name,
        compiler_params=pltpu.CompilerParams(vmem_limit_bytes=grant * 1024 * 1024),
    )(*operands)


def in_hbm(array):
    return pltpu.with_memory_space_constraint(array, pltpu.HBM)


def per_device(initial_state, forcing, coefficients, region_ids):
    size = lax.axis_size("axial")
    device = lax.axis_index("axial")
    assert initial_state.shape == (FIELDS, OWN, SUB * LANES)
    assert region_ids.shape == (OWN, SUB)
    where_ref = jnp.stack([device, jnp.int32(size)]).astype(jnp.int32)
    odd = device % 2
    pair_a = [(i, i ^ 1) for i in range(size)]
    pair_b = [(i, i + 1 if i % 2 else i - 1) for i in range(1, size - 1)]
    swap_a = lambda x: lax.ppermute(x, "axial", pair_a)
    swap_b = lambda x: lax.ppermute(x, "axial", pair_b)

    share = coefficients.shape[1]
    regions = share * size
    per_tile = LANES // OWN
    (gathered,) = call(
        functools.partial(prep_kernel, share),
        "prep",
        4,
        [f32(regions + SUB * -(-size // per_tile), LANES)],
        [where_ref, in_hbm(coefficients.T), in_hbm(region_ids.T)],
        [
            scratch(share, ENTRIES),
            pltpu.VMEM((SUB, OWN), jnp.int32),
            pltpu.SemaphoreType.DMA((2,)),
        ],
        True,
    )

    def doubled(held, step):
        return held + lax.ppermute(held, "axial", [(i, i ^ step) for i in range(size)])

    state, force, send_a, send_b = call(
        split_kernel,
        "split", 12,
        [f32(FIELDS, OWN * SUB, LANES)] * 2 + [f32(2 * FIELDS, FINE_HALO * SUB, LANES)] * 2,
        [where_ref, in_hbm(initial_state), in_hbm(forcing)],
        [
            pltpu.VMEM((3 * 2 * FIELDS * OWN, SUB * LANES), jnp.bfloat16),
            scratch(2, FIELDS, OWN, SUB * LANES),
            pltpu.SemaphoreType.DMA((2,)),
        ],
        True,
    )
    step = 1
    while step < min(size, 8):
        gathered = doubled(gathered, step)
        step *= 2
    gathered, send_a, send_b = lax.optimization_barrier((gathered, send_a, send_b))
    got_b, got_a = swap_b(send_b), swap_a(send_a)
    while step < size:
        gathered = doubled(gathered, step)
        step *= 2
    (table,) = call(
        functools.partial(tables_kernel, regions),
        "tables", 12,
        [f32(2 * ENTRIES, TABLE_ROWS, LANES)],
        [where_ref, gathered],
        [scratch(2, 32 * SUB, LANES), scratch(LANES, 2 * LANES)],
    )

    f0 = None
    for cycle in range(CYCLES):
        fresh = cycle == 0
        inner = call(
            functools.partial(interior_kernel, fresh), "interior", 4,
            [f32(*padded(T0, 0))] * 2 + [f32(*padded(T1, 1)), f32(*plain(T1)), f32(*padded(T1, 1))],
            [where_ref, state, force if fresh else f0, table],
        )
        outs = [f32(*padded(T0, 0)), f32(*padded(T1, 1)), f32(*plain(T1)), f32(*padded(T1, 1)),
                f32(2, 2 * FIELDS, SUB, LANES)]
        temps = [scratch(*padded(T0, 0)), scratch(*padded(T1, 1)), scratch(*plain(T1))]
        if fresh:
            v0, v1, s1, c1, own, f0 = call(
                functools.partial(down_kernel, True), "down_fresh", 14, outs + [f32(*plain(T0))],
                [where_ref, *inner, force, got_a, got_b, table], temps,
            )
        else:
            v0, v1, s1, c1, own = call(
                functools.partial(down_kernel, False), "down", 14, outs,
                [where_ref, *inner, got_a, got_b, f0, table], temps,
            )
        beside = swap_a(own)
        (row,) = call(
            relay_kernel, "relay", 2, [f32(3, 2 * FIELDS, SUB, LANES)], [where_ref, own, beside]
        )
        far = swap_b(row)
        beyond = swap_a(far)
        operands = [where_ref, own, beside, far, beyond, v0, f0, v1, s1, c1, table]
        temps = [scratch(*padded(T0, 0))] * 2 + [scratch(*padded(T1, 1))] * 2
        temps += [scratch(*padded(T2, 2)), scratch(*plain(T2)), scratch(*plain(T2)), scratch(*padded(T2, 2)), scratch(*padded(T2, 2))]
        temps += [scratch(*padded(T3, 3)), scratch(*plain(T3)), scratch(*plain(T3)), scratch(*padded(T3, 3)), scratch(*padded(T3, 3))]
        if cycle == CYCLES - 1:
            return call(
                functools.partial(up_kernel, True), "up_last", 26,
                [f32(FIELDS, OWN, SUB * LANES)], operands,
                [pltpu.VMEM((3 * FIELDS * OWN, SUB * LANES), jnp.bfloat16)] + temps,
            )[0]
        state, send_a, send_b = call(
            functools.partial(up_kernel, False), "up", 26,
            [f32(FIELDS, OWN * SUB, LANES)] + [f32(FIELDS, FINE_HALO * SUB, LANES)] * 2,
            operands, temps,
        )
        got_b, got_a = swap_b(send_b), swap_a(send_a)


def solution(mesh):
    placed = (
        P("sample", "axial", None),
        P("sample", "axial", None),
        P("sample", "axial"),
        P("axial", None),
    )
    return jax.shard_map(
        per_device,
        mesh=mesh,
        in_specs=placed,
        out_specs=P("sample", "axial", None),
        check_vma=False,
    )
```

```python
import functools

import jax
import jax.numpy as jnp
from jax import lax
from jax.experimental import pallas as pl
from jax.experimental.pallas import tpu as pltpu
from jax.sharding import PartitionSpec as P

DIFFUSION = 1.0
RELAXATION = 0.8
SOURCE_GAIN = 0.05
CYCLES = 2

FIELDS = 5
ENTRIES = FIELDS * FIELDS
SUB, LANES = 8, 128

OWN = 32
FINE_HALO = 11
T0, O0 = 64, 16
T1, O1 = 32, 8
T2, O2 = 40, 16
T3, O3 = 20, 8
COARSEST = 3
EDGE_BATCH = 10
GROUP = 4
SPREAD = 16


def stride_of(level):
    return SUB + (0 if level == COARSEST else 2 * 2**level)


def padded_rows(rows, level):
    return stride_of(level) * (rows + SUB)


def at(row, level):
    return stride_of(level) * row + (0 if level == COARSEST else 2**level)


def lane_iota():
    return lax.broadcasted_iota(jnp.int32, (SUB, LANES), 1)


def sub_iota():
    return lax.broadcasted_iota(jnp.int32, (SUB, LANES), 0)


def tile(ref, field, row, level):
    return ref[field, pl.ds(at(row, level), SUB), :]


def put(ref, field, row, level, value):
    ref[field, pl.ds(at(row, level), SUB), :] = value


def edges(ref, level, first, last):
    if level == COARSEST:
        return
    width, stride, lane = 2**level, stride_of(level), lane_iota()
    places = [(row, field) for row in range(first, last, SUB) for field in range(FIELDS)]
    for part in range(0, len(places), EDGE_BATCH):
        written = []
        for row, field in places[part : part + EDGE_BATCH]:
            rows = lambda sub, row=row, field=field: (
                field, pl.ds(at(row, level) + sub, SUB, stride=stride), slice(None)
            )
            before = jnp.where(lane == 0, 0.0, pltpu.roll(ref[rows(SUB - 1)], 1, 1))
            after = jnp.where(lane == LANES - 1, 0.0, pltpu.roll(ref[rows(0)], LANES - 1, 1))
            written.append((rows, before, after))
        for rows, before, after in written:
            for i in range(width):
                ref[rows(i - width)] = before
                ref[rows(SUB + i)] = after


def rows_loop(first, last, body):
    def step(row, carry):
        body(row)
        return carry

    lax.fori_loop(first, last, step, 0)


def batches(first, last, batch, compute, store):
    def body(index):
        rows = [first + index * batch + i for i in range(batch)]
        results = [compute(row) for row in rows]
        for row, result in zip(rows, results):
            store(row, result)

    rows_loop(0, -(-(last - first) // batch), body)


def neighbours(ref, row, level):
    start, width, stride = at(row, level), 2**level, stride_of(level)
    lane = lane_iota()
    sums, centres = [], []
    for field in range(FIELDS):
        load = lambda first, field=field: ref[field, pl.ds(first, SUB), :]
        centre = load(start)
        if level == COARSEST:
            radial = jnp.where(lane == 0, 0.0, pltpu.roll(centre, 1, 1)) + jnp.where(
                lane == LANES - 1, 0.0, pltpu.roll(centre, LANES - 1, 1)
            )
        else:
            radial = load(start - width) + load(start + width)
        sums.append(radial + (load(start - stride) + load(start + stride)))
        centres.append(centre)
    return sums, centres


def block_times(table, level, row, first, vectors):
    row = TABLE_AT[level] + row
    out = []
    for i in range(FIELDS):
        total = None
        for j in range(FIELDS):
            entry = first + FIELDS * i + j
            term = jnp.broadcast_to(table[entry, pl.ds(row, 1), :], (SUB, LANES)) * vectors[j]
            total = term if total is None else total + term
        out.append(total)
    return out


MATRIX_AT = ENTRIES
TABLE_AT = (0, T0, T0 + T1, T0 + T1 + T2)
TABLE_ROWS = 160
NEAR = 5


def gain_of(level):
    return SOURCE_GAIN * 4.0**level / DIFFUSION


def sweep(source_of, old, new, table, level, first, last, more=True, batch=None):
    gain = gain_of(level)

    def compute(row):
        sums, centres = neighbours(old, row, level)
        rest = [
            (source_of(field, row) + sums[field]) - gain * jnp.tanh(centres[field])
            for field in range(FIELDS)
        ]
        moved = block_times(table, level, row, 0, rest)
        return [(1.0 - RELAXATION) * centres[f] + moved[f] for f in range(FIELDS)]

    def store(row, values):
        for field in range(FIELDS):
            put(new, field, row, level, values[field])

    batches(first, last, batch or SWEEP_BATCH, compute, store)
    if more:
        edges(new, level, first, last)


def residual(source_of, values, table, level, row):
    gain = gain_of(level)
    sums, centres = neighbours(values, row, level)
    applied = block_times(table, level, row, MATRIX_AT, centres)
    left = [
        ((source_of(field, row) + sums[field]) - gain * jnp.tanh(centres[field])) - applied[field]
        for field in range(FIELDS)
    ]
    return left, centres


def pair_sum(value, level):
    width = 2**level
    other = pltpu.roll(value, SUB - width, 0)
    if 2 * width != SUB:
        other = jnp.where((sub_iota() & width) == 0, other, pltpu.roll(value, width, 0))
    return value + other


def coarsen(source_of, values, table, level, row):
    upper_r, upper_v = residual(source_of, values, table, level, 2 * row)
    lower_r, lower_v = residual(source_of, values, table, level, 2 * row + 1)
    coarse = [0.25 * pair_sum(upper_v[f] + lower_v[f], level) for f in range(FIELDS)]
    rest = [pair_sum(upper_r[f] + lower_r[f], level) for f in range(FIELDS)]
    return coarse, rest


def first_sweep(coarse, rest, table, level, row):
    moved = block_times(table, level, row, 0, rest)
    return [coarse[f] + moved[f] for f in range(FIELDS)]


def descend(source_of, values, table, level, c, q, first_values, first, last):
    def compute(row):
        coarse, rest = coarsen(source_of, values, table, level, row)
        return coarse, rest, first_sweep(coarse, rest, table, level + 1, row)

    def store(row, results):
        for field in range(FIELDS):
            put(c, field, row, level + 1, results[0][field])
            q[field, row] = results[1][field]
            put(first_values, field, row, level + 1, results[2][field])

    batches(first, last, COARSEN_BATCH, compute, store)
    edges(c, level + 1, first, last)
    edges(first_values, level + 1, first, last)


def make_source(coarse, rest, source, table, level, first, last):
    gain = gain_of(level)

    def compute(row):
        sums, centres = neighbours(coarse, row, level)
        applied = block_times(table, level, row, MATRIX_AT, centres)
        return [
            (applied[f] - sums[f]) + (gain * jnp.tanh(centres[f]) + rest[f, row])
            for f in range(FIELDS)
        ]

    def store(row, values):
        for field in range(FIELDS):
            source[field, row] = values[field]

    batches(first, last, SWEEP_BATCH, compute, store)


def correct(new, fine, after, before, level, offset, first, last):
    def body(index):
        coarse_row = first // 2 + index + offset
        row = first // 2 * 2 + 2 * index
        for field in range(FIELDS):
            change = tile(after, field, coarse_row, level + 1) - tile(before, field, coarse_row, level + 1)
            put(new, field, row, level, tile(fine, field, row, level) + change)
            put(new, field, row + 1, level, tile(fine, field, row + 1, level) + change)

    rows_loop(0, (last + 1) // 2 - first // 2, body)
    edges(new, level, first, last)


SWEEP_BATCH = 4
INNER = 2
COARSEN_BATCH = 2


def three_parts(value):
    high = value.astype(jnp.bfloat16)
    rest = value - high.astype(jnp.float32)
    middle = rest.astype(jnp.bfloat16)
    low = (rest - middle.astype(jnp.float32)).astype(jnp.bfloat16)
    return high, middle, low


def dot(left, right):
    return jnp.dot(left, right, preferred_element_type=jnp.float32)


def prep_kernel(share, where_ref, coefficients_ref, ids_ref, out, own_coefficients, own_ids, sems):
    device, devices = where_ref[0], where_ref[1]
    copies = [
        pltpu.make_async_copy(coefficients_ref, own_coefficients, sems.at[0]),
        pltpu.make_async_copy(ids_ref, own_ids, sems.at[1]),
    ]
    for copy in copies:
        copy.start()
    out[...] = jnp.zeros_like(out)
    for copy in copies:
        copy.wait()
    for i in range(share):
        out[pl.ds(device * share + i, 1), 0:ENTRIES] = own_coefficients[i : i + 1, :]
    ids = own_ids[...].astype(jnp.float32)
    per_tile = LANES // OWN
    start = pl.multiple_of(devices * share + device // per_tile * SUB, SUB)
    for place in range(per_tile):

        @pl.when(device % per_tile == place)
        def _():
            out[pl.ds(start, SUB), place * OWN : (place + 1) * OWN] = ids


def tables_kernel(regions, where_ref, regions_ref, table, mats, parts):
    device, devices = where_ref[0], where_ref[1]
    wide = 2 * LANES
    lane = lane_iota()
    ids = [jnp.full((SUB, LANES), -1.0, jnp.float32)] * 2
    per_tile = LANES // OWN
    for i in range(NEAR):
        owner = jnp.clip(device + (i - NEAR // 2), 0, devices - 1)
        start = pl.multiple_of(regions + owner // per_tile * SUB, SUB)
        held = regions_ref[pl.ds(start, SUB), :]
        turned = pltpu.roll(held, ((i % per_tile) - owner % per_tile + per_tile) % per_tile * OWN, 1)
        place = i // per_tile
        ids[place] = jnp.where(lane // OWN == i % per_tile, turned, ids[place])
    ids = jnp.concatenate(ids, axis=1).astype(jnp.int32)

    coefficients = jnp.transpose(regions_ref[0:regions, :])[0:32]
    coefficients = jnp.concatenate(three_parts(coefficients), axis=0)
    region = lax.broadcasted_iota(jnp.int32, (regions, wide), 0)
    for block in range(SUB):
        chosen = region == jnp.broadcast_to(ids[block : block + 1], (regions, wide))
        found = dot(coefficients, chosen.astype(jnp.float32).astype(jnp.bfloat16))
        found = (found[0:32] + found[32:64]) + found[64:96]
        for half in range(2):
            mats[half, pl.ds(block, 32, stride=SUB), :] = found[:, half * LANES : (half + 1) * LANES]

    fine = lax.broadcasted_iota(jnp.int32, (wide, wide), 0)
    out = lax.broadcasted_iota(jnp.int32, (wide, wide), 1)
    average = jnp.zeros((wide, wide), jnp.float32)
    own_at = NEAR // 2 * OWN
    for level, (first_own, rows) in enumerate(((O0, T0), (O1, T1), (O2, T2), (O3, T3))):
        span = 2**level
        row = out - TABLE_AT[level]
        same = (row >= 0) & (row < rows) & (fine // span == row + (own_at // span - first_own))
        average = jnp.where(same, 1.0 / span, average)
    average = average.astype(jnp.bfloat16)
    used = SUB * ENTRIES
    high, middle, low = three_parts(jnp.concatenate([mats[0, 0:used], mats[1, 0:used]], axis=1))
    levels = (dot(high, average) + dot(middle, average)) + dot(low, average)

    row = lax.broadcasted_iota(jnp.int32, (SUB, wide), 1)
    weight = jnp.zeros((SUB, wide), jnp.float32) + DIFFUSION
    whole = jnp.zeros((SUB, wide), jnp.int32)
    limit = jnp.zeros((SUB, wide), jnp.int32)
    for level, first_own in enumerate((O0, O1, O2, O3)):
        here = row >= TABLE_AT[level]
        weight = jnp.where(here, DIFFUSION / 4.0**level, weight)
        whole = jnp.where(here, row - TABLE_AT[level] - first_own + device * (OWN >> level), whole)
        limit = jnp.where(here, devices * (OWN >> level), limit)
    inside = (whole >= 0) & (whole < limit)
    scale = jnp.where(inside, RELAXATION * weight, 0.0)
    unscale = 1.0 / weight

    n = FIELDS
    block = [[levels[SUB * (n * i + j) : SUB * (n * i + j + 1)] for j in range(n)] for i in range(n)]
    for i in range(n):
        block[i][i] = block[i][i] + 4.0 * weight
    entries = [block[i][j] * unscale for i in range(n) for j in range(n)]
    right = [[None] * n for _ in range(n)]
    for i in range(n):
        right[i][i] = jnp.ones((SUB, wide), jnp.float32)
    for c in range(n):
        lead = 1.0 / block[c][c]
        for j in range(c + 1, n):
            block[c][j] = block[c][j] * lead
        for j in range(n):
            if right[c][j] is not None:
                right[c][j] = right[c][j] * lead
        for i in range(n):
            if i == c:
                continue
            factor = block[i][c]
            for j in range(c + 1, n):
                block[i][j] = block[i][j] - factor * block[c][j]
            for j in range(n):
                if right[c][j] is not None:
                    term = factor * right[c][j]
                    right[i][j] = -term if right[i][j] is None else right[i][j] - term
    entries = [right[i][j] * scale for i in range(n) for j in range(n)] + entries

    group = FIELDS
    into = lax.broadcasted_iota(jnp.int32, (LANES, group * LANES), 0)
    out = lax.broadcasted_iota(jnp.int32, (LANES, group * LANES), 1)
    same = (into // (3 * SUB) == out // LANES) & (into % SUB == out % LANES // SPREAD)
    widen = same.astype(jnp.float32).astype(jnp.bfloat16)
    parts[...] = jnp.zeros_like(parts)
    for first in range(0, len(entries), group):
        for i in range(group):
            for p, part in enumerate(three_parts(entries[first + i])):
                start = (3 * i + p) * SUB
                parts[start : start + SUB, :] = part.astype(jnp.float32)
        turned = jnp.transpose(parts[...])[0:TABLE_ROWS].astype(jnp.bfloat16)
        wide_rows = dot(turned, widen)
        for i in range(group):
            table[first + i] = wide_rows[:, i * LANES : (i + 1) * LANES]


def turn(first_sub, inward):
    into = lax.broadcasted_iota(jnp.int32, (SUB * LANES, 2 * LANES), 0)
    out = lax.broadcasted_iota(jnp.int32, (1, 2 * LANES), 1)
    if inward:
        wanted = (out % LANES) * SUB + first_sub + out // LANES
    else:
        cell = out + first_sub * LANES
        wanted = (cell % SUB) * LANES + cell // SUB
    return (into == wanted).astype(jnp.float32).astype(jnp.bfloat16)


def split_kernel(source_ref, target, parts, held_in, sem):
    copy = pltpu.make_async_copy(source_ref, held_in, sem)
    copy.start()
    held = FIELDS * OWN
    copy.wait()
    for field in range(FIELDS):
        for p, part in enumerate(three_parts(held_in[field])):
            start = p * held + field * OWN
            parts[start : start + OWN, :] = part

    def two_subs(index):
        values = dot(parts[...], turn(2 * index, True))
        values = (values[:held] + values[held : 2 * held]) + values[2 * held :]
        for field in range(FIELDS):
            for half in range(2):
                target[field, pl.ds(2 * index + half, OWN, stride=SUB), :] = values[
                    field * OWN : (field + 1) * OWN, half * LANES : (half + 1) * LANES
                ]

    rows_loop(0, SUB // 2, two_subs)


def split_state_kernel(where_ref, state_ref, state_rows, *scratches):
    split_kernel(state_ref, state_rows, *scratches)


def split_forcing_kernel(where_ref, forcing_ref, state_rows, forcing_rows, send_a, send_b, *scratches):
    split_kernel(forcing_ref, forcing_rows, *scratches)
    odd = where_ref[0] % 2
    low, high = 0, (OWN - FINE_HALO) * SUB
    size = FINE_HALO * SUB
    for which, rows in enumerate((state_rows, forcing_rows)):
        for field in range(FIELDS):
            first = rows[field, low : low + size, :]
            last = rows[field, high : high + size, :]
            send_a[which * FIELDS + field] = jnp.where(odd == 1, first, last)
            send_b[which * FIELDS + field] = jnp.where(odd == 1, last, first)


def place_halo(where_ref, buffer, own_rows, got_a, got_b, first, padded):
    odd = where_ref[0] % 2
    row_a = jnp.where(odd == 1, O0 - FINE_HALO, O0 + OWN)
    row_b = jnp.where(odd == 1, O0 + OWN, O0 - FINE_HALO)

    def put_row(field, row, value):
        if padded:
            put(buffer, field, row, 0, value)
        else:
            buffer[field, row] = value

    def own(row):
        start = pl.multiple_of(row * SUB, SUB)
        for field in range(FIELDS):
            put_row(field, O0 + row, own_rows[field, pl.ds(start, SUB), :])

    def halo(row):
        start = pl.multiple_of(row * SUB, SUB)
        for field in range(FIELDS):
            put_row(field, row_a + row, got_a[first + field, pl.ds(start, SUB), :])
            put_row(field, row_b + row, got_b[first + field, pl.ds(start, SUB), :])

    if own_rows is not None:
        rows_loop(0, OWN, own)
    rows_loop(0, FINE_HALO, halo)


def interior_kernel(fresh, where_ref, state, force, table, v0, tmp0, c1, q1, tmp1):
    def own(row):
        start = pl.multiple_of(row * SUB, SUB)
        for field in range(FIELDS):
            put(v0, field, O0 + row, 0, state[field, pl.ds(start, SUB), :])

    rows_loop(0, OWN, own)
    edges(v0, 0, O0, O0 + OWN)
    if fresh:
        source = lambda field, row: force[field, pl.ds(pl.multiple_of((row - O0) * SUB, SUB), SUB), :]
    else:
        source = lambda field, row: force[field, row]
    sweep(source, v0, tmp0, table, 0, O0 + 1, O0 + OWN - 1, batch=5)
    sweep(source, tmp0, v0, table, 0, O0 + 2, O0 + OWN - 2, batch=4)
    descend(source, v0, table, 0, c1, q1, tmp1, O1 + INNER, O1 + OWN // 2 - INNER)


def down_kernel(fresh, *refs):
    if fresh:
        (where_ref, v0_in, tmp0_in, c1_in, q1_in, tmp1_in, force, got_a, got_b, table,
         v0, v1, s1, c1, send, f0, tmp0, tmp1, q1) = refs
    else:
        (where_ref, v0_in, tmp0_in, c1_in, q1_in, tmp1_in, got_a, got_b, f0, table,
         v0, v1, s1, c1, send, tmp0, tmp1, q1) = refs
    half = OWN // 2

    def take(target, source, level, first, last):
        rows = slice(at(first, level) - 2**level, at(last, level) - 2**level)
        target[:, rows, :] = source[:, rows, :]

    take(v0, v0_in, 0, O0, O0 + OWN)
    take(tmp0, tmp0_in, 0, O0 + 1, O0 + 3)
    take(tmp0, tmp0_in, 0, O0 + OWN - 3, O0 + OWN - 1)
    inner = slice(O1 + INNER, O1 + half - INNER)
    take(c1, c1_in, 1, inner.start, inner.stop)
    take(tmp1, tmp1_in, 1, inner.start, inner.stop)
    q1[:, inner] = q1_in[:, inner]

    place_halo(where_ref, v0, None, got_a, got_b, 0, True)
    edges(v0, 0, O0 - FINE_HALO, O0)
    edges(v0, 0, O0 + OWN, O0 + OWN + FINE_HALO)
    if fresh:
        place_halo(where_ref, f0, force, got_a, got_b, FIELDS, False)
    fine_source = lambda field, row: f0[field, row]
    for swept, (old, new) in enumerate(((v0, tmp0), (tmp0, v0))):
        for first in (O0 - FINE_HALO + swept, O0 + OWN - 1 - swept):
            sweep(fine_source, old, new, table, 0, first, first + FINE_HALO + 1)
    for first in (O1 - 4, O1 + half - INNER):
        descend(fine_source, v0, table, 0, c1, q1, tmp1, first, first + 4 + INNER)
    make_source(c1, q1, s1, table, 1, O1 - 3, O1 + half + 3)
    first_source = lambda field, row: s1[field, row]
    sweep(first_source, tmp1, v1, table, 1, O1 - 3, O1 + half + 3)

    sub = sub_iota()

    def to_second(index):
        coarse, rest = coarsen(first_source, v1, table, 1, index + O1 // 2)
        return coarse + rest

    def pack(index, values):
        group, place = index // GROUP, index % GROUP
        mine = (sub & (GROUP - 1)) == place
        for which in range(2 * FIELDS):
            send[group, which] = jnp.where(mine, values[which], send[group, which])

    send[...] = jnp.zeros_like(send)
    batches(0, OWN // 4, COARSEN_BATCH, to_second, pack)


def spread(source, index, which, place):
    take = lambda sub: jnp.broadcast_to(source[index, which, sub : sub + 1, :], (SUB, LANES))
    return jnp.where(sub_iota() < GROUP, take(place), take(GROUP + place))


def up_kernel(last, *refs):
    if last:
        (where_ref, own, got_a, got_b, got_a2, v0, f0, v1, s1, c1, table, out,
         parts, tmp0, work0, tmp1, work1, c2, q2, s2, v2, tmp2, c3, q3, s3, v3, tmp3) = refs
    else:
        (where_ref, own, got_a, got_b, got_a2, v0, f0, v1, s1, c1, table, out,
         send_a, send_b, tmp0, work0, tmp1, work1, c2, q2, s2, v2, tmp2, c3, q3, s3, v3, tmp3) = refs
    odd = where_ref[0] % 2

    def unpack(source, index, group):
        for place in range(GROUP):
            row = group * GROUP + place
            coarse = [spread(source, index, f, place) for f in range(FIELDS)]
            rest = [spread(source, index, FIELDS + f, place) for f in range(FIELDS)]
            start = first_sweep(coarse, rest, table, 2, row)
            for field in range(FIELDS):
                put(c2, field, row, 2, coarse[field])
                q2[field, row] = rest[field]
                put(tmp2, field, row, 2, start[field])

    pick = lambda a, b: jnp.where(odd == 1, b, a)
    rows_loop(0, 2, lambda i: unpack(own, i, 4 + i))
    rows_loop(0, 2, lambda i: unpack(got_a, i, pick(6, 2) + i))
    rows_loop(0, 3, lambda i: unpack(got_b, i, pick(1, 6) + i))
    rows_loop(0, 1, lambda i: unpack(got_a2, pick(0, 2) + i, pick(8, 1) + i))

    quarter, eighth = OWN // 4, OWN // 8
    for ref in (c2, tmp2):
        edges(ref, 2, O2 - 12, O2 + quarter + 12)
    make_source(c2, q2, s2, table, 2, O2 - 11, O2 + quarter + 11)
    second_source = lambda field, row: s2[field, row]
    sweep(second_source, tmp2, v2, table, 2, O2 - 11, O2 + quarter + 11)

    descend(second_source, v2, table, 2, c3, q3, tmp3, O3 - 5, O3 + eighth + 5)
    make_source(c3, q3, s3, table, 3, O3 - 4, O3 + eighth + 4)
    third_source = lambda field, row: s3[field, row]
    sweep(third_source, tmp3, v3, table, 3, O3 - 4, O3 + eighth + 4)
    sweep(third_source, v3, tmp3, table, 3, O3 - 3, O3 + eighth + 3)
    sweep(third_source, tmp3, v3, table, 3, O3 - 2, O3 + eighth + 2, False)
    correct(v2, v2, v3, c3, 2, 0, O2 - 4, O2 + quarter + 4)
    sweep(second_source, v2, tmp2, table, 2, O2 - 3, O2 + quarter + 3)
    sweep(second_source, tmp2, v2, table, 2, O2 - 2, O2 + quarter + 2, False)

    half = OWN // 2
    first_source = lambda field, row: s1[field, row]
    correct(work1, v1, v2, c2, 1, O2 - O1 // 2, O1 - 3, O1 + half + 3)
    sweep(first_source, work1, tmp1, table, 1, O1 - 2, O1 + half + 2)
    sweep(first_source, tmp1, work1, table, 1, O1 - 1, O1 + half + 1, False)

    fine_source = lambda field, row: f0[field, row]
    correct(work0, v0, work1, c1, 0, 0, O0 - 2, O0 + OWN + 2)
    sweep(fine_source, work0, tmp0, table, 0, O0 - 1, O0 + OWN + 1)
    sweep(fine_source, tmp0, work0, table, 0, O0, O0 + OWN, False)

    if last:
        held = FIELDS * OWN
        for field in range(FIELDS):
            for sub in range(SUB):
                value = work0[field, pl.ds(at(O0, 0) + sub, OWN, stride=stride_of(0)), :]
                for p, part in enumerate(three_parts(value)):
                    start = p * held + field * OWN
                    parts[start : start + OWN, sub * LANES : (sub + 1) * LANES] = part

        def columns_out(index):
            values = dot(parts[...], turn(2 * index, False))
            values = (values[:held] + values[held : 2 * held]) + values[2 * held :]
            cells = pl.ds(pl.multiple_of(index * 2 * LANES, 2 * LANES), 2 * LANES)
            for field in range(FIELDS):
                out[field, :, cells] = values[field * OWN : (field + 1) * OWN]

        rows_loop(0, SUB // 2, columns_out)
        return

    def leave(row):
        start = pl.multiple_of(row * SUB, SUB)
        for field in range(FIELDS):
            out[field, pl.ds(start, SUB), :] = tile(work0, field, O0 + row, 0)

    rows_loop(0, OWN, leave)
    from_a, from_b = pick(OWN - FINE_HALO, 0), pick(0, OWN - FINE_HALO)

    def edge(row):
        start = pl.multiple_of(row * SUB, SUB)
        for field in range(FIELDS):
            send_a[field, pl.ds(start, SUB), :] = tile(work0, field, O0 + from_a + row, 0)
            send_b[field, pl.ds(start, SUB), :] = tile(work0, field, O0 + from_b + row, 0)

    rows_loop(0, FINE_HALO, edge)


def relay_kernel(where_ref, own, beside, row):
    odd = where_ref[0] % 2
    row[odd] = own[0]
    row[odd + 1] = own[1]
    row[2 - 2 * odd] = beside[odd]


VMEM = pl.BlockSpec(memory_space=pltpu.VMEM)
SMEM = pl.BlockSpec(memory_space=pltpu.SMEM)
HBM = pl.BlockSpec(memory_space=pltpu.HBM)


def f32(*shape):
    return jax.ShapeDtypeStruct(shape, jnp.float32)


def scratch(*shape):
    return pltpu.VMEM(shape, jnp.float32)


def padded(rows, level):
    return (FIELDS, padded_rows(rows, level), LANES)


def plain(rows):
    return (FIELDS, rows, SUB, LANES)


def call(kernel, name, grant, outs, operands, scratches=(), raw=()):
    return pl.pallas_call(
        kernel,
        out_shape=outs,
        in_specs=[SMEM] + [HBM if i in raw else VMEM for i in range(1, len(operands))],
        out_specs=[VMEM] * len(outs),
        scratch_shapes=list(scratches),
        name=name,
        compiler_params=pltpu.CompilerParams(vmem_limit_bytes=grant * 1024 * 1024),
    )(*operands)


def in_hbm(array):
    return pltpu.with_memory_space_constraint(array, pltpu.HBM)


def per_device(initial_state, forcing, coefficients, region_ids):
    size = lax.axis_size("axial")
    device = lax.axis_index("axial")
    assert initial_state.shape == (FIELDS, OWN, SUB * LANES)
    assert region_ids.shape == (OWN, SUB)
    where_ref = jnp.stack([device, jnp.int32(size)]).astype(jnp.int32)
    odd = device % 2
    pair_a = [(i, i ^ 1) for i in range(size)]
    pair_b = [(i, i + 1 if i % 2 else i - 1) for i in range(1, size - 1)]
    swap_a = lambda x: lax.ppermute(x, "axial", pair_a)
    swap_b = lambda x: lax.ppermute(x, "axial", pair_b)

    share = coefficients.shape[1]
    regions = share * size
    per_tile = LANES // OWN
    (gathered,) = call(
        functools.partial(prep_kernel, share),
        "prep",
        4,
        [f32(regions + SUB * -(-size // per_tile), LANES)],
        [where_ref, in_hbm(coefficients.T), in_hbm(region_ids.T)],
        [
            scratch(share, ENTRIES),
            pltpu.VMEM((SUB, OWN), jnp.int32),
            pltpu.SemaphoreType.DMA((2,)),
        ],
        (1, 2),
    )

    def doubled(held, step):
        return held + lax.ppermute(held, "axial", [(i, i ^ step) for i in range(size)])

    temps = [
        pltpu.VMEM((3 * FIELDS * OWN, SUB * LANES), jnp.bfloat16),
        scratch(FIELDS, OWN, SUB * LANES),
        pltpu.SemaphoreType.DMA,
    ]
    rows = f32(FIELDS, OWN * SUB, LANES)
    (state,) = call(
        split_state_kernel, "split_state", 8, [rows], [where_ref, in_hbm(initial_state)], temps, (1,)
    )
    force, send_a, send_b = call(
        split_forcing_kernel, "split_forcing", 10,
        [rows] + [f32(2 * FIELDS, FINE_HALO * SUB, LANES)] * 2,
        [where_ref, in_hbm(forcing), state], temps, (1,),
    )
    step = 1
    while step < size:
        gathered = doubled(gathered, step)
        step *= 2
        if step == 4:
            gathered, state = lax.optimization_barrier((gathered, state))
        elif step == 8:
            gathered, force = lax.optimization_barrier((gathered, force))
    gathered, send_a, send_b = lax.optimization_barrier((gathered, send_a, send_b))
    got_b, got_a = swap_b(send_b), swap_a(send_a)
    (table,) = call(
        functools.partial(tables_kernel, regions),
        "tables", 12,
        [f32(2 * ENTRIES, TABLE_ROWS, LANES)],
        [where_ref, gathered],
        [scratch(2, 32 * SUB, LANES), scratch(LANES, 2 * LANES)],
    )

    f0 = None
    for cycle in range(CYCLES):
        fresh = cycle == 0
        inner = call(
            functools.partial(interior_kernel, fresh), "interior", 4,
            [f32(*padded(T0, 0))] * 2 + [f32(*padded(T1, 1)), f32(*plain(T1)), f32(*padded(T1, 1))],
            [where_ref, state, force if fresh else f0, table],
        )
        outs = [f32(*padded(T0, 0)), f32(*padded(T1, 1)), f32(*plain(T1)), f32(*padded(T1, 1)),
                f32(2, 2 * FIELDS, SUB, LANES)]
        temps = [scratch(*padded(T0, 0)), scratch(*padded(T1, 1)), scratch(*plain(T1))]
        if fresh:
            v0, v1, s1, c1, own, f0 = call(
                functools.partial(down_kernel, True), "down_fresh", 14, outs + [f32(*plain(T0))],
                [where_ref, *inner, force, got_a, got_b, table], temps,
            )
        else:
            v0, v1, s1, c1, own = call(
                functools.partial(down_kernel, False), "down", 14, outs,
                [where_ref, *inner, got_a, got_b, f0, table], temps,
            )
        beside = swap_a(own)
        (row,) = call(
            relay_kernel, "relay", 2, [f32(3, 2 * FIELDS, SUB, LANES)], [where_ref, own, beside]
        )
        far = swap_b(row)
        beyond = swap_a(far)
        operands = [where_ref, own, beside, far, beyond, v0, f0, v1, s1, c1, table]
        temps = [scratch(*padded(T0, 0))] * 2 + [scratch(*padded(T1, 1))] * 2
        temps += [scratch(*padded(T2, 2)), scratch(*plain(T2)), scratch(*plain(T2)), scratch(*padded(T2, 2)), scratch(*padded(T2, 2))]
        temps += [scratch(*padded(T3, 3)), scratch(*plain(T3)), scratch(*plain(T3)), scratch(*padded(T3, 3)), scratch(*padded(T3, 3))]
        if cycle == CYCLES - 1:
            return call(
                functools.partial(up_kernel, True), "up_last", 26,
                [f32(FIELDS, OWN, SUB * LANES)], operands,
                [pltpu.VMEM((3 * FIELDS * OWN, SUB * LANES), jnp.bfloat16)] + temps,
            )[0]
        state, send_a, send_b = call(
            functools.partial(up_kernel, False), "up", 26,
            [f32(FIELDS, OWN * SUB, LANES)] + [f32(FIELDS, FINE_HALO * SUB, LANES)] * 2,
            operands, temps,
        )
        got_b, got_a = swap_b(send_b), swap_a(send_a)


def solution(mesh):
    placed = (
        P("sample", "axial", None),
        P("sample", "axial", None),
        P("sample", "axial"),
        P("axial", None),
    )
    return jax.shard_map(
        per_device,
        mesh=mesh,
        in_specs=placed,
        out_specs=P("sample", "axial", None),
        check_vma=False,
    )
```

```python
import functools

import jax
import jax.numpy as jnp
from jax import lax
from jax.experimental import pallas as pl
from jax.experimental.pallas import tpu as pltpu
from jax.sharding import PartitionSpec as P

DIFFUSION = 1.0
RELAXATION = 0.8
SOURCE_GAIN = 0.05
CYCLES = 2

FIELDS = 5
ENTRIES = FIELDS * FIELDS
SUB, LANES = 8, 128

OWN = 32
FINE_HALO = 11
T0, O0 = 64, 16
T1, O1 = 32, 8
T2, O2 = 40, 16
T3, O3 = 20, 8
COARSEST = 3
EDGE_BATCH = 10
GROUP = 4
SPREAD = 16


def stride_of(level):
    return SUB + (0 if level == COARSEST else 2 * 2**level) + (level == 2)


def padded_rows(rows, level):
    return stride_of(level) * (rows + SUB)


def at(row, level):
    return stride_of(level) * row + (0 if level == COARSEST else 2**level)


def lane_iota():
    return lax.broadcasted_iota(jnp.int32, (SUB, LANES), 1)


def sub_iota():
    return lax.broadcasted_iota(jnp.int32, (SUB, LANES), 0)


def tile(ref, field, row, level):
    return ref[field, pl.ds(at(row, level), SUB), :]


def put(ref, field, row, level, value):
    ref[field, pl.ds(at(row, level), SUB), :] = value


def edges(ref, level, first, last):
    if level == COARSEST:
        return
    width, stride, lane = 2**level, stride_of(level), lane_iota()
    places = [(row, field) for row in range(first, last, SUB) for field in range(FIELDS)]
    for part in range(0, len(places), EDGE_BATCH):
        written = []
        for row, field in places[part : part + EDGE_BATCH]:
            rows = lambda sub, row=row, field=field: (
                field, pl.ds(at(row, level) + sub, SUB, stride=stride), slice(None)
            )
            before = jnp.where(lane == 0, 0.0, pltpu.roll(ref[rows(SUB - 1)], 1, 1))
            after = jnp.where(lane == LANES - 1, 0.0, pltpu.roll(ref[rows(0)], LANES - 1, 1))
            written.append((rows, before, after))
        for rows, before, after in written:
            for i in range(width):
                ref[rows(i - width)] = before
                ref[rows(SUB + i)] = after


def rows_loop(first, last, body):
    def step(row, carry):
        body(row)
        return carry

    lax.fori_loop(first, last, step, 0)


def batches(first, last, batch, compute, store):
    def body(index):
        rows = [first + index * batch + i for i in range(batch)]
        results = [compute(row) for row in rows]
        for row, result in zip(rows, results):
            store(row, result)

    rows_loop(0, -(-(last - first) // batch), body)


def neighbours(ref, row, level):
    start, width, stride = at(row, level), 2**level, stride_of(level)
    lane = lane_iota()
    sums, centres = [], []
    for field in range(FIELDS):
        load = lambda first, field=field: ref[field, pl.ds(first, SUB), :]
        centre = load(start)
        if level == COARSEST:
            radial = jnp.where(lane == 0, 0.0, pltpu.roll(centre, 1, 1)) + jnp.where(
                lane == LANES - 1, 0.0, pltpu.roll(centre, LANES - 1, 1)
            )
        else:
            radial = load(start - width) + load(start + width)
        sums.append(radial + (load(start - stride) + load(start + stride)))
        centres.append(centre)
    return sums, centres


def block_times(table, level, row, first, vectors):
    row = TABLE_AT[level] + row
    out = []
    for i in range(FIELDS):
        total = None
        for j in range(FIELDS):
            entry = first + FIELDS * i + j
            term = jnp.broadcast_to(table[entry, pl.ds(row, 1), :], (SUB, LANES)) * vectors[j]
            total = term if total is None else total + term
        out.append(total)
    return out


MATRIX_AT = ENTRIES
TABLE_AT = (0, T0, T0 + T1, T0 + T1 + T2)
TABLE_ROWS = 160
NEAR = 5


def gain_of(level):
    return SOURCE_GAIN * 4.0**level / DIFFUSION


def sweep(source_of, old, new, table, level, first, last, more=True, batch=None):
    gain = gain_of(level)

    def compute(row):
        sums, centres = neighbours(old, row, level)
        rest = [
            (source_of(field, row) + sums[field]) - gain * jnp.tanh(centres[field])
            for field in range(FIELDS)
        ]
        moved = block_times(table, level, row, 0, rest)
        return [(1.0 - RELAXATION) * centres[f] + moved[f] for f in range(FIELDS)]

    def store(row, values):
        for field in range(FIELDS):
            put(new, field, row, level, values[field])

    batches(first, last, batch or SWEEP_BATCH, compute, store)
    if more:
        edges(new, level, first, last)


def residual(source_of, values, table, level, row):
    gain = gain_of(level)
    sums, centres = neighbours(values, row, level)
    applied = block_times(table, level, row, MATRIX_AT, centres)
    left = [
        ((source_of(field, row) + sums[field]) - gain * jnp.tanh(centres[field])) - applied[field]
        for field in range(FIELDS)
    ]
    return left, centres


def pair_sum(value, level):
    width = 2**level
    other = pltpu.roll(value, SUB - width, 0)
    if 2 * width != SUB:
        other = jnp.where((sub_iota() & width) == 0, other, pltpu.roll(value, width, 0))
    return value + other


def coarsen(source_of, values, table, level, row):
    upper_r, upper_v = residual(source_of, values, table, level, 2 * row)
    lower_r, lower_v = residual(source_of, values, table, level, 2 * row + 1)
    coarse = [0.25 * pair_sum(upper_v[f] + lower_v[f], level) for f in range(FIELDS)]
    rest = [pair_sum(upper_r[f] + lower_r[f], level) for f in range(FIELDS)]
    return coarse, rest


def first_sweep(coarse, rest, table, level, row):
    moved = block_times(table, level, row, 0, rest)
    return [coarse[f] + moved[f] for f in range(FIELDS)]


def descend(source_of, values, table, level, c, q, first_values, first, last):
    def compute(row):
        coarse, rest = coarsen(source_of, values, table, level, row)
        return coarse, rest, first_sweep(coarse, rest, table, level + 1, row)

    def store(row, results):
        for field in range(FIELDS):
            put(c, field, row, level + 1, results[0][field])
            q[field, row] = results[1][field]
            put(first_values, field, row, level + 1, results[2][field])

    batches(first, last, COARSEN_BATCH, compute, store)
    edges(c, level + 1, first, last)
    edges(first_values, level + 1, first, last)


def make_source(coarse, rest, source, table, level, first, last):
    gain = gain_of(level)

    def compute(row):
        sums, centres = neighbours(coarse, row, level)
        applied = block_times(table, level, row, MATRIX_AT, centres)
        return [
            (applied[f] - sums[f]) + (gain * jnp.tanh(centres[f]) + rest[f, row])
            for f in range(FIELDS)
        ]

    def store(row, values):
        for field in range(FIELDS):
            source[field, row] = values[field]

    batches(first, last, SWEEP_BATCH, compute, store)


def correct(new, fine, after, before, level, offset, first, last):
    def body(index):
        coarse_row = first // 2 + index + offset
        row = first // 2 * 2 + 2 * index
        for field in range(FIELDS):
            change = tile(after, field, coarse_row, level + 1) - tile(before, field, coarse_row, level + 1)
            put(new, field, row, level, tile(fine, field, row, level) + change)
            put(new, field, row + 1, level, tile(fine, field, row + 1, level) + change)

    rows_loop(0, (last + 1) // 2 - first // 2, body)
    edges(new, level, first, last)


SWEEP_BATCH = 4
INNER = 2
COARSEN_BATCH = 2


def three_parts(value):
    high = value.astype(jnp.bfloat16)
    rest = value - high.astype(jnp.float32)
    middle = rest.astype(jnp.bfloat16)
    low = (rest - middle.astype(jnp.float32)).astype(jnp.bfloat16)
    return high, middle, low


def dot(left, right):
    return jnp.dot(left, right, preferred_element_type=jnp.float32)


def prep_kernel(share, where_ref, coefficients_ref, ids_ref, out, own_coefficients, own_ids, sems):
    device, devices = where_ref[0], where_ref[1]
    copies = [
        pltpu.make_async_copy(coefficients_ref, own_coefficients, sems.at[0]),
        pltpu.make_async_copy(ids_ref, own_ids, sems.at[1]),
    ]
    for copy in copies:
        copy.start()
    out[...] = jnp.zeros_like(out)
    for copy in copies:
        copy.wait()
    for i in range(share):
        out[pl.ds(device * share + i, 1), 0:ENTRIES] = own_coefficients[i : i + 1, :]
    ids = own_ids[...].astype(jnp.float32)
    per_tile = LANES // OWN
    start = pl.multiple_of(devices * share + device // per_tile * SUB, SUB)
    for place in range(per_tile):

        @pl.when(device % per_tile == place)
        def _():
            out[pl.ds(start, SUB), place * OWN : (place + 1) * OWN] = ids


def tables_kernel(regions, where_ref, regions_ref, table, mats, parts):
    device, devices = where_ref[0], where_ref[1]
    wide = 2 * LANES
    lane = lane_iota()
    ids = [jnp.full((SUB, LANES), -1.0, jnp.float32)] * 2
    per_tile = LANES // OWN
    for i in range(NEAR):
        owner = jnp.clip(device + (i - NEAR // 2), 0, devices - 1)
        start = pl.multiple_of(regions + owner // per_tile * SUB, SUB)
        held = regions_ref[pl.ds(start, SUB), :]
        turned = pltpu.roll(held, ((i % per_tile) - owner % per_tile + per_tile) % per_tile * OWN, 1)
        place = i // per_tile
        ids[place] = jnp.where(lane // OWN == i % per_tile, turned, ids[place])
    ids = jnp.concatenate(ids, axis=1).astype(jnp.int32)

    coefficients = jnp.transpose(regions_ref[0:regions, :])[0:32]
    coefficients = jnp.concatenate(three_parts(coefficients), axis=0)
    region = lax.broadcasted_iota(jnp.int32, (regions, wide), 0)
    for block in range(SUB):
        chosen = region == jnp.broadcast_to(ids[block : block + 1], (regions, wide))
        found = dot(coefficients, chosen.astype(jnp.float32).astype(jnp.bfloat16))
        found = (found[0:32] + found[32:64]) + found[64:96]
        for half in range(2):
            mats[half, pl.ds(block, 32, stride=SUB), :] = found[:, half * LANES : (half + 1) * LANES]

    fine = lax.broadcasted_iota(jnp.int32, (wide, wide), 0)
    out = lax.broadcasted_iota(jnp.int32, (wide, wide), 1)
    average = jnp.zeros((wide, wide), jnp.float32)
    own_at = NEAR // 2 * OWN
    for level, (first_own, rows) in enumerate(((O0, T0), (O1, T1), (O2, T2), (O3, T3))):
        span = 2**level
        row = out - TABLE_AT[level]
        same = (row >= 0) & (row < rows) & (fine // span == row + (own_at // span - first_own))
        average = jnp.where(same, 1.0 / span, average)
    average = average.astype(jnp.bfloat16)
    used = SUB * ENTRIES
    high, middle, low = three_parts(jnp.concatenate([mats[0, 0:used], mats[1, 0:used]], axis=1))
    levels = (dot(high, average) + dot(middle, average)) + dot(low, average)

    row = lax.broadcasted_iota(jnp.int32, (SUB, wide), 1)
    weight = jnp.zeros((SUB, wide), jnp.float32) + DIFFUSION
    whole = jnp.zeros((SUB, wide), jnp.int32)
    limit = jnp.zeros((SUB, wide), jnp.int32)
    for level, first_own in enumerate((O0, O1, O2, O3)):
        here = row >= TABLE_AT[level]
        weight = jnp.where(here, DIFFUSION / 4.0**level, weight)
        whole = jnp.where(here, row - TABLE_AT[level] - first_own + device * (OWN >> level), whole)
        limit = jnp.where(here, devices * (OWN >> level), limit)
    inside = (whole >= 0) & (whole < limit)
    scale = jnp.where(inside, RELAXATION * weight, 0.0)
    unscale = 1.0 / weight

    n = FIELDS
    block = [[levels[SUB * (n * i + j) : SUB * (n * i + j + 1)] for j in range(n)] for i in range(n)]
    for i in range(n):
        block[i][i] = block[i][i] + 4.0 * weight
    entries = [block[i][j] * unscale for i in range(n) for j in range(n)]
    right = [[None] * n for _ in range(n)]
    for i in range(n):
        right[i][i] = jnp.ones((SUB, wide), jnp.float32)
    for c in range(n):
        lead = 1.0 / block[c][c]
        for j in range(c + 1, n):
            block[c][j] = block[c][j] * lead
        for j in range(n):
            if right[c][j] is not None:
                right[c][j] = right[c][j] * lead
        for i in range(n):
            if i == c:
                continue
            factor = block[i][c]
            for j in range(c + 1, n):
                block[i][j] = block[i][j] - factor * block[c][j]
            for j in range(n):
                if right[c][j] is not None:
                    term = factor * right[c][j]
                    right[i][j] = -term if right[i][j] is None else right[i][j] - term
    entries = [right[i][j] * scale for i in range(n) for j in range(n)] + entries

    group = FIELDS
    into = lax.broadcasted_iota(jnp.int32, (LANES, group * LANES), 0)
    out = lax.broadcasted_iota(jnp.int32, (LANES, group * LANES), 1)
    same = (into // (3 * SUB) == out // LANES) & (into % SUB == out % LANES // SPREAD)
    widen = same.astype(jnp.float32).astype(jnp.bfloat16)
    parts[...] = jnp.zeros_like(parts)
    for first in range(0, len(entries), group):
        for i in range(group):
            for p, part in enumerate(three_parts(entries[first + i])):
                start = (3 * i + p) * SUB
                parts[start : start + SUB, :] = part.astype(jnp.float32)
        turned = jnp.transpose(parts[...])[0:TABLE_ROWS].astype(jnp.bfloat16)
        wide_rows = dot(turned, widen)
        for i in range(group):
            table[first + i] = wide_rows[:, i * LANES : (i + 1) * LANES]


def turn(first_sub, inward):
    into = lax.broadcasted_iota(jnp.int32, (SUB * LANES, 2 * LANES), 0)
    out = lax.broadcasted_iota(jnp.int32, (1, 2 * LANES), 1)
    if inward:
        wanted = (out % LANES) * SUB + first_sub + out // LANES
    else:
        cell = out + first_sub * LANES
        wanted = (cell % SUB) * LANES + cell // SUB
    return (into == wanted).astype(jnp.float32).astype(jnp.bfloat16)


def split_kernel(where_ref, state_ref, forcing_ref, state_rows, forcing_rows, send_a, send_b, parts, held_in, sems):
    copies = [
        pltpu.make_async_copy(source, held_in.at[i], sems.at[i])
        for i, source in enumerate((state_ref, forcing_ref))
    ]
    for copy in copies:
        copy.start()
    odd = where_ref[0] % 2
    held = 2 * FIELDS * OWN
    for which, copy in enumerate(copies):
        copy.wait()
        for field in range(FIELDS):
            for p, part in enumerate(three_parts(held_in[which, field])):
                start = p * held + (which * FIELDS + field) * OWN
                parts[start : start + OWN, :] = part

    def two_subs(index):
        values = dot(parts[...], turn(2 * index, True))
        values = (values[:held] + values[held : 2 * held]) + values[2 * held :]
        for which, target in enumerate((state_rows, forcing_rows)):
            for field in range(FIELDS):
                start = (which * FIELDS + field) * OWN
                for half in range(2):
                    target[field, pl.ds(2 * index + half, OWN, stride=SUB), :] = values[
                        start : start + OWN, half * LANES : (half + 1) * LANES
                    ]

    rows_loop(0, SUB // 2, two_subs)
    low, high = 0, (OWN - FINE_HALO) * SUB
    size = FINE_HALO * SUB
    for which, rows in enumerate((state_rows, forcing_rows)):
        for field in range(FIELDS):
            first = rows[field, low : low + size, :]
            last = rows[field, high : high + size, :]
            send_a[which * FIELDS + field] = jnp.where(odd == 1, first, last)
            send_b[which * FIELDS + field] = jnp.where(odd == 1, last, first)


def place_halo(where_ref, buffer, own_rows, got_a, got_b, first, padded):
    odd = where_ref[0] % 2
    row_a = jnp.where(odd == 1, O0 - FINE_HALO, O0 + OWN)
    row_b = jnp.where(odd == 1, O0 + OWN, O0 - FINE_HALO)

    def put_row(field, row, value):
        if padded:
            put(buffer, field, row, 0, value)
        else:
            buffer[field, row] = value

    def own(row):
        start = pl.multiple_of(row * SUB, SUB)
        for field in range(FIELDS):
            put_row(field, O0 + row, own_rows[field, pl.ds(start, SUB), :])

    def halo(row):
        start = pl.multiple_of(row * SUB, SUB)
        for field in range(FIELDS):
            put_row(field, row_a + row, got_a[first + field, pl.ds(start, SUB), :])
            put_row(field, row_b + row, got_b[first + field, pl.ds(start, SUB), :])

    if own_rows is not None:
        rows_loop(0, OWN, own)
    rows_loop(0, FINE_HALO, halo)


def interior_kernel(where_ref, state, f0, table, v0, tmp0, c1, q1, tmp1):
    def own(row):
        start = pl.multiple_of(row * SUB, SUB)
        for field in range(FIELDS):
            put(v0, field, O0 + row, 0, state[field, pl.ds(start, SUB), :])

    rows_loop(0, OWN, own)
    edges(v0, 0, O0, O0 + OWN)
    source = lambda field, row: f0[field, row]
    sweep(source, v0, tmp0, table, 0, O0 + 1, O0 + OWN - 1, batch=5)
    sweep(source, tmp0, v0, table, 0, O0 + 2, O0 + OWN - 2, batch=4)
    descend(source, v0, table, 0, c1, q1, tmp1, O1 + INNER, O1 + OWN // 2 - INNER)


def down_kernel(fresh, *refs):
    half = OWN // 2
    low, high = O0 - FINE_HALO, O0 + OWN + FINE_HALO
    if fresh:
        where_ref, state, force, got_a, got_b, table, v0, v1, s1, c1, send, f0, tmp0, tmp1, q1 = refs
        place_halo(where_ref, v0, state, got_a, got_b, 0, True)
        edges(v0, 0, low, high)
        place_halo(where_ref, f0, force, got_a, got_b, FIELDS, False)
    else:
        (where_ref, v0_in, tmp0_in, c1_in, q1_in, tmp1_in, got_a, got_b, f0, table,
         v0, v1, s1, c1, send, tmp0, tmp1, q1) = refs

        def take(target, source, level, first, last):
            rows = slice(at(first, level) - 2**level, at(last, level) - 2**level)
            target[:, rows, :] = source[:, rows, :]

        take(v0, v0_in, 0, O0, O0 + OWN)
        take(tmp0, tmp0_in, 0, O0 + 1, O0 + 3)
        take(tmp0, tmp0_in, 0, O0 + OWN - 3, O0 + OWN - 1)
        inner = slice(O1 + INNER, O1 + half - INNER)
        take(c1, c1_in, 1, inner.start, inner.stop)
        take(tmp1, tmp1_in, 1, inner.start, inner.stop)
        q1[:, inner] = q1_in[:, inner]
        place_halo(where_ref, v0, None, got_a, got_b, 0, True)
        edges(v0, 0, low, O0)
        edges(v0, 0, O0 + OWN, high)
    fine_source = lambda field, row: f0[field, row]
    if fresh:
        sweep(fine_source, v0, tmp0, table, 0, low + 1, high - 1)
        sweep(fine_source, tmp0, v0, table, 0, low + 2, high - 2)
        descend(fine_source, v0, table, 0, c1, q1, tmp1, O1 - 4, O1 + half + 4)
    else:
        for swept, (old, new) in enumerate(((v0, tmp0), (tmp0, v0))):
            for first in (low + swept, O0 + OWN - 1 - swept):
                sweep(fine_source, old, new, table, 0, first, first + FINE_HALO + 1)
        for first in (O1 - 4, O1 + half - INNER):
            descend(fine_source, v0, table, 0, c1, q1, tmp1, first, first + 4 + INNER)
    make_source(c1, q1, s1, table, 1, O1 - 3, O1 + half + 3)
    first_source = lambda field, row: s1[field, row]
    sweep(first_source, tmp1, v1, table, 1, O1 - 3, O1 + half + 3)

    sub = sub_iota()

    def to_second(index):
        coarse, rest = coarsen(first_source, v1, table, 1, index + O1 // 2)
        return coarse + rest

    def pack(index, values):
        group, place = index // GROUP, index % GROUP
        mine = (sub & (GROUP - 1)) == place
        for which in range(2 * FIELDS):
            send[group, which] = jnp.where(mine, values[which], send[group, which])

    send[...] = jnp.zeros_like(send)
    batches(0, OWN // 4, COARSEN_BATCH, to_second, pack)


def spread(source, index, which, place):
    take = lambda sub: jnp.broadcast_to(source[index, which, sub : sub + 1, :], (SUB, LANES))
    return jnp.where(sub_iota() < GROUP, take(place), take(GROUP + place))


def up_kernel(last, *refs):
    if last:
        (where_ref, own, got_a, got_b, got_a2, v0, f0, v1, s1, c1, table, out,
         parts, tmp0, work0, tmp1, work1, c2, q2, s2, v2, tmp2, c3, q3, s3, v3, tmp3) = refs
    else:
        (where_ref, own, got_a, got_b, got_a2, v0, f0, v1, s1, c1, table, out,
         send_a, send_b, tmp0, work0, tmp1, work1, c2, q2, s2, v2, tmp2, c3, q3, s3, v3, tmp3) = refs
    odd = where_ref[0] % 2

    def unpack(source, index, group):
        for place in range(GROUP):
            row = group * GROUP + place
            coarse = [spread(source, index, f, place) for f in range(FIELDS)]
            rest = [spread(source, index, FIELDS + f, place) for f in range(FIELDS)]
            start = first_sweep(coarse, rest, table, 2, row)
            for field in range(FIELDS):
                put(c2, field, row, 2, coarse[field])
                q2[field, row] = rest[field]
                put(tmp2, field, row, 2, start[field])

    pick = lambda a, b: jnp.where(odd == 1, b, a)
    rows_loop(0, 2, lambda i: unpack(own, i, 4 + i))
    rows_loop(0, 2, lambda i: unpack(got_a, i, pick(6, 2) + i))
    rows_loop(0, 3, lambda i: unpack(got_b, i, pick(1, 6) + i))
    rows_loop(0, 1, lambda i: unpack(got_a2, pick(0, 2) + i, pick(8, 1) + i))

    quarter, eighth = OWN // 4, OWN // 8
    for ref in (c2, tmp2):
        edges(ref, 2, O2 - 12, O2 + quarter + 12)
    make_source(c2, q2, s2, table, 2, O2 - 11, O2 + quarter + 11)
    second_source = lambda field, row: s2[field, row]
    sweep(second_source, tmp2, v2, table, 2, O2 - 11, O2 + quarter + 11)

    descend(second_source, v2, table, 2, c3, q3, tmp3, O3 - 5, O3 + eighth + 5)
    make_source(c3, q3, s3, table, 3, O3 - 4, O3 + eighth + 4)
    third_source = lambda field, row: s3[field, row]
    sweep(third_source, tmp3, v3, table, 3, O3 - 4, O3 + eighth + 4)
    sweep(third_source, v3, tmp3, table, 3, O3 - 3, O3 + eighth + 3)
    sweep(third_source, tmp3, v3, table, 3, O3 - 2, O3 + eighth + 2, False)
    correct(v2, v2, v3, c3, 2, 0, O2 - 4, O2 + quarter + 4)
    sweep(second_source, v2, tmp2, table, 2, O2 - 3, O2 + quarter + 3)
    sweep(second_source, tmp2, v2, table, 2, O2 - 2, O2 + quarter + 2, False)

    half = OWN // 2
    first_source = lambda field, row: s1[field, row]
    correct(work1, v1, v2, c2, 1, O2 - O1 // 2, O1 - 3, O1 + half + 3)
    sweep(first_source, work1, tmp1, table, 1, O1 - 2, O1 + half + 2)
    sweep(first_source, tmp1, work1, table, 1, O1 - 1, O1 + half + 1, False)

    fine_source = lambda field, row: f0[field, row]
    correct(work0, v0, work1, c1, 0, 0, O0 - 2, O0 + OWN + 2)
    sweep(fine_source, work0, tmp0, table, 0, O0 - 1, O0 + OWN + 1)
    sweep(fine_source, tmp0, work0, table, 0, O0, O0 + OWN, False)

    if last:
        held = FIELDS * OWN
        for field in range(FIELDS):
            for sub in range(SUB):
                value = work0[field, pl.ds(at(O0, 0) + sub, OWN, stride=stride_of(0)), :]
                for p, part in enumerate(three_parts(value)):
                    start = p * held + field * OWN
                    parts[start : start + OWN, sub * LANES : (sub + 1) * LANES] = part

        def columns_out(index):
            values = dot(parts[...], turn(2 * index, False))
            values = (values[:held] + values[held : 2 * held]) + values[2 * held :]
            cells = pl.ds(pl.multiple_of(index * 2 * LANES, 2 * LANES), 2 * LANES)
            for field in range(FIELDS):
                out[field, :, cells] = values[field * OWN : (field + 1) * OWN]

        rows_loop(0, SUB // 2, columns_out)
        return

    def leave(row):
        start = pl.multiple_of(row * SUB, SUB)
        for field in range(FIELDS):
            out[field, pl.ds(start, SUB), :] = tile(work0, field, O0 + row, 0)

    rows_loop(0, OWN, leave)
    from_a, from_b = pick(OWN - FINE_HALO, 0), pick(0, OWN - FINE_HALO)

    def edge(row):
        start = pl.multiple_of(row * SUB, SUB)
        for field in range(FIELDS):
            send_a[field, pl.ds(start, SUB), :] = tile(work0, field, O0 + from_a + row, 0)
            send_b[field, pl.ds(start, SUB), :] = tile(work0, field, O0 + from_b + row, 0)

    rows_loop(0, FINE_HALO, edge)


def relay_kernel(where_ref, own, beside, row):
    odd = where_ref[0] % 2
    row[odd] = own[0]
    row[odd + 1] = own[1]
    row[2 - 2 * odd] = beside[odd]


VMEM = pl.BlockSpec(memory_space=pltpu.VMEM)
SMEM = pl.BlockSpec(memory_space=pltpu.SMEM)
HBM = pl.BlockSpec(memory_space=pltpu.HBM)


def f32(*shape):
    return jax.ShapeDtypeStruct(shape, jnp.float32)


def scratch(*shape):
    return pltpu.VMEM(shape, jnp.float32)


def padded(rows, level):
    return (FIELDS, padded_rows(rows, level), LANES)


def plain(rows):
    return (FIELDS, rows, SUB, LANES)


def call(kernel, name, grant, outs, operands, scratches=(), raw=()):
    return pl.pallas_call(
        kernel,
        out_shape=outs,
        in_specs=[SMEM] + [HBM if i in raw else VMEM for i in range(1, len(operands))],
        out_specs=[VMEM] * len(outs),
        scratch_shapes=list(scratches),
        name=name,
        compiler_params=pltpu.CompilerParams(vmem_limit_bytes=grant * 1024 * 1024),
    )(*operands)


def in_hbm(array):
    return pltpu.with_memory_space_constraint(array, pltpu.HBM)


def per_device(initial_state, forcing, coefficients, region_ids):
    size = lax.axis_size("axial")
    device = lax.axis_index("axial")
    assert initial_state.shape == (FIELDS, OWN, SUB * LANES)
    assert region_ids.shape == (OWN, SUB)
    where_ref = jnp.stack([device, jnp.int32(size)]).astype(jnp.int32)
    odd = device % 2
    pair_a = [(i, i ^ 1) for i in range(size)]
    pair_b = [(i, i + 1 if i % 2 else i - 1) for i in range(1, size - 1)]
    swap_a = lambda x: lax.ppermute(x, "axial", pair_a)
    swap_b = lambda x: lax.ppermute(x, "axial", pair_b)

    share = coefficients.shape[1]
    regions = share * size
    per_tile = LANES // OWN
    (gathered,) = call(
        functools.partial(prep_kernel, share),
        "prep",
        4,
        [f32(regions + SUB * -(-size // per_tile), LANES)],
        [where_ref, in_hbm(coefficients.T), in_hbm(region_ids.T)],
        [
            scratch(share, ENTRIES),
            pltpu.VMEM((SUB, OWN), jnp.int32),
            pltpu.SemaphoreType.DMA((2,)),
        ],
        (1, 2),
    )

    def doubled(held, step):
        return held + lax.ppermute(held, "axial", [(i, i ^ step) for i in range(size)])

    state, force, send_a, send_b = call(
        split_kernel,
        "split",
        12,
        [f32(FIELDS, OWN * SUB, LANES)] * 2 + [f32(2 * FIELDS, FINE_HALO * SUB, LANES)] * 2,
        [where_ref, in_hbm(initial_state), in_hbm(forcing)],
        [
            pltpu.VMEM((3 * 2 * FIELDS * OWN, SUB * LANES), jnp.bfloat16),
            scratch(2, FIELDS, OWN, SUB * LANES),
            pltpu.SemaphoreType.DMA((2,)),
        ],
        (1, 2),
    )
    step = 1
    while step < min(size, 4):
        gathered = doubled(gathered, step)
        step *= 2
    gathered, send_a, send_b = lax.optimization_barrier((gathered, send_a, send_b))
    got_b, got_a = swap_b(send_b), swap_a(send_a)
    while step < size:
        gathered = doubled(gathered, step)
        step *= 2
    (table,) = call(
        functools.partial(tables_kernel, regions),
        "tables", 12,
        [f32(2 * ENTRIES, TABLE_ROWS, LANES)],
        [where_ref, gathered],
        [scratch(2, 32 * SUB, LANES), scratch(LANES, 2 * LANES)],
    )

    f0 = None
    for cycle in range(CYCLES):
        outs = [f32(*padded(T0, 0)), f32(*padded(T1, 1)), f32(*plain(T1)), f32(*padded(T1, 1)),
                f32(2, 2 * FIELDS, SUB, LANES)]
        temps = [scratch(*padded(T0, 0)), scratch(*padded(T1, 1)), scratch(*plain(T1))]
        if cycle == 0:
            v0, v1, s1, c1, own, f0 = call(
                functools.partial(down_kernel, True), "down_fresh", 14, outs + [f32(*plain(T0))],
                [where_ref, state, force, got_a, got_b, table], temps,
            )
        else:
            inner = call(
                interior_kernel, "interior", 4,
                [f32(*padded(T0, 0))] * 2 + [f32(*padded(T1, 1)), f32(*plain(T1)), f32(*padded(T1, 1))],
                [where_ref, state, f0, table],
            )
            v0, v1, s1, c1, own = call(
                functools.partial(down_kernel, False), "down", 14, outs,
                [where_ref, *inner, got_a, got_b, f0, table], temps,
            )
        beside = swap_a(own)
        (row,) = call(
            relay_kernel, "relay", 2, [f32(3, 2 * FIELDS, SUB, LANES)], [where_ref, own, beside]
        )
        far = swap_b(row)
        beyond = swap_a(far)
        operands = [where_ref, own, beside, far, beyond, v0, f0, v1, s1, c1, table]
        temps = [scratch(*padded(T0, 0))] * 2 + [scratch(*padded(T1, 1))] * 2
        temps += [scratch(*padded(T2, 2)), scratch(*plain(T2)), scratch(*plain(T2)), scratch(*padded(T2, 2)), scratch(*padded(T2, 2))]
        temps += [scratch(*padded(T3, 3)), scratch(*plain(T3)), scratch(*plain(T3)), scratch(*padded(T3, 3)), scratch(*padded(T3, 3))]
        if cycle == CYCLES - 1:
            return call(
                functools.partial(up_kernel, True), "up_last", 26,
                [f32(FIELDS, OWN, SUB * LANES)], operands,
                [pltpu.VMEM((3 * FIELDS * OWN, SUB * LANES), jnp.bfloat16)] + temps,
            )[0]
        state, send_a, send_b = call(
            functools.partial(up_kernel, False), "up", 26,
            [f32(FIELDS, OWN * SUB, LANES)] + [f32(FIELDS, FINE_HALO * SUB, LANES)] * 2,
            operands, temps,
        )
        got_b, got_a = swap_b(send_b), swap_a(send_a)


def solution(mesh):
    placed = (
        P("sample", "axial", None),
        P("sample", "axial", None),
        P("sample", "axial"),
        P("axial", None),
    )
    return jax.shard_map(
        per_device,
        mesh=mesh,
        in_specs=placed,
        out_specs=P("sample", "axial", None),
        check_vma=False,
    )
```

```python
import functools

import jax
import jax.numpy as jnp
from jax import lax
from jax.experimental import pallas as pl
from jax.experimental.pallas import tpu as pltpu
from jax.sharding import PartitionSpec as P

DIFFUSION = 1.0
RELAXATION = 0.8
SOURCE_GAIN = 0.05
CYCLES = 2

FIELDS = 5
ENTRIES = FIELDS * FIELDS
SUB, LANES = 8, 128

OWN = 32
FINE_HALO = 11
T0, O0 = 64, 16
T1, O1 = 32, 8
T2, O2 = 40, 16
T3, O3 = 20, 8
COARSEST = 3
EDGE_BATCH = 10
GROUP = 4
SPREAD = 16


def stride_of(level):
    return SUB + (0 if level == COARSEST else 2 * 2**level) + (level == 2)


def padded_rows(rows, level):
    return stride_of(level) * (rows + SUB)


def at(row, level):
    return stride_of(level) * row + (0 if level == COARSEST else 2**level)


def lane_iota():
    return lax.broadcasted_iota(jnp.int32, (SUB, LANES), 1)


def sub_iota():
    return lax.broadcasted_iota(jnp.int32, (SUB, LANES), 0)


def tile(ref, field, row, level):
    return ref[field, pl.ds(at(row, level), SUB), :]


def put(ref, field, row, level, value):
    ref[field, pl.ds(at(row, level), SUB), :] = value


def edges(ref, level, first, last):
    if level == COARSEST:
        return
    width, stride, lane = 2**level, stride_of(level), lane_iota()
    places = [(row, field) for row in range(first, last, SUB) for field in range(FIELDS)]
    for part in range(0, len(places), EDGE_BATCH):
        written = []
        for row, field in places[part : part + EDGE_BATCH]:
            rows = lambda sub, row=row, field=field: (
                field, pl.ds(at(row, level) + sub, SUB, stride=stride), slice(None)
            )
            before = jnp.where(lane == 0, 0.0, pltpu.roll(ref[rows(SUB - 1)], 1, 1))
            after = jnp.where(lane == LANES - 1, 0.0, pltpu.roll(ref[rows(0)], LANES - 1, 1))
            written.append((rows, before, after))
        for rows, before, after in written:
            for i in range(width):
                ref[rows(i - width)] = before
                ref[rows(SUB + i)] = after


def rows_loop(first, last, body):
    def step(row, carry):
        body(row)
        return carry

    lax.fori_loop(first, last, step, 0)


def batches(first, last, batch, compute, store):
    def body(index):
        rows = [first + index * batch + i for i in range(batch)]
        results = [compute(row) for row in rows]
        for row, result in zip(rows, results):
            store(row, result)

    rows_loop(0, -(-(last - first) // batch), body)


def neighbours(ref, row, level):
    start, width, stride = at(row, level), 2**level, stride_of(level)
    lane = lane_iota()
    sums, centres = [], []
    for field in range(FIELDS):
        load = lambda first, field=field: ref[field, pl.ds(first, SUB), :]
        centre = load(start)
        if level == COARSEST:
            radial = jnp.where(lane == 0, 0.0, pltpu.roll(centre, 1, 1)) + jnp.where(
                lane == LANES - 1, 0.0, pltpu.roll(centre, LANES - 1, 1)
            )
        else:
            radial = load(start - width) + load(start + width)
        sums.append(radial + (load(start - stride) + load(start + stride)))
        centres.append(centre)
    return sums, centres


def block_times(table, level, row, first, vectors):
    row = TABLE_AT[level] + row
    out = []
    for i in range(FIELDS):
        total = None
        for j in range(FIELDS):
            entry = first + FIELDS * i + j
            term = jnp.broadcast_to(table[entry, pl.ds(row, 1), :], (SUB, LANES)) * vectors[j]
            total = term if total is None else total + term
        out.append(total)
    return out


MATRIX_AT = ENTRIES
TABLE_AT = (0, T0, T0 + T1, T0 + T1 + T2)
TABLE_ROWS = 160
NEAR = 5


def gain_of(level):
    return SOURCE_GAIN * 4.0**level / DIFFUSION


def sweep(source_of, old, new, table, level, first, last, more=True, batch=None):
    gain = gain_of(level)

    def compute(row):
        sums, centres = neighbours(old, row, level)
        rest = [
            (source_of(field, row) + sums[field]) - gain * jnp.tanh(centres[field])
            for field in range(FIELDS)
        ]
        moved = block_times(table, level, row, 0, rest)
        return [(1.0 - RELAXATION) * centres[f] + moved[f] for f in range(FIELDS)]

    def store(row, values):
        for field in range(FIELDS):
            put(new, field, row, level, values[field])

    batches(first, last, batch or SWEEP_BATCH, compute, store)
    if more:
        edges(new, level, first, last)


def residual(source_of, values, table, level, row):
    gain = gain_of(level)
    sums, centres = neighbours(values, row, level)
    applied = block_times(table, level, row, MATRIX_AT, centres)
    left = [
        ((source_of(field, row) + sums[field]) - gain * jnp.tanh(centres[field])) - applied[field]
        for field in range(FIELDS)
    ]
    return left, centres


def pair_sum(value, level):
    width = 2**level
    other = pltpu.roll(value, SUB - width, 0)
    if 2 * width != SUB:
        other = jnp.where((sub_iota() & width) == 0, other, pltpu.roll(value, width, 0))
    return value + other


def coarsen(source_of, values, table, level, row):
    upper_r, upper_v = residual(source_of, values, table, level, 2 * row)
    lower_r, lower_v = residual(source_of, values, table, level, 2 * row + 1)
    coarse = [0.25 * pair_sum(upper_v[f] + lower_v[f], level) for f in range(FIELDS)]
    rest = [pair_sum(upper_r[f] + lower_r[f], level) for f in range(FIELDS)]
    return coarse, rest


def first_sweep(coarse, rest, table, level, row):
    moved = block_times(table, level, row, 0, rest)
    return [coarse[f] + moved[f] for f in range(FIELDS)]


def descend(source_of, values, table, level, c, q, first_values, first, last):
    def compute(row):
        coarse, rest = coarsen(source_of, values, table, level, row)
        return coarse, rest, first_sweep(coarse, rest, table, level + 1, row)

    def store(row, results):
        for field in range(FIELDS):
            put(c, field, row, level + 1, results[0][field])
            q[field, row] = results[1][field]
            put(first_values, field, row, level + 1, results[2][field])

    batches(first, last, COARSEN_BATCH, compute, store)
    edges(c, level + 1, first, last)
    edges(first_values, level + 1, first, last)


def make_source(coarse, rest, source, table, level, first, last):
    gain = gain_of(level)

    def compute(row):
        sums, centres = neighbours(coarse, row, level)
        applied = block_times(table, level, row, MATRIX_AT, centres)
        return [
            (applied[f] - sums[f]) + (gain * jnp.tanh(centres[f]) + rest[f, row])
            for f in range(FIELDS)
        ]

    def store(row, values):
        for field in range(FIELDS):
            source[field, row] = values[field]

    batches(first, last, SWEEP_BATCH, compute, store)


def correct(new, fine, after, before, level, offset, first, last):
    def body(index):
        coarse_row = first // 2 + index + offset
        row = first // 2 * 2 + 2 * index
        for field in range(FIELDS):
            change = tile(after, field, coarse_row, level + 1) - tile(before, field, coarse_row, level + 1)
            put(new, field, row, level, tile(fine, field, row, level) + change)
            put(new, field, row + 1, level, tile(fine, field, row + 1, level) + change)

    rows_loop(0, (last + 1) // 2 - first // 2, body)
    edges(new, level, first, last)


SWEEP_BATCH = 4
INNER = 2
COARSEN_BATCH = 2


def three_parts(value):
    high = value.astype(jnp.bfloat16)
    rest = value - high.astype(jnp.float32)
    middle = rest.astype(jnp.bfloat16)
    low = (rest - middle.astype(jnp.float32)).astype(jnp.bfloat16)
    return high, middle, low


def dot(left, right):
    return jnp.dot(left, right, preferred_element_type=jnp.float32)


def prep_kernel(share, where_ref, coefficients_ref, ids_ref, out, own_coefficients, own_ids, sems):
    device, devices = where_ref[0], where_ref[1]
    copies = [
        pltpu.make_async_copy(coefficients_ref, own_coefficients, sems.at[0]),
        pltpu.make_async_copy(ids_ref, own_ids, sems.at[1]),
    ]
    for copy in copies:
        copy.start()
    out[...] = jnp.zeros_like(out)
    for copy in copies:
        copy.wait()
    for i in range(share):
        out[pl.ds(device * share + i, 1), 0:ENTRIES] = own_coefficients[i : i + 1, :]
    ids = own_ids[...].astype(jnp.float32)
    per_tile = LANES // OWN
    start = pl.multiple_of(devices * share + device // per_tile * SUB, SUB)
    for place in range(per_tile):

        @pl.when(device % per_tile == place)
        def _():
            out[pl.ds(start, SUB), place * OWN : (place + 1) * OWN] = ids


def tables_kernel(regions, where_ref, regions_ref, table, mats, parts):
    device, devices = where_ref[0], where_ref[1]
    wide = 2 * LANES
    lane = lane_iota()
    ids = [jnp.full((SUB, LANES), -1.0, jnp.float32)] * 2
    per_tile = LANES // OWN
    for i in range(NEAR):
        owner = jnp.clip(device + (i - NEAR // 2), 0, devices - 1)
        start = pl.multiple_of(regions + owner // per_tile * SUB, SUB)
        held = regions_ref[pl.ds(start, SUB), :]
        turned = pltpu.roll(held, ((i % per_tile) - owner % per_tile + per_tile) % per_tile * OWN, 1)
        place = i // per_tile
        ids[place] = jnp.where(lane // OWN == i % per_tile, turned, ids[place])
    ids = jnp.concatenate(ids, axis=1).astype(jnp.int32)

    coefficients = jnp.transpose(regions_ref[0:regions, :])[0:32]
    coefficients = jnp.concatenate(three_parts(coefficients), axis=0)
    region = lax.broadcasted_iota(jnp.int32, (regions, wide), 0)
    for block in range(SUB):
        chosen = region == jnp.broadcast_to(ids[block : block + 1], (regions, wide))
        found = dot(coefficients, chosen.astype(jnp.float32).astype(jnp.bfloat16))
        found = (found[0:32] + found[32:64]) + found[64:96]
        for half in range(2):
            mats[half, pl.ds(block, 32, stride=SUB), :] = found[:, half * LANES : (half + 1) * LANES]

    fine = lax.broadcasted_iota(jnp.int32, (wide, wide), 0)
    out = lax.broadcasted_iota(jnp.int32, (wide, wide), 1)
    average = jnp.zeros((wide, wide), jnp.float32)
    own_at = NEAR // 2 * OWN
    for level, (first_own, rows) in enumerate(((O0, T0), (O1, T1), (O2, T2), (O3, T3))):
        span = 2**level
        row = out - TABLE_AT[level]
        same = (row >= 0) & (row < rows) & (fine // span == row + (own_at // span - first_own))
        average = jnp.where(same, 1.0 / span, average)
    average = average.astype(jnp.bfloat16)
    used = SUB * ENTRIES
    high, middle, low = three_parts(jnp.concatenate([mats[0, 0:used], mats[1, 0:used]], axis=1))
    levels = (dot(high, average) + dot(middle, average)) + dot(low, average)

    row = lax.broadcasted_iota(jnp.int32, (SUB, wide), 1)
    weight = jnp.zeros((SUB, wide), jnp.float32) + DIFFUSION
    whole = jnp.zeros((SUB, wide), jnp.int32)
    limit = jnp.zeros((SUB, wide), jnp.int32)
    for level, first_own in enumerate((O0, O1, O2, O3)):
        here = row >= TABLE_AT[level]
        weight = jnp.where(here, DIFFUSION / 4.0**level, weight)
        whole = jnp.where(here, row - TABLE_AT[level] - first_own + device * (OWN >> level), whole)
        limit = jnp.where(here, devices * (OWN >> level), limit)
    inside = (whole >= 0) & (whole < limit)
    scale = jnp.where(inside, RELAXATION * weight, 0.0)
    unscale = 1.0 / weight

    n = FIELDS
    block = [[levels[SUB * (n * i + j) : SUB * (n * i + j + 1)] for j in range(n)] for i in range(n)]
    for i in range(n):
        block[i][i] = block[i][i] + 4.0 * weight
    entries = [block[i][j] * unscale for i in range(n) for j in range(n)]
    right = [[None] * n for _ in range(n)]
    for i in range(n):
        right[i][i] = jnp.ones((SUB, wide), jnp.float32)
    for c in range(n):
        lead = 1.0 / block[c][c]
        for j in range(c + 1, n):
            block[c][j] = block[c][j] * lead
        for j in range(n):
            if right[c][j] is not None:
                right[c][j] = right[c][j] * lead
        for i in range(n):
            if i == c:
                continue
            factor = block[i][c]
            for j in range(c + 1, n):
                block[i][j] = block[i][j] - factor * block[c][j]
            for j in range(n):
                if right[c][j] is not None:
                    term = factor * right[c][j]
                    right[i][j] = -term if right[i][j] is None else right[i][j] - term
    entries = [right[i][j] * scale for i in range(n) for j in range(n)] + entries

    group = FIELDS
    into = lax.broadcasted_iota(jnp.int32, (LANES, group * LANES), 0)
    out = lax.broadcasted_iota(jnp.int32, (LANES, group * LANES), 1)
    same = (into // (3 * SUB) == out // LANES) & (into % SUB == out % LANES // SPREAD)
    widen = same.astype(jnp.float32).astype(jnp.bfloat16)
    parts[...] = jnp.zeros_like(parts)
    for first in range(0, len(entries), group):
        for i in range(group):
            for p, part in enumerate(three_parts(entries[first + i])):
                start = (3 * i + p) * SUB
                parts[start : start + SUB, :] = part.astype(jnp.float32)
        turned = jnp.transpose(parts[...])[0:TABLE_ROWS].astype(jnp.bfloat16)
        wide_rows = dot(turned, widen)
        for i in range(group):
            table[first + i] = wide_rows[:, i * LANES : (i + 1) * LANES]


def turn(first_sub, inward):
    into = lax.broadcasted_iota(jnp.int32, (SUB * LANES, 2 * LANES), 0)
    out = lax.broadcasted_iota(jnp.int32, (1, 2 * LANES), 1)
    if inward:
        wanted = (out % LANES) * SUB + first_sub + out // LANES
    else:
        cell = out + first_sub * LANES
        wanted = (cell % SUB) * LANES + cell // SUB
    return (into == wanted).astype(jnp.float32).astype(jnp.bfloat16)


def split_kernel(where_ref, state_ref, forcing_ref, state_rows, forcing_rows, send_a, send_b, parts, held_in, sems):
    copies = [
        pltpu.make_async_copy(source, held_in.at[i], sems.at[i])
        for i, source in enumerate((state_ref, forcing_ref))
    ]
    for copy in copies:
        copy.start()
    odd = where_ref[0] % 2
    held = 2 * FIELDS * OWN
    for which, copy in enumerate(copies):
        copy.wait()
        for field in range(FIELDS):
            for p, part in enumerate(three_parts(held_in[which, field])):
                start = p * held + (which * FIELDS + field) * OWN
                parts[start : start + OWN, :] = part

    def two_subs(index):
        values = dot(parts[...], turn(2 * index, True))
        values = (values[:held] + values[held : 2 * held]) + values[2 * held :]
        for which, target in enumerate((state_rows, forcing_rows)):
            for field in range(FIELDS):
                start = (which * FIELDS + field) * OWN
                for half in range(2):
                    target[field, pl.ds(2 * index + half, OWN, stride=SUB), :] = values[
                        start : start + OWN, half * LANES : (half + 1) * LANES
                    ]

    rows_loop(0, SUB // 2, two_subs)
    low, high = 0, (OWN - FINE_HALO) * SUB
    size = FINE_HALO * SUB
    for which, rows in enumerate((state_rows, forcing_rows)):
        for field in range(FIELDS):
            first = rows[field, low : low + size, :]
            last = rows[field, high : high + size, :]
            send_a[which * FIELDS + field] = jnp.where(odd == 1, first, last)
            send_b[which * FIELDS + field] = jnp.where(odd == 1, last, first)


def place_halo(where_ref, buffer, own_rows, got_a, got_b, first, padded):
    odd = where_ref[0] % 2
    row_a = jnp.where(odd == 1, O0 - FINE_HALO, O0 + OWN)
    row_b = jnp.where(odd == 1, O0 + OWN, O0 - FINE_HALO)

    def put_row(field, row, value):
        if padded:
            put(buffer, field, row, 0, value)
        else:
            buffer[field, row] = value

    def own(row):
        start = pl.multiple_of(row * SUB, SUB)
        for field in range(FIELDS):
            put_row(field, O0 + row, own_rows[field, pl.ds(start, SUB), :])

    def halo(row):
        start = pl.multiple_of(row * SUB, SUB)
        for field in range(FIELDS):
            put_row(field, row_a + row, got_a[first + field, pl.ds(start, SUB), :])
            put_row(field, row_b + row, got_b[first + field, pl.ds(start, SUB), :])

    if own_rows is not None:
        rows_loop(0, OWN, own)
    rows_loop(0, FINE_HALO, halo)


def interior_kernel(where_ref, state, f0, table, v0, tmp0, c1, q1, tmp1):
    def own(row):
        start = pl.multiple_of(row * SUB, SUB)
        for field in range(FIELDS):
            put(v0, field, O0 + row, 0, state[field, pl.ds(start, SUB), :])

    rows_loop(0, OWN, own)
    edges(v0, 0, O0, O0 + OWN)
    source = lambda field, row: f0[field, row]
    sweep(source, v0, tmp0, table, 0, O0 + 1, O0 + OWN - 1, batch=5)
    sweep(source, tmp0, v0, table, 0, O0 + 2, O0 + OWN - 2, batch=4)
    descend(source, v0, table, 0, c1, q1, tmp1, O1 + INNER, O1 + OWN // 2 - INNER)


def down_kernel(fresh, *refs):
    half = OWN // 2
    low, high = O0 - FINE_HALO, O0 + OWN + FINE_HALO
    if fresh:
        where_ref, state, force, got_a, got_b, table, v0, v1, s1, c1, send, f0, tmp0, tmp1, q1 = refs
        place_halo(where_ref, v0, state, got_a, got_b, 0, True)
        edges(v0, 0, low, high)
        place_halo(where_ref, f0, force, got_a, got_b, FIELDS, False)
    else:
        (where_ref, v0_in, tmp0_in, c1_in, q1_in, tmp1_in, got_a, got_b, f0, table,
         v0, v1, s1, c1, send, tmp0, tmp1, q1) = refs

        def take(target, source, level, first, last):
            rows = slice(at(first, level) - 2**level, at(last, level) - 2**level)
            target[:, rows, :] = source[:, rows, :]

        take(v0, v0_in, 0, O0, O0 + OWN)
        take(tmp0, tmp0_in, 0, O0 + 1, O0 + 3)
        take(tmp0, tmp0_in, 0, O0 + OWN - 3, O0 + OWN - 1)
        inner = slice(O1 + INNER, O1 + half - INNER)
        take(c1, c1_in, 1, inner.start, inner.stop)
        take(tmp1, tmp1_in, 1, inner.start, inner.stop)
        q1[:, inner] = q1_in[:, inner]
        place_halo(where_ref, v0, None, got_a, got_b, 0, True)
        edges(v0, 0, low, O0)
        edges(v0, 0, O0 + OWN, high)
    fine_source = lambda field, row: f0[field, row]
    if fresh:
        sweep(fine_source, v0, tmp0, table, 0, low + 1, high - 1)
        sweep(fine_source, tmp0, v0, table, 0, low + 2, high - 2)
        descend(fine_source, v0, table, 0, c1, q1, tmp1, O1 - 4, O1 + half + 4)
    else:
        for swept, (old, new) in enumerate(((v0, tmp0), (tmp0, v0))):
            for first in (low + swept, O0 + OWN - 1 - swept):
                sweep(fine_source, old, new, table, 0, first, first + FINE_HALO + 1)
        for first in (O1 - 4, O1 + half - INNER):
            descend(fine_source, v0, table, 0, c1, q1, tmp1, first, first + 4 + INNER)
    make_source(c1, q1, s1, table, 1, O1 - 3, O1 + half + 3)
    first_source = lambda field, row: s1[field, row]
    sweep(first_source, tmp1, v1, table, 1, O1 - 3, O1 + half + 3)

    sub = sub_iota()

    def to_second(index):
        coarse, rest = coarsen(first_source, v1, table, 1, index + O1 // 2)
        return coarse + rest

    def pack(index, values):
        group, place = index // GROUP, index % GROUP
        mine = (sub & (GROUP - 1)) == place
        for which in range(2 * FIELDS):
            send[group, which] = jnp.where(mine, values[which], send[group, which])

    send[...] = jnp.zeros_like(send)
    batches(0, OWN // 4, COARSEN_BATCH, to_second, pack)


def spread(source, index, which, place):
    take = lambda sub: jnp.broadcast_to(source[index, which, sub : sub + 1, :], (SUB, LANES))
    return jnp.where(sub_iota() < GROUP, take(place), take(GROUP + place))


def up_kernel(last, *refs):
    if last:
        (where_ref, own, got_a, got_b, got_a2, v0, f0, v1, s1, c1, table, out,
         parts, tmp0, work0, tmp1, work1, c2, q2, s2, v2, tmp2, c3, q3, s3, v3, tmp3) = refs
    else:
        (where_ref, own, got_a, got_b, got_a2, v0, f0, v1, s1, c1, table, out,
         send_a, send_b, tmp0, work0, tmp1, work1, c2, q2, s2, v2, tmp2, c3, q3, s3, v3, tmp3) = refs
    odd = where_ref[0] % 2

    def unpack(source, index, group):
        for place in range(GROUP):
            row = group * GROUP + place
            coarse = [spread(source, index, f, place) for f in range(FIELDS)]
            rest = [spread(source, index, FIELDS + f, place) for f in range(FIELDS)]
            start = first_sweep(coarse, rest, table, 2, row)
            for field in range(FIELDS):
                put(c2, field, row, 2, coarse[field])
                q2[field, row] = rest[field]
                put(tmp2, field, row, 2, start[field])

    pick = lambda a, b: jnp.where(odd == 1, b, a)
    rows_loop(0, 2, lambda i: unpack(own, i, 4 + i))
    rows_loop(0, 2, lambda i: unpack(got_a, i, pick(6, 2) + i))
    rows_loop(0, 3, lambda i: unpack(got_b, i, pick(1, 6) + i))
    rows_loop(0, 1, lambda i: unpack(got_a2, pick(0, 2) + i, pick(8, 1) + i))

    quarter, eighth = OWN // 4, OWN // 8
    for ref in (c2, tmp2):
        edges(ref, 2, O2 - 12, O2 + quarter + 12)
    make_source(c2, q2, s2, table, 2, O2 - 11, O2 + quarter + 11)
    second_source = lambda field, row: s2[field, row]
    sweep(second_source, tmp2, v2, table, 2, O2 - 11, O2 + quarter + 11)

    descend(second_source, v2, table, 2, c3, q3, tmp3, O3 - 5, O3 + eighth + 5)
    make_source(c3, q3, s3, table, 3, O3 - 4, O3 + eighth + 4)
    third_source = lambda field, row: s3[field, row]
    sweep(third_source, tmp3, v3, table, 3, O3 - 4, O3 + eighth + 4)
    sweep(third_source, v3, tmp3, table, 3, O3 - 3, O3 + eighth + 3)
    sweep(third_source, tmp3, v3, table, 3, O3 - 2, O3 + eighth + 2, False)
    correct(v2, v2, v3, c3, 2, 0, O2 - 4, O2 + quarter + 4)
    sweep(second_source, v2, tmp2, table, 2, O2 - 3, O2 + quarter + 3)
    sweep(second_source, tmp2, v2, table, 2, O2 - 2, O2 + quarter + 2, False)

    half = OWN // 2
    first_source = lambda field, row: s1[field, row]
    correct(work1, v1, v2, c2, 1, O2 - O1 // 2, O1 - 3, O1 + half + 3)
    sweep(first_source, work1, tmp1, table, 1, O1 - 2, O1 + half + 2)
    sweep(first_source, tmp1, work1, table, 1, O1 - 1, O1 + half + 1, False)

    fine_source = lambda field, row: f0[field, row]
    correct(work0, v0, work1, c1, 0, 0, O0 - 2, O0 + OWN + 2)
    sweep(fine_source, work0, tmp0, table, 0, O0 - 1, O0 + OWN + 1)
    sweep(fine_source, tmp0, work0, table, 0, O0, O0 + OWN, False)

    if last:
        held = FIELDS * OWN
        for field in range(FIELDS):
            for sub in range(SUB):
                value = work0[field, pl.ds(at(O0, 0) + sub, OWN, stride=stride_of(0)), :]
                for p, part in enumerate(three_parts(value)):
                    start = p * held + field * OWN
                    parts[start : start + OWN, sub * LANES : (sub + 1) * LANES] = part

        def columns_out(index):
            values = dot(parts[...], turn(2 * index, False))
            values = (values[:held] + values[held : 2 * held]) + values[2 * held :]
            cells = pl.ds(pl.multiple_of(index * 2 * LANES, 2 * LANES), 2 * LANES)
            for field in range(FIELDS):
                out[field, :, cells] = values[field * OWN : (field + 1) * OWN]

        rows_loop(0, SUB // 2, columns_out)
        return

    def leave(row):
        start = pl.multiple_of(row * SUB, SUB)
        for field in range(FIELDS):
            out[field, pl.ds(start, SUB), :] = tile(work0, field, O0 + row, 0)

    rows_loop(0, OWN, leave)
    from_a, from_b = pick(OWN - FINE_HALO, 0), pick(0, OWN - FINE_HALO)

    def edge(row):
        start = pl.multiple_of(row * SUB, SUB)
        for field in range(FIELDS):
            send_a[field, pl.ds(start, SUB), :] = tile(work0, field, O0 + from_a + row, 0)
            send_b[field, pl.ds(start, SUB), :] = tile(work0, field, O0 + from_b + row, 0)

    rows_loop(0, FINE_HALO, edge)


def relay_kernel(where_ref, own, beside, row):
    odd = where_ref[0] % 2
    row[odd] = own[0]
    row[odd + 1] = own[1]
    row[2 - 2 * odd] = beside[odd]


VMEM = pl.BlockSpec(memory_space=pltpu.VMEM)
SMEM = pl.BlockSpec(memory_space=pltpu.SMEM)
HBM = pl.BlockSpec(memory_space=pltpu.HBM)


def f32(*shape):
    return jax.ShapeDtypeStruct(shape, jnp.float32)


def scratch(*shape):
    return pltpu.VMEM(shape, jnp.float32)


def padded(rows, level):
    return (FIELDS, padded_rows(rows, level), LANES)


def plain(rows):
    return (FIELDS, rows, SUB, LANES)


def call(kernel, name, grant, outs, operands, scratches=(), raw=()):
    return pl.pallas_call(
        kernel,
        out_shape=outs,
        in_specs=[SMEM] + [HBM if i in raw else VMEM for i in range(1, len(operands))],
        out_specs=[VMEM] * len(outs),
        scratch_shapes=list(scratches),
        name=name,
        compiler_params=pltpu.CompilerParams(vmem_limit_bytes=grant * 1024 * 1024),
    )(*operands)


def in_hbm(array):
    return pltpu.with_memory_space_constraint(array, pltpu.HBM)


def per_device(initial_state, forcing, coefficients, region_ids):
    size = lax.axis_size("axial")
    device = lax.axis_index("axial")
    assert initial_state.shape == (FIELDS, OWN, SUB * LANES)
    assert region_ids.shape == (OWN, SUB)
    where_ref = jnp.stack([device, jnp.int32(size)]).astype(jnp.int32)
    odd = device % 2
    pair_a = [(i, i ^ 1) for i in range(size)]
    pair_b = [(i, i + 1 if i % 2 else i - 1) for i in range(1, size - 1)]
    swap_a = lambda x: lax.ppermute(x, "axial", pair_a)
    swap_b = lambda x: lax.ppermute(x, "axial", pair_b)

    share = coefficients.shape[1]
    regions = share * size
    per_tile = LANES // OWN
    (gathered,) = call(
        functools.partial(prep_kernel, share),
        "prep",
        4,
        [f32(regions + SUB * -(-size // per_tile), LANES)],
        [where_ref, in_hbm(coefficients.T), in_hbm(region_ids.T)],
        [
            scratch(share, ENTRIES),
            pltpu.VMEM((SUB, OWN), jnp.int32),
            pltpu.SemaphoreType.DMA((2,)),
        ],
        (1, 2),
    )

    def doubled(held, step):
        return held + lax.ppermute(held, "axial", [(i, i ^ step) for i in range(size)])

    state, force, send_a, send_b = call(
        split_kernel,
        "split",
        12,
        [f32(FIELDS, OWN * SUB, LANES)] * 2 + [f32(2 * FIELDS, FINE_HALO * SUB, LANES)] * 2,
        [where_ref, in_hbm(initial_state), in_hbm(forcing)],
        [
            pltpu.VMEM((3 * 2 * FIELDS * OWN, SUB * LANES), jnp.bfloat16),
            scratch(2, FIELDS, OWN, SUB * LANES),
            pltpu.SemaphoreType.DMA((2,)),
        ],
        (1, 2),
    )
    step = 1
    while step < min(size, 4):
        gathered = doubled(gathered, step)
        step *= 2
    gathered, send_a, send_b = lax.optimization_barrier((gathered, send_a, send_b))
    got_b, got_a = swap_b(send_b), swap_a(send_a)
    if size > 4:
        free = [i for i in range(size) if i % 2 != i // 2 % 2]
        while step < size:
            gathered = gathered + lax.ppermute(gathered, "axial", [(i, i ^ step) for i in free])
            step *= 2
        gathered = jnp.where(odd != device // 2 % 2, gathered, swap_a(gathered))
    (table,) = call(
        functools.partial(tables_kernel, regions),
        "tables", 12,
        [f32(2 * ENTRIES, TABLE_ROWS, LANES)],
        [where_ref, gathered],
        [scratch(2, 32 * SUB, LANES), scratch(LANES, 2 * LANES)],
    )

    f0 = None
    for cycle in range(CYCLES):
        outs = [f32(*padded(T0, 0)), f32(*padded(T1, 1)), f32(*plain(T1)), f32(*padded(T1, 1)),
                f32(2, 2 * FIELDS, SUB, LANES)]
        temps = [scratch(*padded(T0, 0)), scratch(*padded(T1, 1)), scratch(*plain(T1))]
        if cycle == 0:
            v0, v1, s1, c1, own, f0 = call(
                functools.partial(down_kernel, True), "down_fresh", 14, outs + [f32(*plain(T0))],
                [where_ref, state, force, got_a, got_b, table], temps,
            )
        else:
            inner = call(
                interior_kernel, "interior", 4,
                [f32(*padded(T0, 0))] * 2 + [f32(*padded(T1, 1)), f32(*plain(T1)), f32(*padded(T1, 1))],
                [where_ref, state, f0, table],
            )
            v0, v1, s1, c1, own = call(
                functools.partial(down_kernel, False), "down", 14, outs,
                [where_ref, *inner, got_a, got_b, f0, table], temps,
            )
        beside = swap_a(own)
        (row,) = call(
            relay_kernel, "relay", 2, [f32(3, 2 * FIELDS, SUB, LANES)], [where_ref, own, beside]
        )
        far = swap_b(row)
        beyond = swap_a(far)
        operands = [where_ref, own, beside, far, beyond, v0, f0, v1, s1, c1, table]
        temps = [scratch(*padded(T0, 0))] * 2 + [scratch(*padded(T1, 1))] * 2
        temps += [scratch(*padded(T2, 2)), scratch(*plain(T2)), scratch(*plain(T2)), scratch(*padded(T2, 2)), scratch(*padded(T2, 2))]
        temps += [scratch(*padded(T3, 3)), scratch(*plain(T3)), scratch(*plain(T3)), scratch(*padded(T3, 3)), scratch(*padded(T3, 3))]
        if cycle == CYCLES - 1:
            return call(
                functools.partial(up_kernel, True), "up_last", 26,
                [f32(FIELDS, OWN, SUB * LANES)], operands,
                [pltpu.VMEM((3 * FIELDS * OWN, SUB * LANES), jnp.bfloat16)] + temps,
            )[0]
        state, send_a, send_b = call(
            functools.partial(up_kernel, False), "up", 26,
            [f32(FIELDS, OWN * SUB, LANES)] + [f32(FIELDS, FINE_HALO * SUB, LANES)] * 2,
            operands, temps,
        )
        got_b, got_a = swap_b(send_b), swap_a(send_a)


def solution(mesh):
    placed = (
        P("sample", "axial", None),
        P("sample", "axial", None),
        P("sample", "axial"),
        P("axial", None),
    )
    return jax.shard_map(
        per_device,
        mesh=mesh,
        in_specs=placed,
        out_specs=P("sample", "axial", None),
        check_vma=False,
    )
```

```python
import functools

import jax
import jax.numpy as jnp
from jax import lax
from jax.experimental import pallas as pl
from jax.experimental.pallas import tpu as pltpu
from jax.sharding import PartitionSpec as P

DIFFUSION = 1.0
RELAXATION = 0.8
SOURCE_GAIN = 0.05
CYCLES = 2

FIELDS = 5
ENTRIES = FIELDS * FIELDS
SUB, LANES = 8, 128

OWN = 32
FINE_HALO = 11
T0, O0 = 64, 16
T1, O1 = 32, 8
T2, O2 = 40, 16
T3, O3 = 20, 8
COARSEST = 3
EDGE_BATCH = 10
GROUP = 4
HELD_PARTS = 2
SPREAD = 16


def stride_of(level):
    return SUB + (0 if level == COARSEST else 2 * 2**level) + (level == 2)


def padded_rows(rows, level):
    return stride_of(level) * (rows + SUB)


def at(row, level):
    return stride_of(level) * row + (0 if level == COARSEST else 2**level)


def lane_iota():
    return lax.broadcasted_iota(jnp.int32, (SUB, LANES), 1)


def sub_iota():
    return lax.broadcasted_iota(jnp.int32, (SUB, LANES), 0)


def tile(ref, field, row, level):
    return ref[field, pl.ds(at(row, level), SUB), :]


def put(ref, field, row, level, value):
    ref[field, pl.ds(at(row, level), SUB), :] = value


def edges(ref, level, first, last):
    if level == COARSEST:
        return
    width, stride, lane = 2**level, stride_of(level), lane_iota()
    places = [(row, field) for row in range(first, last, SUB) for field in range(FIELDS)]
    for part in range(0, len(places), EDGE_BATCH):
        written = []
        for row, field in places[part : part + EDGE_BATCH]:
            rows = lambda sub, row=row, field=field: (
                field, pl.ds(at(row, level) + sub, SUB, stride=stride), slice(None)
            )
            before = jnp.where(lane == 0, 0.0, pltpu.roll(ref[rows(SUB - 1)], 1, 1))
            after = jnp.where(lane == LANES - 1, 0.0, pltpu.roll(ref[rows(0)], LANES - 1, 1))
            written.append((rows, before, after))
        for rows, before, after in written:
            for i in range(width):
                ref[rows(i - width)] = before
                ref[rows(SUB + i)] = after


def rows_loop(first, last, body):
    def step(row, carry):
        body(row)
        return carry

    lax.fori_loop(first, last, step, 0)


def batches(first, last, batch, compute, store):
    def body(index):
        rows = [first + index * batch + i for i in range(batch)]
        results = [compute(row) for row in rows]
        for row, result in zip(rows, results):
            store(row, result)

    rows_loop(0, -(-(last - first) // batch), body)


def neighbours(ref, row, level):
    start, width, stride = at(row, level), 2**level, stride_of(level)
    lane = lane_iota()
    sums, centres = [], []
    for field in range(FIELDS):
        load = lambda first, field=field: ref[field, pl.ds(first, SUB), :]
        centre = load(start)
        if level == COARSEST:
            radial = jnp.where(lane == 0, 0.0, pltpu.roll(centre, 1, 1)) + jnp.where(
                lane == LANES - 1, 0.0, pltpu.roll(centre, LANES - 1, 1)
            )
        else:
            radial = load(start - width) + load(start + width)
        sums.append(radial + (load(start - stride) + load(start + stride)))
        centres.append(centre)
    return sums, centres


def block_times(table, level, row, first, vectors):
    row = TABLE_AT[level] + row
    out = []
    for i in range(FIELDS):
        total = None
        for j in range(FIELDS):
            entry = first + FIELDS * i + j
            term = jnp.broadcast_to(table[entry, pl.ds(row, 1), :], (SUB, LANES)) * vectors[j]
            total = term if total is None else total + term
        out.append(total)
    return out


MATRIX_AT = ENTRIES
TABLE_AT = (0, T0, T0 + T1, T0 + T1 + T2)
TABLE_ROWS = 160
NEAR = 5


def gain_of(level):
    return SOURCE_GAIN * 4.0**level / DIFFUSION


def sweep(source_of, old, new, table, level, first, last, more=True, batch=None):
    gain = gain_of(level)

    def compute(row):
        sums, centres = neighbours(old, row, level)
        rest = [
            (source_of(field, row) + sums[field]) - gain * jnp.tanh(centres[field])
            for field in range(FIELDS)
        ]
        moved = block_times(table, level, row, 0, rest)
        return [(1.0 - RELAXATION) * centres[f] + moved[f] for f in range(FIELDS)]

    def store(row, values):
        for field in range(FIELDS):
            put(new, field, row, level, values[field])

    batches(first, last, batch or SWEEP_BATCH, compute, store)
    if more:
        edges(new, level, first, last)


def residual(source_of, values, table, level, row):
    gain = gain_of(level)
    sums, centres = neighbours(values, row, level)
    applied = block_times(table, level, row, MATRIX_AT, centres)
    left = [
        ((source_of(field, row) + sums[field]) - gain * jnp.tanh(centres[field])) - applied[field]
        for field in range(FIELDS)
    ]
    return left, centres


def pair_sum(value, level):
    width = 2**level
    other = pltpu.roll(value, SUB - width, 0)
    if 2 * width != SUB:
        other = jnp.where((sub_iota() & width) == 0, other, pltpu.roll(value, width, 0))
    return value + other


def coarsen(source_of, values, table, level, row):
    upper_r, upper_v = residual(source_of, values, table, level, 2 * row)
    lower_r, lower_v = residual(source_of, values, table, level, 2 * row + 1)
    coarse = [0.25 * pair_sum(upper_v[f] + lower_v[f], level) for f in range(FIELDS)]
    rest = [pair_sum(upper_r[f] + lower_r[f], level) for f in range(FIELDS)]
    return coarse, rest


def first_sweep(coarse, rest, table, level, row):
    moved = block_times(table, level, row, 0, rest)
    return [coarse[f] + moved[f] for f in range(FIELDS)]


def descend(source_of, values, table, level, c, q, first_values, first, last):
    def compute(row):
        coarse, rest = coarsen(source_of, values, table, level, row)
        return coarse, rest, first_sweep(coarse, rest, table, level + 1, row)

    def store(row, results):
        for field in range(FIELDS):
            put(c, field, row, level + 1, results[0][field])
            q[field, row] = results[1][field]
            put(first_values, field, row, level + 1, results[2][field])

    batches(first, last, COARSEN_BATCH, compute, store)
    edges(c, level + 1, first, last)
    edges(first_values, level + 1, first, last)


def make_source(coarse, rest, source, table, level, first, last):
    gain = gain_of(level)

    def compute(row):
        sums, centres = neighbours(coarse, row, level)
        applied = block_times(table, level, row, MATRIX_AT, centres)
        return [
            (applied[f] - sums[f]) + (gain * jnp.tanh(centres[f]) + rest[f, row])
            for f in range(FIELDS)
        ]

    def store(row, values):
        for field in range(FIELDS):
            source[field, row] = values[field]

    batches(first, last, SWEEP_BATCH, compute, store)


def correct(new, fine, after, before, level, offset, first, last):
    def body(index):
        coarse_row = first // 2 + index + offset
        row = first // 2 * 2 + 2 * index
        for field in range(FIELDS):
            change = tile(after, field, coarse_row, level + 1) - tile(before, field, coarse_row, level + 1)
            put(new, field, row, level, tile(fine, field, row, level) + change)
            put(new, field, row + 1, level, tile(fine, field, row + 1, level) + change)

    rows_loop(0, (last + 1) // 2 - first // 2, body)
    edges(new, level, first, last)


SWEEP_BATCH = 4
INNER = 2
COARSEN_BATCH = 2


def three_parts(value):
    high = value.astype(jnp.bfloat16)
    rest = value - high.astype(jnp.float32)
    middle = rest.astype(jnp.bfloat16)
    low = (rest - middle.astype(jnp.float32)).astype(jnp.bfloat16)
    return high, middle, low


def dot(left, right):
    return jnp.dot(left, right, preferred_element_type=jnp.float32)


def prep_kernel(share, where_ref, coefficients_ref, ids_ref, out, own_coefficients, own_ids, sems):
    device, devices = where_ref[0], where_ref[1]
    copies = [
        pltpu.make_async_copy(coefficients_ref, own_coefficients, sems.at[0]),
        pltpu.make_async_copy(ids_ref, own_ids, sems.at[1]),
    ]
    for copy in copies:
        copy.start()
    out[...] = jnp.zeros_like(out)
    for copy in copies:
        copy.wait()
    for i in range(share):
        out[pl.ds(device * share + i, 1), 0:ENTRIES] = own_coefficients[i : i + 1, :]
    ids = own_ids[...].astype(jnp.float32)
    per_tile = LANES // OWN
    start = pl.multiple_of(devices * share + device // per_tile * SUB, SUB)
    for place in range(per_tile):

        @pl.when(device % per_tile == place)
        def _():
            out[pl.ds(start, SUB), place * OWN : (place + 1) * OWN] = ids


def tables_kernel(regions, where_ref, regions_ref, table, mats, parts):
    device, devices = where_ref[0], where_ref[1]
    wide = 2 * LANES
    lane = lane_iota()
    ids = [jnp.full((SUB, LANES), -1.0, jnp.float32)] * 2
    per_tile = LANES // OWN
    for i in range(NEAR):
        owner = jnp.clip(device + (i - NEAR // 2), 0, devices - 1)
        start = pl.multiple_of(regions + owner // per_tile * SUB, SUB)
        held = regions_ref[pl.ds(start, SUB), :]
        turned = pltpu.roll(held, ((i % per_tile) - owner % per_tile + per_tile) % per_tile * OWN, 1)
        place = i // per_tile
        ids[place] = jnp.where(lane // OWN == i % per_tile, turned, ids[place])
    ids = jnp.concatenate(ids, axis=1).astype(jnp.int32)

    coefficients = jnp.transpose(regions_ref[0:regions, :])[0:32]
    coefficients = jnp.concatenate(three_parts(coefficients), axis=0)
    region = lax.broadcasted_iota(jnp.int32, (regions, wide), 0)
    for block in range(SUB):
        chosen = region == jnp.broadcast_to(ids[block : block + 1], (regions, wide))
        found = dot(coefficients, chosen.astype(jnp.float32).astype(jnp.bfloat16))
        found = (found[0:32] + found[32:64]) + found[64:96]
        for half in range(2):
            mats[half, pl.ds(block, 32, stride=SUB), :] = found[:, half * LANES : (half + 1) * LANES]

    fine = lax.broadcasted_iota(jnp.int32, (wide, wide), 0)
    out = lax.broadcasted_iota(jnp.int32, (wide, wide), 1)
    average = jnp.zeros((wide, wide), jnp.float32)
    own_at = NEAR // 2 * OWN
    for level, (first_own, rows) in enumerate(((O0, T0), (O1, T1), (O2, T2), (O3, T3))):
        span = 2**level
        row = out - TABLE_AT[level]
        same = (row >= 0) & (row < rows) & (fine // span == row + (own_at // span - first_own))
        average = jnp.where(same, 1.0 / span, average)
    average = average.astype(jnp.bfloat16)
    used = SUB * ENTRIES
    high, middle, low = three_parts(jnp.concatenate([mats[0, 0:used], mats[1, 0:used]], axis=1))
    levels = (dot(high, average) + dot(middle, average)) + dot(low, average)

    row = lax.broadcasted_iota(jnp.int32, (SUB, wide), 1)
    weight = jnp.zeros((SUB, wide), jnp.float32) + DIFFUSION
    whole = jnp.zeros((SUB, wide), jnp.int32)
    limit = jnp.zeros((SUB, wide), jnp.int32)
    for level, first_own in enumerate((O0, O1, O2, O3)):
        here = row >= TABLE_AT[level]
        weight = jnp.where(here, DIFFUSION / 4.0**level, weight)
        whole = jnp.where(here, row - TABLE_AT[level] - first_own + device * (OWN >> level), whole)
        limit = jnp.where(here, devices * (OWN >> level), limit)
    inside = (whole >= 0) & (whole < limit)
    scale = jnp.where(inside, RELAXATION * weight, 0.0)
    unscale = 1.0 / weight

    n = FIELDS
    block = [[levels[SUB * (n * i + j) : SUB * (n * i + j + 1)] for j in range(n)] for i in range(n)]
    for i in range(n):
        block[i][i] = block[i][i] + 4.0 * weight
    entries = [block[i][j] * unscale for i in range(n) for j in range(n)]
    right = [[None] * n for _ in range(n)]
    for i in range(n):
        right[i][i] = jnp.ones((SUB, wide), jnp.float32)
    for c in range(n):
        lead = 1.0 / block[c][c]
        for j in range(c + 1, n):
            block[c][j] = block[c][j] * lead
        for j in range(n):
            if right[c][j] is not None:
                right[c][j] = right[c][j] * lead
        for i in range(n):
            if i == c:
                continue
            factor = block[i][c]
            for j in range(c + 1, n):
                block[i][j] = block[i][j] - factor * block[c][j]
            for j in range(n):
                if right[c][j] is not None:
                    term = factor * right[c][j]
                    right[i][j] = -term if right[i][j] is None else right[i][j] - term
    entries = [right[i][j] * scale for i in range(n) for j in range(n)] + entries

    group = FIELDS
    into = lax.broadcasted_iota(jnp.int32, (LANES, group * LANES), 0)
    out = lax.broadcasted_iota(jnp.int32, (LANES, group * LANES), 1)
    same = (into // (3 * SUB) == out // LANES) & (into % SUB == out % LANES // SPREAD)
    widen = same.astype(jnp.float32).astype(jnp.bfloat16)
    parts[...] = jnp.zeros_like(parts)
    for first in range(0, len(entries), group):
        for i in range(group):
            for p, part in enumerate(three_parts(entries[first + i])):
                start = (3 * i + p) * SUB
                parts[start : start + SUB, :] = part.astype(jnp.float32)
        turned = jnp.transpose(parts[...])[0:TABLE_ROWS].astype(jnp.bfloat16)
        wide_rows = dot(turned, widen)
        for i in range(group):
            table[first + i] = wide_rows[:, i * LANES : (i + 1) * LANES]


def turn(first_sub, inward):
    into = lax.broadcasted_iota(jnp.int32, (SUB * LANES, 2 * LANES), 0)
    out = lax.broadcasted_iota(jnp.int32, (1, 2 * LANES), 1)
    if inward:
        wanted = (out % LANES) * SUB + first_sub + out // LANES
    else:
        cell = out + first_sub * LANES
        wanted = (cell % SUB) * LANES + cell // SUB
    return (into == wanted).astype(jnp.float32).astype(jnp.bfloat16)


def split_kernel(where_ref, state_ref, forcing_ref, state_rows, forcing_rows, send_a, send_b, parts, held_in, sems):
    copies = [
        pltpu.make_async_copy(source, held_in.at[i], sems.at[i])
        for i, source in enumerate((state_ref, forcing_ref))
    ]
    for copy in copies:
        copy.start()
    odd = where_ref[0] % 2
    held = 2 * FIELDS * OWN
    for which, copy in enumerate(copies):
        copy.wait()
        for field in range(FIELDS):
            for p, part in enumerate(three_parts(held_in[which, field])[:HELD_PARTS]):
                start = p * held + (which * FIELDS + field) * OWN
                parts[start : start + OWN, :] = part

    def two_subs(index):
        values = dot(parts[...], turn(2 * index, True))
        values = values[:held] + values[held:]
        for which, target in enumerate((state_rows, forcing_rows)):
            for field in range(FIELDS):
                start = (which * FIELDS + field) * OWN
                for half in range(2):
                    target[field, pl.ds(2 * index + half, OWN, stride=SUB), :] = values[
                        start : start + OWN, half * LANES : (half + 1) * LANES
                    ]

    rows_loop(0, SUB // 2, two_subs)
    low, high = 0, (OWN - FINE_HALO) * SUB
    size = FINE_HALO * SUB
    for which, rows in enumerate((state_rows, forcing_rows)):
        for field in range(FIELDS):
            first = rows[field, low : low + size, :]
            last = rows[field, high : high + size, :]
            send_a[which * FIELDS + field] = jnp.where(odd == 1, first, last)
            send_b[which * FIELDS + field] = jnp.where(odd == 1, last, first)


def place_halo(where_ref, buffer, own_rows, got_a, got_b, first, padded):
    odd = where_ref[0] % 2
    row_a = jnp.where(odd == 1, O0 - FINE_HALO, O0 + OWN)
    row_b = jnp.where(odd == 1, O0 + OWN, O0 - FINE_HALO)

    def put_row(field, row, value):
        if padded:
            put(buffer, field, row, 0, value)
        else:
            buffer[field, row] = value

    def own(row):
        start = pl.multiple_of(row * SUB, SUB)
        for field in range(FIELDS):
            put_row(field, O0 + row, own_rows[field, pl.ds(start, SUB), :])

    def halo(row):
        start = pl.multiple_of(row * SUB, SUB)
        for field in range(FIELDS):
            put_row(field, row_a + row, got_a[first + field, pl.ds(start, SUB), :])
            put_row(field, row_b + row, got_b[first + field, pl.ds(start, SUB), :])

    if own_rows is not None:
        rows_loop(0, OWN, own)
    rows_loop(0, FINE_HALO, halo)


def interior_kernel(fresh, where_ref, state, force, table, v0, tmp0, c1, q1, tmp1):
    def own(row):
        start = pl.multiple_of(row * SUB, SUB)
        for field in range(FIELDS):
            put(v0, field, O0 + row, 0, state[field, pl.ds(start, SUB), :])

    rows_loop(0, OWN, own)
    edges(v0, 0, O0, O0 + OWN)
    if fresh:
        source = lambda field, row: force[field, pl.ds(pl.multiple_of((row - O0) * SUB, SUB), SUB), :]
    else:
        source = lambda field, row: force[field, row]
    sweep(source, v0, tmp0, table, 0, O0 + 1, O0 + OWN - 1, batch=5)
    sweep(source, tmp0, v0, table, 0, O0 + 2, O0 + OWN - 2, batch=4)
    descend(source, v0, table, 0, c1, q1, tmp1, O1 + INNER, O1 + OWN // 2 - INNER)


def down_kernel(fresh, *refs):
    half = OWN // 2
    low, high = O0 - FINE_HALO, O0 + OWN + FINE_HALO
    if fresh:
        (where_ref, v0_in, tmp0_in, c1_in, q1_in, tmp1_in, force, got_a, got_b, table,
         v0, v1, s1, c1, send, f0, tmp0, tmp1, q1) = refs
        place_halo(where_ref, f0, force, got_a, got_b, FIELDS, False)
    else:
        (where_ref, v0_in, tmp0_in, c1_in, q1_in, tmp1_in, got_a, got_b, f0, table,
         v0, v1, s1, c1, send, tmp0, tmp1, q1) = refs

    def take(target, source, level, first, last):
        rows = slice(at(first, level) - 2**level, at(last, level) - 2**level)
        target[:, rows, :] = source[:, rows, :]

    take(v0, v0_in, 0, O0, O0 + OWN)
    take(tmp0, tmp0_in, 0, O0 + 1, O0 + 3)
    take(tmp0, tmp0_in, 0, O0 + OWN - 3, O0 + OWN - 1)
    inner = slice(O1 + INNER, O1 + half - INNER)
    take(c1, c1_in, 1, inner.start, inner.stop)
    take(tmp1, tmp1_in, 1, inner.start, inner.stop)
    q1[:, inner] = q1_in[:, inner]
    place_halo(where_ref, v0, None, got_a, got_b, 0, True)
    edges(v0, 0, low, O0)
    edges(v0, 0, O0 + OWN, high)
    fine_source = lambda field, row: f0[field, row]
    for swept, (old, new) in enumerate(((v0, tmp0), (tmp0, v0))):
        for first in (low + swept, O0 + OWN - 1 - swept):
            sweep(fine_source, old, new, table, 0, first, first + FINE_HALO + 1)
    for first in (O1 - 4, O1 + half - INNER):
        descend(fine_source, v0, table, 0, c1, q1, tmp1, first, first + 4 + INNER)
    make_source(c1, q1, s1, table, 1, O1 - 3, O1 + half + 3)
    first_source = lambda field, row: s1[field, row]
    sweep(first_source, tmp1, v1, table, 1, O1 - 3, O1 + half + 3)

    sub = sub_iota()

    def to_second(index):
        coarse, rest = coarsen(first_source, v1, table, 1, index + O1 // 2)
        return coarse + rest

    def pack(index, values):
        group, place = index // GROUP, index % GROUP
        mine = (sub & (GROUP - 1)) == place
        for which in range(2 * FIELDS):
            send[group, which] = jnp.where(mine, values[which], send[group, which])

    send[...] = jnp.zeros_like(send)
    batches(0, OWN // 4, COARSEN_BATCH, to_second, pack)


def spread(source, index, which, place):
    take = lambda sub: jnp.broadcast_to(source[index, which, sub : sub + 1, :], (SUB, LANES))
    return jnp.where(sub_iota() < GROUP, take(place), take(GROUP + place))


def up_kernel(last, *refs):
    if last:
        (where_ref, own, got_a, got_b, got_a2, v0, f0, v1, s1, c1, table, out,
         parts, tmp0, work0, tmp1, work1, c2, q2, s2, v2, tmp2, c3, q3, s3, v3, tmp3) = refs
    else:
        (where_ref, own, got_a, got_b, got_a2, v0, f0, v1, s1, c1, table, out,
         send_a, send_b, tmp0, work0, tmp1, work1, c2, q2, s2, v2, tmp2, c3, q3, s3, v3, tmp3) = refs
    odd = where_ref[0] % 2

    def unpack(source, index, group):
        for place in range(GROUP):
            row = group * GROUP + place
            coarse = [spread(source, index, f, place) for f in range(FIELDS)]
            rest = [spread(source, index, FIELDS + f, place) for f in range(FIELDS)]
            start = first_sweep(coarse, rest, table, 2, row)
            for field in range(FIELDS):
                put(c2, field, row, 2, coarse[field])
                q2[field, row] = rest[field]
                put(tmp2, field, row, 2, start[field])

    pick = lambda a, b: jnp.where(odd == 1, b, a)
    rows_loop(0, 2, lambda i: unpack(own, i, 4 + i))
    rows_loop(0, 2, lambda i: unpack(got_a, i, pick(6, 2) + i))
    rows_loop(0, 3, lambda i: unpack(got_b, i, pick(1, 6) + i))
    rows_loop(0, 1, lambda i: unpack(got_a2, pick(0, 2) + i, pick(8, 1) + i))

    quarter, eighth = OWN // 4, OWN // 8
    for ref in (c2, tmp2):
        edges(ref, 2, O2 - 12, O2 + quarter + 12)
    make_source(c2, q2, s2, table, 2, O2 - 11, O2 + quarter + 11)
    second_source = lambda field, row: s2[field, row]
    sweep(second_source, tmp2, v2, table, 2, O2 - 11, O2 + quarter + 11)

    descend(second_source, v2, table, 2, c3, q3, tmp3, O3 - 5, O3 + eighth + 5)
    make_source(c3, q3, s3, table, 3, O3 - 4, O3 + eighth + 4)
    third_source = lambda field, row: s3[field, row]
    sweep(third_source, tmp3, v3, table, 3, O3 - 4, O3 + eighth + 4)
    sweep(third_source, v3, tmp3, table, 3, O3 - 3, O3 + eighth + 3)
    sweep(third_source, tmp3, v3, table, 3, O3 - 2, O3 + eighth + 2, False)
    correct(v2, v2, v3, c3, 2, 0, O2 - 4, O2 + quarter + 4)
    sweep(second_source, v2, tmp2, table, 2, O2 - 3, O2 + quarter + 3)
    sweep(second_source, tmp2, v2, table, 2, O2 - 2, O2 + quarter + 2, False)

    half = OWN // 2
    first_source = lambda field, row: s1[field, row]
    correct(work1, v1, v2, c2, 1, O2 - O1 // 2, O1 - 3, O1 + half + 3)
    sweep(first_source, work1, tmp1, table, 1, O1 - 2, O1 + half + 2)
    sweep(first_source, tmp1, work1, table, 1, O1 - 1, O1 + half + 1, False)

    fine_source = lambda field, row: f0[field, row]
    correct(work0, v0, work1, c1, 0, 0, O0 - 2, O0 + OWN + 2)
    sweep(fine_source, work0, tmp0, table, 0, O0 - 1, O0 + OWN + 1)
    sweep(fine_source, tmp0, work0, table, 0, O0, O0 + OWN, False)

    if last:
        held = FIELDS * OWN
        for field in range(FIELDS):
            for sub in range(SUB):
                value = work0[field, pl.ds(at(O0, 0) + sub, OWN, stride=stride_of(0)), :]
                for p, part in enumerate(three_parts(value)[:HELD_PARTS]):
                    start = p * held + field * OWN
                    parts[start : start + OWN, sub * LANES : (sub + 1) * LANES] = part

        def columns_out(index):
            values = dot(parts[...], turn(2 * index, False))
            values = values[:held] + values[held:]
            cells = pl.ds(pl.multiple_of(index * 2 * LANES, 2 * LANES), 2 * LANES)
            for field in range(FIELDS):
                out[field, :, cells] = values[field * OWN : (field + 1) * OWN]

        rows_loop(0, SUB // 2, columns_out)
        return

    def leave(row):
        start = pl.multiple_of(row * SUB, SUB)
        for field in range(FIELDS):
            out[field, pl.ds(start, SUB), :] = tile(work0, field, O0 + row, 0)

    rows_loop(0, OWN, leave)
    from_a, from_b = pick(OWN - FINE_HALO, 0), pick(0, OWN - FINE_HALO)

    def edge(row):
        start = pl.multiple_of(row * SUB, SUB)
        for field in range(FIELDS):
            send_a[field, pl.ds(start, SUB), :] = tile(work0, field, O0 + from_a + row, 0)
            send_b[field, pl.ds(start, SUB), :] = tile(work0, field, O0 + from_b + row, 0)

    rows_loop(0, FINE_HALO, edge)


def relay_kernel(where_ref, own, beside, row):
    odd = where_ref[0] % 2
    row[odd] = own[0]
    row[odd + 1] = own[1]
    row[2 - 2 * odd] = beside[odd]


VMEM = pl.BlockSpec(memory_space=pltpu.VMEM)
SMEM = pl.BlockSpec(memory_space=pltpu.SMEM)
HBM = pl.BlockSpec(memory_space=pltpu.HBM)


def f32(*shape):
    return jax.ShapeDtypeStruct(shape, jnp.float32)


def scratch(*shape):
    return pltpu.VMEM(shape, jnp.float32)


def padded(rows, level):
    return (FIELDS, padded_rows(rows, level), LANES)


def plain(rows):
    return (FIELDS, rows, SUB, LANES)


def call(kernel, name, grant, outs, operands, scratches=(), raw=()):
    return pl.pallas_call(
        kernel,
        out_shape=outs,
        in_specs=[SMEM] + [HBM if i in raw else VMEM for i in range(1, len(operands))],
        out_specs=[VMEM] * len(outs),
        scratch_shapes=list(scratches),
        name=name,
        compiler_params=pltpu.CompilerParams(vmem_limit_bytes=grant * 1024 * 1024),
    )(*operands)


def in_hbm(array):
    return pltpu.with_memory_space_constraint(array, pltpu.HBM)


def per_device(initial_state, forcing, coefficients, region_ids):
    size = lax.axis_size("axial")
    device = lax.axis_index("axial")
    assert initial_state.shape == (FIELDS, OWN, SUB * LANES)
    assert region_ids.shape == (OWN, SUB)
    where_ref = jnp.stack([device, jnp.int32(size)]).astype(jnp.int32)
    odd = device % 2
    pair_a = [(i, i ^ 1) for i in range(size)]
    pair_b = [(i, i + 1 if i % 2 else i - 1) for i in range(1, size - 1)]
    swap_a = lambda x: lax.ppermute(x, "axial", pair_a)
    swap_b = lambda x: lax.ppermute(x, "axial", pair_b)

    share = coefficients.shape[1]
    regions = share * size
    per_tile = LANES // OWN
    (gathered,) = call(
        functools.partial(prep_kernel, share),
        "prep",
        4,
        [f32(regions + SUB * -(-size // per_tile), LANES)],
        [where_ref, in_hbm(coefficients.T), in_hbm(region_ids.T)],
        [
            scratch(share, ENTRIES),
            pltpu.VMEM((SUB, OWN), jnp.int32),
            pltpu.SemaphoreType.DMA((2,)),
        ],
        (1, 2),
    )

    def doubled(held, step):
        return held + lax.ppermute(held, "axial", [(i, i ^ step) for i in range(size)])

    state, force, send_a, send_b = call(
        split_kernel,
        "split",
        12,
        [f32(FIELDS, OWN * SUB, LANES)] * 2 + [f32(2 * FIELDS, FINE_HALO * SUB, LANES)] * 2,
        [where_ref, in_hbm(initial_state), in_hbm(forcing)],
        [
            pltpu.VMEM((HELD_PARTS * 2 * FIELDS * OWN, SUB * LANES), jnp.bfloat16),
            scratch(2, FIELDS, OWN, SUB * LANES),
            pltpu.SemaphoreType.DMA((2,)),
        ],
        (1, 2),
    )
    step = 1
    while step < min(size, 8):
        gathered = doubled(gathered, step)
        step *= 2
    gathered, send_a, send_b = lax.optimization_barrier((gathered, send_a, send_b))
    got_b, got_a = swap_b(send_b), swap_a(send_a)
    if step < size:
        free = [i for i in range(size) if i % 2 != i // 2 % 2]
        while step < size:
            gathered = gathered + lax.ppermute(gathered, "axial", [(i, i ^ step) for i in free])
            step *= 2
        gathered = jnp.where(odd != device // 2 % 2, gathered, swap_a(gathered))
    (table,) = call(
        functools.partial(tables_kernel, regions),
        "tables", 12,
        [f32(2 * ENTRIES, TABLE_ROWS, LANES)],
        [where_ref, gathered],
        [scratch(2, 32 * SUB, LANES), scratch(LANES, 2 * LANES)],
    )

    f0 = None
    for cycle in range(CYCLES):
        outs = [f32(*padded(T0, 0)), f32(*padded(T1, 1)), f32(*plain(T1)), f32(*padded(T1, 1)),
                f32(2, 2 * FIELDS, SUB, LANES)]
        temps = [scratch(*padded(T0, 0)), scratch(*padded(T1, 1)), scratch(*plain(T1))]
        fresh = cycle == 0
        inner = call(
            functools.partial(interior_kernel, fresh), "interior", 4,
            [f32(*padded(T0, 0))] * 2 + [f32(*padded(T1, 1)), f32(*plain(T1)), f32(*padded(T1, 1))],
            [where_ref, state, force if fresh else f0, table],
        )
        if fresh:
            v0, v1, s1, c1, own, f0 = call(
                functools.partial(down_kernel, True), "down_fresh", 14, outs + [f32(*plain(T0))],
                [where_ref, *inner, force, got_a, got_b, table], temps,
            )
        else:
            v0, v1, s1, c1, own = call(
                functools.partial(down_kernel, False), "down", 14, outs,
                [where_ref, *inner, got_a, got_b, f0, table], temps,
            )
        beside = swap_a(own)
        (row,) = call(
            relay_kernel, "relay", 2, [f32(3, 2 * FIELDS, SUB, LANES)], [where_ref, own, beside]
        )
        far = swap_b(row)
        beyond = swap_a(far)
        operands = [where_ref, own, beside, far, beyond, v0, f0, v1, s1, c1, table]
        temps = [scratch(*padded(T0, 0))] * 2 + [scratch(*padded(T1, 1))] * 2
        temps += [scratch(*padded(T2, 2)), scratch(*plain(T2)), scratch(*plain(T2)), scratch(*padded(T2, 2)), scratch(*padded(T2, 2))]
        temps += [scratch(*padded(T3, 3)), scratch(*plain(T3)), scratch(*plain(T3)), scratch(*padded(T3, 3)), scratch(*padded(T3, 3))]
        if cycle == CYCLES - 1:
            return call(
                functools.partial(up_kernel, True), "up_last", 26,
                [f32(FIELDS, OWN, SUB * LANES)], operands,
                [pltpu.VMEM((HELD_PARTS * FIELDS * OWN, SUB * LANES), jnp.bfloat16)] + temps,
            )[0]
        state, send_a, send_b = call(
            functools.partial(up_kernel, False), "up", 26,
            [f32(FIELDS, OWN * SUB, LANES)] + [f32(FIELDS, FINE_HALO * SUB, LANES)] * 2,
            operands, temps,
        )
        got_b, got_a = swap_b(send_b), swap_a(send_a)


def solution(mesh):
    placed = (
        P("sample", "axial", None),
        P("sample", "axial", None),
        P("sample", "axial"),
        P("axial", None),
    )
    return jax.shard_map(
        per_device,
        mesh=mesh,
        in_specs=placed,
        out_specs=P("sample", "axial", None),
        check_vma=False,
    )
```

```python
import functools

import jax
import jax.numpy as jnp
from jax import lax
from jax.experimental import pallas as pl
from jax.experimental.pallas import tpu as pltpu
from jax.sharding import PartitionSpec as P


DIFFUSION = 1.0
RELAXATION = 0.8
SOURCE_GAIN = 0.05
CYCLES = 2

FIELDS = 5
ENTRIES = FIELDS * FIELDS
SUB, LANES = 8, 128

OWN = 32
FINE_HALO = 11
T0, O0 = 64, 16
T1, O1 = 32, 8
T2, O2 = 40, 16
T3, O3 = 20, 8
COARSEST = 3
EDGE_BATCH = 10
GROUP = 4
HELD_PARTS = 2
SPREAD = 16


def stride_of(level):
    return SUB + (0 if level == COARSEST else 2 * 2**level) + (level == 2)


def padded_rows(rows, level):
    return stride_of(level) * (rows + SUB)


def at(row, level):
    return stride_of(level) * row + (0 if level == COARSEST else 2**level)


def lane_iota():
    return lax.broadcasted_iota(jnp.int32, (SUB, LANES), 1)


def sub_iota():
    return lax.broadcasted_iota(jnp.int32, (SUB, LANES), 0)


def tile(ref, field, row, level):
    return ref[field, pl.ds(at(row, level), SUB), :]


def put(ref, field, row, level, value):
    ref[field, pl.ds(at(row, level), SUB), :] = value


def edges(ref, level, first, last):
    if level == COARSEST:
        return
    width, stride, lane = 2**level, stride_of(level), lane_iota()
    places = [(row, field) for row in range(first, last, SUB) for field in range(FIELDS)]
    for part in range(0, len(places), EDGE_BATCH):
        written = []
        for row, field in places[part : part + EDGE_BATCH]:
            rows = lambda sub, row=row, field=field: (
                field, pl.ds(at(row, level) + sub, SUB, stride=stride), slice(None)
            )
            before = jnp.where(lane == 0, 0.0, pltpu.roll(ref[rows(SUB - 1)], 1, 1))
            after = jnp.where(lane == LANES - 1, 0.0, pltpu.roll(ref[rows(0)], LANES - 1, 1))
            written.append((rows, before, after))
        for rows, before, after in written:
            for i in range(width):
                ref[rows(i - width)] = before
                ref[rows(SUB + i)] = after


def rows_loop(first, last, body):
    def step(row, carry):
        body(row)
        return carry

    lax.fori_loop(first, last, step, 0)


def batches(first, last, batch, compute, store):
    def body(index):
        rows = [first + index * batch + i for i in range(batch)]
        results = [compute(row) for row in rows]
        for row, result in zip(rows, results):
            store(row, result)

    rows_loop(0, -(-(last - first) // batch), body)


def neighbours(ref, row, level):
    start, width, stride = at(row, level), 2**level, stride_of(level)
    lane = lane_iota()
    sums, centres = [], []
    for field in range(FIELDS):
        load = lambda first, field=field: ref[field, pl.ds(first, SUB), :]
        centre = load(start)
        if level == COARSEST:
            radial = jnp.where(lane == 0, 0.0, pltpu.roll(centre, 1, 1)) + jnp.where(
                lane == LANES - 1, 0.0, pltpu.roll(centre, LANES - 1, 1)
            )
        else:
            radial = load(start - width) + load(start + width)
        sums.append(radial + (load(start - stride) + load(start + stride)))
        centres.append(centre)
    return sums, centres


def block_times(table, level, row, first, vectors):
    row = TABLE_AT[level] + row
    out = []
    for i in range(FIELDS):
        total = None
        for j in range(FIELDS):
            entry = first + FIELDS * i + j
            term = jnp.broadcast_to(table[entry, pl.ds(row, 1), :], (SUB, LANES)) * vectors[j]
            total = term if total is None else total + term
        out.append(total)
    return out


MATRIX_AT = ENTRIES
TABLE_AT = (0, T0, T0 + T1, T0 + T1 + T2)
TABLE_ROWS = 160
NEAR = 5


def gain_of(level):
    return SOURCE_GAIN * 4.0**level / DIFFUSION


def sweep(source_of, old, new, table, level, first, last, more=True, batch=None):
    gain = gain_of(level)

    def compute(row):
        sums, centres = neighbours(old, row, level)
        rest = [
            (source_of(field, row) + sums[field]) - gain * jnp.tanh(centres[field])
            for field in range(FIELDS)
        ]
        moved = block_times(table, level, row, 0, rest)
        return [(1.0 - RELAXATION) * centres[f] + moved[f] for f in range(FIELDS)]

    def store(row, values):
        for field in range(FIELDS):
            put(new, field, row, level, values[field])

    batches(first, last, batch or SWEEP_BATCH, compute, store)
    if more:
        edges(new, level, first, last)


def residual(source_of, values, table, level, row):
    gain = gain_of(level)
    sums, centres = neighbours(values, row, level)
    applied = block_times(table, level, row, MATRIX_AT, centres)
    left = [
        ((source_of(field, row) + sums[field]) - gain * jnp.tanh(centres[field])) - applied[field]
        for field in range(FIELDS)
    ]
    return left, centres


def pair_sum(value, level):
    width = 2**level
    other = pltpu.roll(value, SUB - width, 0)
    if 2 * width != SUB:
        other = jnp.where((sub_iota() & width) == 0, other, pltpu.roll(value, width, 0))
    return value + other


def coarsen(source_of, values, table, level, row):
    upper_r, upper_v = residual(source_of, values, table, level, 2 * row)
    lower_r, lower_v = residual(source_of, values, table, level, 2 * row + 1)
    coarse = [0.25 * pair_sum(upper_v[f] + lower_v[f], level) for f in range(FIELDS)]
    rest = [pair_sum(upper_r[f] + lower_r[f], level) for f in range(FIELDS)]
    return coarse, rest


def first_sweep(coarse, rest, table, level, row):
    moved = block_times(table, level, row, 0, rest)
    return [coarse[f] + moved[f] for f in range(FIELDS)]


def descend(source_of, values, table, level, c, q, first_values, first, last):
    def compute(row):
        coarse, rest = coarsen(source_of, values, table, level, row)
        return coarse, rest, first_sweep(coarse, rest, table, level + 1, row)

    def store(row, results):
        for field in range(FIELDS):
            put(c, field, row, level + 1, results[0][field])
            q[field, row] = results[1][field]
            put(first_values, field, row, level + 1, results[2][field])

    batches(first, last, COARSEN_BATCH, compute, store)
    edges(c, level + 1, first, last)
    edges(first_values, level + 1, first, last)


def make_source(coarse, rest, source, table, level, first, last):
    gain = gain_of(level)

    def compute(row):
        sums, centres = neighbours(coarse, row, level)
        applied = block_times(table, level, row, MATRIX_AT, centres)
        return [
            (applied[f] - sums[f]) + (gain * jnp.tanh(centres[f]) + rest[f, row])
            for f in range(FIELDS)
        ]

    def store(row, values):
        for field in range(FIELDS):
            source[field, row] = values[field]

    batches(first, last, SWEEP_BATCH, compute, store)


def correct(new, fine, after, before, level, offset, first, last):
    def body(index):
        coarse_row = first // 2 + index + offset
        row = first // 2 * 2 + 2 * index
        for field in range(FIELDS):
            change = tile(after, field, coarse_row, level + 1) - tile(before, field, coarse_row, level + 1)
            put(new, field, row, level, tile(fine, field, row, level) + change)
            put(new, field, row + 1, level, tile(fine, field, row + 1, level) + change)

    rows_loop(0, (last + 1) // 2 - first // 2, body)
    edges(new, level, first, last)


SWEEP_BATCH = 4
INNER = 2
COARSEN_BATCH = 2


def three_parts(value):
    high = value.astype(jnp.bfloat16)
    rest = value - high.astype(jnp.float32)
    middle = rest.astype(jnp.bfloat16)
    low = (rest - middle.astype(jnp.float32)).astype(jnp.bfloat16)
    return high, middle, low


def dot(left, right):
    return jnp.dot(left, right, preferred_element_type=jnp.float32)


def prep_kernel(share, where_ref, coefficients_ref, ids_ref, out, own_coefficients, own_ids, sems):
    device, devices = where_ref[0], where_ref[1]
    copies = [
        pltpu.make_async_copy(coefficients_ref, own_coefficients, sems.at[0]),
        pltpu.make_async_copy(ids_ref, own_ids, sems.at[1]),
    ]
    for copy in copies:
        copy.start()
    out[...] = jnp.zeros_like(out)
    for copy in copies:
        copy.wait()
    for i in range(share):
        out[pl.ds(device * share + i, 1), 0:ENTRIES] = own_coefficients[i : i + 1, :]
    ids = own_ids[...].astype(jnp.float32)
    per_tile = LANES // OWN
    start = pl.multiple_of(devices * share + device // per_tile * SUB, SUB)
    for place in range(per_tile):

        @pl.when(device % per_tile == place)
        def _():
            out[pl.ds(start, SUB), place * OWN : (place + 1) * OWN] = ids


def tables_kernel(regions, where_ref, regions_ref, table, mats, parts):
    device, devices = where_ref[0], where_ref[1]
    wide = 2 * LANES
    lane = lane_iota()
    ids = [jnp.full((SUB, LANES), -1.0, jnp.float32)] * 2
    per_tile = LANES // OWN
    for i in range(NEAR):
        owner = jnp.clip(device + (i - NEAR // 2), 0, devices - 1)
        start = pl.multiple_of(regions + owner // per_tile * SUB, SUB)
        held = regions_ref[pl.ds(start, SUB), :]
        turned = pltpu.roll(held, ((i % per_tile) - owner % per_tile + per_tile) % per_tile * OWN, 1)
        place = i // per_tile
        ids[place] = jnp.where(lane // OWN == i % per_tile, turned, ids[place])
    ids = jnp.concatenate(ids, axis=1).astype(jnp.int32)

    coefficients = jnp.transpose(regions_ref[0:regions, :])[0:32]
    coefficients = jnp.concatenate(three_parts(coefficients), axis=0)
    region = lax.broadcasted_iota(jnp.int32, (regions, wide), 0)
    for block in range(SUB):
        chosen = region == jnp.broadcast_to(ids[block : block + 1], (regions, wide))
        found = dot(coefficients, chosen.astype(jnp.float32).astype(jnp.bfloat16))
        found = (found[0:32] + found[32:64]) + found[64:96]
        for half in range(2):
            mats[half, pl.ds(block, 32, stride=SUB), :] = found[:, half * LANES : (half + 1) * LANES]

    fine = lax.broadcasted_iota(jnp.int32, (wide, wide), 0)
    out = lax.broadcasted_iota(jnp.int32, (wide, wide), 1)
    average = jnp.zeros((wide, wide), jnp.float32)
    own_at = NEAR // 2 * OWN
    for level, (first_own, rows) in enumerate(((O0, T0), (O1, T1), (O2, T2), (O3, T3))):
        span = 2**level
        row = out - TABLE_AT[level]
        same = (row >= 0) & (row < rows) & (fine // span == row + (own_at // span - first_own))
        average = jnp.where(same, 1.0 / span, average)
    average = average.astype(jnp.bfloat16)
    used = SUB * ENTRIES
    high, middle, low = three_parts(jnp.concatenate([mats[0, 0:used], mats[1, 0:used]], axis=1))
    levels = (dot(high, average) + dot(middle, average)) + dot(low, average)

    row = lax.broadcasted_iota(jnp.int32, (SUB, wide), 1)
    weight = jnp.zeros((SUB, wide), jnp.float32) + DIFFUSION
    whole = jnp.zeros((SUB, wide), jnp.int32)
    limit = jnp.zeros((SUB, wide), jnp.int32)
    for level, first_own in enumerate((O0, O1, O2, O3)):
        here = row >= TABLE_AT[level]
        weight = jnp.where(here, DIFFUSION / 4.0**level, weight)
        whole = jnp.where(here, row - TABLE_AT[level] - first_own + device * (OWN >> level), whole)
        limit = jnp.where(here, devices * (OWN >> level), limit)
    inside = (whole >= 0) & (whole < limit)
    scale = jnp.where(inside, RELAXATION * weight, 0.0)
    unscale = 1.0 / weight

    n = FIELDS
    block = [[levels[SUB * (n * i + j) : SUB * (n * i + j + 1)] for j in range(n)] for i in range(n)]
    for i in range(n):
        block[i][i] = block[i][i] + 4.0 * weight
    entries = [block[i][j] * unscale for i in range(n) for j in range(n)]
    right = [[None] * n for _ in range(n)]
    for i in range(n):
        right[i][i] = jnp.ones((SUB, wide), jnp.float32)
    for c in range(n):
        lead = 1.0 / block[c][c]
        for j in range(c + 1, n):
            block[c][j] = block[c][j] * lead
        for j in range(n):
            if right[c][j] is not None:
                right[c][j] = right[c][j] * lead
        for i in range(n):
            if i == c:
                continue
            factor = block[i][c]
            for j in range(c + 1, n):
                block[i][j] = block[i][j] - factor * block[c][j]
            for j in range(n):
                if right[c][j] is not None:
                    term = factor * right[c][j]
                    right[i][j] = -term if right[i][j] is None else right[i][j] - term
    entries = [right[i][j] * scale for i in range(n) for j in range(n)] + entries

    group = FIELDS
    into = lax.broadcasted_iota(jnp.int32, (LANES, group * LANES), 0)
    out = lax.broadcasted_iota(jnp.int32, (LANES, group * LANES), 1)
    same = (into // (3 * SUB) == out // LANES) & (into % SUB == out % LANES // SPREAD)
    widen = same.astype(jnp.float32).astype(jnp.bfloat16)
    parts[...] = jnp.zeros_like(parts)
    for first in range(0, len(entries), group):
        for i in range(group):
            for p, part in enumerate(three_parts(entries[first + i])):
                start = (3 * i + p) * SUB
                parts[start : start + SUB, :] = part.astype(jnp.float32)
        turned = jnp.transpose(parts[...])[0:TABLE_ROWS].astype(jnp.bfloat16)
        wide_rows = dot(turned, widen)
        for i in range(group):
            table[first + i] = wide_rows[:, i * LANES : (i + 1) * LANES]


def turn(first_sub, inward):
    into = lax.broadcasted_iota(jnp.int32, (SUB * LANES, 2 * LANES), 0)
    out = lax.broadcasted_iota(jnp.int32, (1, 2 * LANES), 1)
    if inward:
        wanted = (out % LANES) * SUB + first_sub + out // LANES
    else:
        cell = out + first_sub * LANES
        wanted = (cell % SUB) * LANES + cell // SUB
    return (into == wanted).astype(jnp.float32).astype(jnp.bfloat16)


def split_kernel(where_ref, state_ref, forcing_ref, state_rows, forcing_rows, send_a, send_b, parts, held_in, sems):
    copies = [
        pltpu.make_async_copy(source, held_in.at[i], sems.at[i])
        for i, source in enumerate((state_ref, forcing_ref))
    ]
    for copy in copies:
        copy.start()
    odd = where_ref[0] % 2
    held = 2 * FIELDS * OWN
    for which, copy in enumerate(copies):
        copy.wait()
        for field in range(FIELDS):
            for p, part in enumerate(three_parts(held_in[which, field])[:HELD_PARTS]):
                start = p * held + (which * FIELDS + field) * OWN
                parts[start : start + OWN, :] = part

    def two_subs(index):
        values = dot(parts[...], turn(2 * index, True))
        values = values[:held] + values[held:]
        for which, target in enumerate((state_rows, forcing_rows)):
            for field in range(FIELDS):
                start = (which * FIELDS + field) * OWN
                for half in range(2):
                    target[field, pl.ds(2 * index + half, OWN, stride=SUB), :] = values[
                        start : start + OWN, half * LANES : (half + 1) * LANES
                    ]

    rows_loop(0, SUB // 2, two_subs)
    low, high = 0, (OWN - FINE_HALO) * SUB
    size = FINE_HALO * SUB
    for which, rows in enumerate((state_rows, forcing_rows)):
        for field in range(FIELDS):
            first = rows[field, low : low + size, :]
            last = rows[field, high : high + size, :]
            send_a[which * FIELDS + field] = jnp.where(odd == 1, first, last)
            send_b[which * FIELDS + field] = jnp.where(odd == 1, last, first)


def place_halo(where_ref, buffer, own_rows, got_a, got_b, first, padded):
    odd = where_ref[0] % 2
    row_a = jnp.where(odd == 1, O0 - FINE_HALO, O0 + OWN)
    row_b = jnp.where(odd == 1, O0 + OWN, O0 - FINE_HALO)

    def put_row(field, row, value):
        if padded:
            put(buffer, field, row, 0, value)
        else:
            buffer[field, row] = value

    def own(row):
        start = pl.multiple_of(row * SUB, SUB)
        for field in range(FIELDS):
            put_row(field, O0 + row, own_rows[field, pl.ds(start, SUB), :])

    def halo(row):
        start = pl.multiple_of(row * SUB, SUB)
        for field in range(FIELDS):
            put_row(field, row_a + row, got_a[first + field, pl.ds(start, SUB), :])
            put_row(field, row_b + row, got_b[first + field, pl.ds(start, SUB), :])

    if own_rows is not None:
        rows_loop(0, OWN, own)
    rows_loop(0, FINE_HALO, halo)


def interior_kernel(fresh, where_ref, state, force, table, v0, tmp0, c1, q1, tmp1):
    def own(row):
        start = pl.multiple_of(row * SUB, SUB)
        for field in range(FIELDS):
            put(v0, field, O0 + row, 0, state[field, pl.ds(start, SUB), :])

    rows_loop(0, OWN, own)
    edges(v0, 0, O0, O0 + OWN)
    if fresh:
        source = lambda field, row: force[field, pl.ds(pl.multiple_of((row - O0) * SUB, SUB), SUB), :]
    else:
        source = lambda field, row: force[field, row]
    sweep(source, v0, tmp0, table, 0, O0 + 1, O0 + OWN - 1, batch=5)
    sweep(source, tmp0, v0, table, 0, O0 + 2, O0 + OWN - 2, batch=4)
    descend(source, v0, table, 0, c1, q1, tmp1, O1 + INNER, O1 + OWN // 2 - INNER)


def down_kernel(fresh, *refs):
    half = OWN // 2
    low, high = O0 - FINE_HALO, O0 + OWN + FINE_HALO
    if fresh:
        (where_ref, v0_in, tmp0_in, c1_in, q1_in, tmp1_in, force, got_a, got_b, table,
         v0, v1, s1, c1, send, f0, tmp0, tmp1, q1) = refs
        place_halo(where_ref, f0, force, got_a, got_b, FIELDS, False)
    else:
        (where_ref, v0_in, tmp0_in, c1_in, q1_in, tmp1_in, got_a, got_b, f0, table,
         v0, v1, s1, c1, send, tmp0, tmp1, q1) = refs

    def take(target, source, level, first, last):
        rows = slice(at(first, level) - 2**level, at(last, level) - 2**level)
        target[:, rows, :] = source[:, rows, :]

    take(v0, v0_in, 0, O0, O0 + OWN)
    take(tmp0, tmp0_in, 0, O0 + 1, O0 + 3)
    take(tmp0, tmp0_in, 0, O0 + OWN - 3, O0 + OWN - 1)
    inner = slice(O1 + INNER, O1 + half - INNER)
    take(c1, c1_in, 1, inner.start, inner.stop)
    take(tmp1, tmp1_in, 1, inner.start, inner.stop)
    q1[:, inner] = q1_in[:, inner]
    place_halo(where_ref, v0, None, got_a, got_b, 0, True)
    edges(v0, 0, low, O0)
    edges(v0, 0, O0 + OWN, high)
    fine_source = lambda field, row: f0[field, row]
    for swept, (old, new) in enumerate(((v0, tmp0), (tmp0, v0))):
        for first in (low + swept, O0 + OWN - 1 - swept):
            sweep(fine_source, old, new, table, 0, first, first + FINE_HALO + 1)
    for first in (O1 - 4, O1 + half - INNER):
        descend(fine_source, v0, table, 0, c1, q1, tmp1, first, first + 4 + INNER)
    make_source(c1, q1, s1, table, 1, O1 - 3, O1 + half + 3)
    first_source = lambda field, row: s1[field, row]
    sweep(first_source, tmp1, v1, table, 1, O1 - 3, O1 + half + 3)

    sub = sub_iota()

    def to_second(index):
        coarse, rest = coarsen(first_source, v1, table, 1, index + O1 // 2)
        return coarse + rest

    def pack(index, values):
        group, place = index // GROUP, index % GROUP
        mine = (sub & (GROUP - 1)) == place
        for which in range(2 * FIELDS):
            send[group, which] = jnp.where(mine, values[which], send[group, which])

    send[...] = jnp.zeros_like(send)
    batches(0, OWN // 4, COARSEN_BATCH, to_second, pack)


def spread(source, index, which, place):
    take = lambda sub: jnp.broadcast_to(source[index, which, sub : sub + 1, :], (SUB, LANES))
    return jnp.where(sub_iota() < GROUP, take(place), take(GROUP + place))


def up_kernel(last, *refs):
    if last:
        (where_ref, own, got_a, got_b, got_a2, v0, f0, v1, s1, c1, table, out,
         parts, tmp0, work0, tmp1, work1, c2, q2, s2, v2, tmp2, c3, q3, s3, v3, tmp3) = refs
    else:
        (where_ref, own, got_a, got_b, got_a2, v0, f0, v1, s1, c1, table, out,
         send_a, send_b, tmp0, work0, tmp1, work1, c2, q2, s2, v2, tmp2, c3, q3, s3, v3, tmp3) = refs
    odd = where_ref[0] % 2

    def unpack(source, index, group):
        for place in range(GROUP):
            row = group * GROUP + place
            coarse = [spread(source, index, f, place) for f in range(FIELDS)]
            rest = [spread(source, index, FIELDS + f, place) for f in range(FIELDS)]
            start = first_sweep(coarse, rest, table, 2, row)
            for field in range(FIELDS):
                put(c2, field, row, 2, coarse[field])
                q2[field, row] = rest[field]
                put(tmp2, field, row, 2, start[field])

    pick = lambda a, b: jnp.where(odd == 1, b, a)
    rows_loop(0, 2, lambda i: unpack(own, i, 4 + i))
    rows_loop(0, 2, lambda i: unpack(got_a, i, pick(6, 2) + i))
    rows_loop(0, 3, lambda i: unpack(got_b, i, pick(1, 6) + i))
    rows_loop(0, 1, lambda i: unpack(got_a2, pick(0, 2) + i, pick(8, 1) + i))

    quarter, eighth = OWN // 4, OWN // 8
    for ref in (c2, tmp2):
        edges(ref, 2, O2 - 12, O2 + quarter + 12)
    make_source(c2, q2, s2, table, 2, O2 - 11, O2 + quarter + 11)
    second_source = lambda field, row: s2[field, row]
    sweep(second_source, tmp2, v2, table, 2, O2 - 11, O2 + quarter + 11)

    descend(second_source, v2, table, 2, c3, q3, tmp3, O3 - 5, O3 + eighth + 5)
    make_source(c3, q3, s3, table, 3, O3 - 4, O3 + eighth + 4)
    third_source = lambda field, row: s3[field, row]
    sweep(third_source, tmp3, v3, table, 3, O3 - 4, O3 + eighth + 4)
    sweep(third_source, v3, tmp3, table, 3, O3 - 3, O3 + eighth + 3)
    sweep(third_source, tmp3, v3, table, 3, O3 - 2, O3 + eighth + 2, False)
    correct(v2, v2, v3, c3, 2, 0, O2 - 4, O2 + quarter + 4)
    sweep(second_source, v2, tmp2, table, 2, O2 - 3, O2 + quarter + 3)
    sweep(second_source, tmp2, v2, table, 2, O2 - 2, O2 + quarter + 2, False)

    half = OWN // 2
    first_source = lambda field, row: s1[field, row]
    correct(work1, v1, v2, c2, 1, O2 - O1 // 2, O1 - 3, O1 + half + 3)
    sweep(first_source, work1, tmp1, table, 1, O1 - 2, O1 + half + 2)
    sweep(first_source, tmp1, work1, table, 1, O1 - 1, O1 + half + 1, False)

    fine_source = lambda field, row: f0[field, row]
    correct(work0, v0, work1, c1, 0, 0, O0 - 2, O0 + OWN + 2)
    sweep(fine_source, work0, tmp0, table, 0, O0 - 1, O0 + OWN + 1)
    sweep(fine_source, tmp0, work0, table, 0, O0, O0 + OWN, False)

    if last:
        held = FIELDS * OWN
        for field in range(FIELDS):
            for sub in range(SUB):
                value = work0[field, pl.ds(at(O0, 0) + sub, OWN, stride=stride_of(0)), :]
                for p, part in enumerate(three_parts(value)[:HELD_PARTS]):
                    start = p * held + field * OWN
                    parts[start : start + OWN, sub * LANES : (sub + 1) * LANES] = part

        def columns_out(index):
            values = dot(parts[...], turn(2 * index, False))
            values = values[:held] + values[held:]
            cells = pl.ds(pl.multiple_of(index * 2 * LANES, 2 * LANES), 2 * LANES)
            for field in range(FIELDS):
                out[field, :, cells] = values[field * OWN : (field + 1) * OWN]

        rows_loop(0, SUB // 2, columns_out)
        return

    def leave(row):
        start = pl.multiple_of(row * SUB, SUB)
        for field in range(FIELDS):
            out[field, pl.ds(start, SUB), :] = tile(work0, field, O0 + row, 0)

    rows_loop(0, OWN, leave)
    from_a, from_b = pick(OWN - FINE_HALO, 0), pick(0, OWN - FINE_HALO)

    def edge(row):
        start = pl.multiple_of(row * SUB, SUB)
        for field in range(FIELDS):
            send_a[field, pl.ds(start, SUB), :] = tile(work0, field, O0 + from_a + row, 0)
            send_b[field, pl.ds(start, SUB), :] = tile(work0, field, O0 + from_b + row, 0)

    rows_loop(0, FINE_HALO, edge)


def relay_kernel(where_ref, own, beside, row):
    odd = where_ref[0] % 2
    row[odd] = own[0]
    row[odd + 1] = own[1]
    row[2 - 2 * odd] = beside[odd]


VMEM = pl.BlockSpec(memory_space=pltpu.VMEM)
SMEM = pl.BlockSpec(memory_space=pltpu.SMEM)
HBM = pl.BlockSpec(memory_space=pltpu.HBM)


def f32(*shape):
    return jax.ShapeDtypeStruct(shape, jnp.float32)


def scratch(*shape):
    return pltpu.VMEM(shape, jnp.float32)


def padded(rows, level):
    return (FIELDS, padded_rows(rows, level), LANES)


def plain(rows):
    return (FIELDS, rows, SUB, LANES)


def call(kernel, grant, outs, operands, scratches=(), raw=()):
    return pl.pallas_call(
        kernel,
        out_shape=outs,
        in_specs=[SMEM] + [HBM if i in raw else VMEM for i in range(1, len(operands))],
        out_specs=[VMEM] * len(outs),
        scratch_shapes=list(scratches),
        compiler_params=pltpu.CompilerParams(vmem_limit_bytes=grant * 1024 * 1024),
    )(*operands)


def in_hbm(array):
    return pltpu.with_memory_space_constraint(array, pltpu.HBM)


def per_device(initial_state, forcing, coefficients, region_ids):
    size = lax.axis_size("axial")
    device = lax.axis_index("axial")
    assert initial_state.shape == (FIELDS, OWN, SUB * LANES)
    assert region_ids.shape == (OWN, SUB)
    where_ref = jnp.stack([device, jnp.int32(size)]).astype(jnp.int32)
    pair_a = [(i, i ^ 1) for i in range(size)]
    pair_b = [(i, i + 1 if i % 2 else i - 1) for i in range(1, size - 1)]
    swap_a = lambda x: lax.ppermute(x, "axial", pair_a)
    swap_b = lambda x: lax.ppermute(x, "axial", pair_b)

    share = coefficients.shape[1]
    regions = share * size
    per_tile = LANES // OWN
    (gathered,) = call(
        functools.partial(prep_kernel, share),
        4,
        [f32(regions + SUB * -(-size // per_tile), LANES)],
        [where_ref, in_hbm(coefficients.T), in_hbm(region_ids.T)],
        [
            scratch(share, ENTRIES),
            pltpu.VMEM((SUB, OWN), jnp.int32),
            pltpu.SemaphoreType.DMA((2,)),
        ],
        (1, 2),
    )

    def doubled(held, step):
        return held + lax.ppermute(held, "axial", [(i, i ^ step) for i in range(size)])

    state, force, send_a, send_b = call(
        split_kernel,
        12,
        [f32(FIELDS, OWN * SUB, LANES)] * 2 + [f32(2 * FIELDS, FINE_HALO * SUB, LANES)] * 2,
        [where_ref, in_hbm(initial_state), in_hbm(forcing)],
        [
            pltpu.VMEM((HELD_PARTS * 2 * FIELDS * OWN, SUB * LANES), jnp.bfloat16),
            scratch(2, FIELDS, OWN, SUB * LANES),
            pltpu.SemaphoreType.DMA((2,)),
        ],
        (1, 2),
    )
    step = 1
    while step < min(size, 8):
        gathered = doubled(gathered, step)
        step *= 2
    gathered, send_a, send_b = lax.optimization_barrier((gathered, send_a, send_b))
    got_b, got_a = swap_b(send_b), swap_a(send_a)
    while step < size:
        gathered = doubled(gathered, step)
        step *= 2
    (table,) = call(
        functools.partial(tables_kernel, regions),
        12,
        [f32(2 * ENTRIES, TABLE_ROWS, LANES)],
        [where_ref, gathered],
        [scratch(2, 32 * SUB, LANES), scratch(LANES, 2 * LANES)],
    )

    f0 = None
    for cycle in range(CYCLES):
        outs = [f32(*padded(T0, 0)), f32(*padded(T1, 1)), f32(*plain(T1)), f32(*padded(T1, 1)),
                f32(2, 2 * FIELDS, SUB, LANES)]
        temps = [scratch(*padded(T0, 0)), scratch(*padded(T1, 1)), scratch(*plain(T1))]
        fresh = cycle == 0
        inner = call(
            functools.partial(interior_kernel, fresh), 4,
            [f32(*padded(T0, 0))] * 2 + [f32(*padded(T1, 1)), f32(*plain(T1)), f32(*padded(T1, 1))],
            [where_ref, state, force if fresh else f0, table],
        )
        if fresh:
            v0, v1, s1, c1, own, f0 = call(
                functools.partial(down_kernel, True), 14, outs + [f32(*plain(T0))],
                [where_ref, *inner, force, got_a, got_b, table], temps,
            )
        else:
            v0, v1, s1, c1, own = call(
                functools.partial(down_kernel, False), 14, outs,
                [where_ref, *inner, got_a, got_b, f0, table], temps,
            )
        beside = swap_a(own)
        (row,) = call(relay_kernel, 2, [f32(3, 2 * FIELDS, SUB, LANES)], [where_ref, own, beside])
        far = swap_b(row)
        beyond = swap_a(far)
        operands = [where_ref, own, beside, far, beyond, v0, f0, v1, s1, c1, table]
        temps = [scratch(*padded(T0, 0))] * 2 + [scratch(*padded(T1, 1))] * 2
        temps += [scratch(*padded(T2, 2)), scratch(*plain(T2)), scratch(*plain(T2)), scratch(*padded(T2, 2)), scratch(*padded(T2, 2))]
        temps += [scratch(*padded(T3, 3)), scratch(*plain(T3)), scratch(*plain(T3)), scratch(*padded(T3, 3)), scratch(*padded(T3, 3))]
        if cycle == CYCLES - 1:
            return call(
                functools.partial(up_kernel, True), 26,
                [f32(FIELDS, OWN, SUB * LANES)], operands,
                [pltpu.VMEM((HELD_PARTS * FIELDS * OWN, SUB * LANES), jnp.bfloat16)] + temps,
            )[0]
        state, send_a, send_b = call(
            functools.partial(up_kernel, False), 26,
            [f32(FIELDS, OWN * SUB, LANES)] + [f32(FIELDS, FINE_HALO * SUB, LANES)] * 2,
            operands, temps,
        )
        got_b, got_a = swap_b(send_b), swap_a(send_a)


def solution(mesh):
    placed = (
        P("sample", "axial", None),
        P("sample", "axial", None),
        P("sample", "axial"),
        P("axial", None),
    )
    return jax.shard_map(
        per_device,
        mesh=mesh,
        in_specs=placed,
        out_specs=P("sample", "axial", None),
        check_vma=False,
    )
```

```python
import functools

import jax
import jax.numpy as jnp
from jax import lax
from jax.experimental import pallas as pl
from jax.experimental.pallas import tpu as pltpu
from jax.sharding import PartitionSpec as P

DIFFUSION = 1.0
RELAXATION = 0.8
SOURCE_GAIN = 0.05
CYCLES = 2

FIELDS = 5
ENTRIES = FIELDS * FIELDS
SUB, LANES = 8, 128

OWN = 32
FINE_HALO = 11
T0, O0 = 64, 16
T1, O1 = 32, 8
T2, O2 = 40, 16
T3, O3 = 20, 8
COARSEST = 3
EDGE_BATCH = 10
GROUP = 4
HELD_PARTS = 2
SPREAD = 16


def stride_of(level):
    return SUB + (0 if level == COARSEST else 2 * 2**level) + (level == 2)


def padded_rows(rows, level):
    return stride_of(level) * (rows + SUB)


def at(row, level):
    return stride_of(level) * row + (0 if level == COARSEST else 2**level)


def lane_iota():
    return lax.broadcasted_iota(jnp.int32, (SUB, LANES), 1)


def sub_iota():
    return lax.broadcasted_iota(jnp.int32, (SUB, LANES), 0)


def tile(ref, field, row, level):
    return ref[field, pl.ds(at(row, level), SUB), :]


def put(ref, field, row, level, value):
    ref[field, pl.ds(at(row, level), SUB), :] = value


def edges(ref, level, first, last):
    if level == COARSEST:
        return
    width, stride, lane = 2**level, stride_of(level), lane_iota()
    places = [(row, field) for row in range(first, last, SUB) for field in range(FIELDS)]
    for part in range(0, len(places), EDGE_BATCH):
        written = []
        for row, field in places[part : part + EDGE_BATCH]:
            rows = lambda sub, row=row, field=field: (
                field, pl.ds(at(row, level) + sub, SUB, stride=stride), slice(None)
            )
            before = jnp.where(lane == 0, 0.0, pltpu.roll(ref[rows(SUB - 1)], 1, 1))
            after = jnp.where(lane == LANES - 1, 0.0, pltpu.roll(ref[rows(0)], LANES - 1, 1))
            written.append((rows, before, after))
        for rows, before, after in written:
            for i in range(width):
                ref[rows(i - width)] = before
                ref[rows(SUB + i)] = after


def rows_loop(first, last, body):
    def step(row, carry):
        body(row)
        return carry

    lax.fori_loop(first, last, step, 0)


def batches(first, last, batch, compute, store):
    def body(index):
        rows = [first + index * batch + i for i in range(batch)]
        results = [compute(row) for row in rows]
        for row, result in zip(rows, results):
            store(row, result)

    rows_loop(0, -(-(last - first) // batch), body)


def neighbours(ref, row, level):
    start, width, stride = at(row, level), 2**level, stride_of(level)
    lane = lane_iota()
    sums, centres = [], []
    for field in range(FIELDS):
        load = lambda first, field=field: ref[field, pl.ds(first, SUB), :]
        centre = load(start)
        if level == COARSEST:
            radial = jnp.where(lane == 0, 0.0, pltpu.roll(centre, 1, 1)) + jnp.where(
                lane == LANES - 1, 0.0, pltpu.roll(centre, LANES - 1, 1)
            )
        else:
            radial = load(start - width) + load(start + width)
        sums.append(radial + (load(start - stride) + load(start + stride)))
        centres.append(centre)
    return sums, centres


def block_times(table, level, row, first, vectors):
    row = TABLE_AT[level] + row
    out = []
    for i in range(FIELDS):
        total = None
        for j in range(FIELDS):
            entry = first + FIELDS * i + j
            term = jnp.broadcast_to(table[entry, pl.ds(row, 1), :], (SUB, LANES)) * vectors[j]
            total = term if total is None else total + term
        out.append(total)
    return out


MATRIX_AT = ENTRIES
TABLE_AT = (0, T0, T0 + T1, T0 + T1 + T2)
TABLE_ROWS = 160
NEAR = 5


def gain_of(level):
    return SOURCE_GAIN * 4.0**level / DIFFUSION


def sweep(source_of, old, new, table, level, first, last, more=True, batch=None):
    gain = gain_of(level)

    def compute(row):
        sums, centres = neighbours(old, row, level)
        rest = [
            (source_of(field, row) + sums[field]) - gain * jnp.tanh(centres[field])
            for field in range(FIELDS)
        ]
        moved = block_times(table, level, row, 0, rest)
        return [(1.0 - RELAXATION) * centres[f] + moved[f] for f in range(FIELDS)]

    def store(row, values):
        for field in range(FIELDS):
            put(new, field, row, level, values[field])

    batches(first, last, batch or SWEEP_BATCH, compute, store)
    if more:
        edges(new, level, first, last)


def residual(source_of, values, table, level, row):
    gain = gain_of(level)
    sums, centres = neighbours(values, row, level)
    applied = block_times(table, level, row, MATRIX_AT, centres)
    left = [
        ((source_of(field, row) + sums[field]) - gain * jnp.tanh(centres[field])) - applied[field]
        for field in range(FIELDS)
    ]
    return left, centres


def pair_sum(value, level):
    width = 2**level
    other = pltpu.roll(value, SUB - width, 0)
    if 2 * width != SUB:
        other = jnp.where((sub_iota() & width) == 0, other, pltpu.roll(value, width, 0))
    return value + other


def coarsen(source_of, values, table, level, row):
    upper_r, upper_v = residual(source_of, values, table, level, 2 * row)
    lower_r, lower_v = residual(source_of, values, table, level, 2 * row + 1)
    coarse = [0.25 * pair_sum(upper_v[f] + lower_v[f], level) for f in range(FIELDS)]
    rest = [pair_sum(upper_r[f] + lower_r[f], level) for f in range(FIELDS)]
    return coarse, rest


def first_sweep(coarse, rest, table, level, row):
    moved = block_times(table, level, row, 0, rest)
    return [coarse[f] + moved[f] for f in range(FIELDS)]


def descend(source_of, values, table, level, c, q, first_values, first, last):
    def compute(row):
        coarse, rest = coarsen(source_of, values, table, level, row)
        return coarse, rest, first_sweep(coarse, rest, table, level + 1, row)

    def store(row, results):
        for field in range(FIELDS):
            put(c, field, row, level + 1, results[0][field])
            q[field, row] = results[1][field]
            put(first_values, field, row, level + 1, results[2][field])

    batches(first, last, COARSEN_BATCH, compute, store)
    edges(c, level + 1, first, last)
    edges(first_values, level + 1, first, last)


def make_source(coarse, rest, source, table, level, first, last):
    gain = gain_of(level)

    def compute(row):
        sums, centres = neighbours(coarse, row, level)
        applied = block_times(table, level, row, MATRIX_AT, centres)
        return [
            (applied[f] - sums[f]) + (gain * jnp.tanh(centres[f]) + rest[f, row])
            for f in range(FIELDS)
        ]

    def store(row, values):
        for field in range(FIELDS):
            source[field, row] = values[field]

    batches(first, last, SWEEP_BATCH, compute, store)


def correct(new, fine, after, before, level, offset, first, last):
    def body(index):
        coarse_row = first // 2 + index + offset
        row = first // 2 * 2 + 2 * index
        for field in range(FIELDS):
            change = tile(after, field, coarse_row, level + 1) - tile(before, field, coarse_row, level + 1)
            put(new, field, row, level, tile(fine, field, row, level) + change)
            put(new, field, row + 1, level, tile(fine, field, row + 1, level) + change)

    rows_loop(0, (last + 1) // 2 - first // 2, body)
    edges(new, level, first, last)


SWEEP_BATCH = 4
INNER = 2
COARSEN_BATCH = 2


def three_parts(value):
    high = value.astype(jnp.bfloat16)
    rest = value - high.astype(jnp.float32)
    middle = rest.astype(jnp.bfloat16)
    low = (rest - middle.astype(jnp.float32)).astype(jnp.bfloat16)
    return high, middle, low


def dot(left, right):
    return jnp.dot(left, right, preferred_element_type=jnp.float32)


def prep_kernel(share, where_ref, coefficients_ref, ids_ref, out, own_coefficients, own_ids, sems):
    device, devices = where_ref[0], where_ref[1]
    copies = [
        pltpu.make_async_copy(coefficients_ref, own_coefficients, sems.at[0]),
        pltpu.make_async_copy(ids_ref, own_ids, sems.at[1]),
    ]
    for copy in copies:
        copy.start()
    out[...] = jnp.zeros_like(out)
    for copy in copies:
        copy.wait()
    for i in range(share):
        out[pl.ds(device * share + i, 1), 0:ENTRIES] = own_coefficients[i : i + 1, :]
    ids = own_ids[...].astype(jnp.float32)
    per_tile = LANES // OWN
    start = pl.multiple_of(devices * share + device // per_tile * SUB, SUB)
    for place in range(per_tile):

        @pl.when(device % per_tile == place)
        def _():
            out[pl.ds(start, SUB), place * OWN : (place + 1) * OWN] = ids


def tables_kernel(regions, where_ref, regions_ref, table, mats, parts):
    device, devices = where_ref[0], where_ref[1]
    wide = 2 * LANES
    lane = lane_iota()
    ids = [jnp.full((SUB, LANES), -1.0, jnp.float32)] * 2
    per_tile = LANES // OWN
    for i in range(NEAR):
        owner = jnp.clip(device + (i - NEAR // 2), 0, devices - 1)
        start = pl.multiple_of(regions + owner // per_tile * SUB, SUB)
        held = regions_ref[pl.ds(start, SUB), :]
        turned = pltpu.roll(held, ((i % per_tile) - owner % per_tile + per_tile) % per_tile * OWN, 1)
        place = i // per_tile
        ids[place] = jnp.where(lane // OWN == i % per_tile, turned, ids[place])
    ids = jnp.concatenate(ids, axis=1).astype(jnp.int32)

    coefficients = jnp.transpose(regions_ref[0:regions, :])[0:32]
    coefficients = jnp.concatenate(three_parts(coefficients), axis=0)
    region = lax.broadcasted_iota(jnp.int32, (regions, wide), 0)
    for block in range(SUB):
        chosen = region == jnp.broadcast_to(ids[block : block + 1], (regions, wide))
        found = dot(coefficients, chosen.astype(jnp.float32).astype(jnp.bfloat16))
        found = (found[0:32] + found[32:64]) + found[64:96]
        for half in range(2):
            mats[half, pl.ds(block, 32, stride=SUB), :] = found[:, half * LANES : (half + 1) * LANES]

    fine = lax.broadcasted_iota(jnp.int32, (wide, wide), 0)
    out = lax.broadcasted_iota(jnp.int32, (wide, wide), 1)
    average = jnp.zeros((wide, wide), jnp.float32)
    own_at = NEAR // 2 * OWN
    for level, (first_own, rows) in enumerate(((O0, T0), (O1, T1), (O2, T2), (O3, T3))):
        span = 2**level
        row = out - TABLE_AT[level]
        same = (row >= 0) & (row < rows) & (fine // span == row + (own_at // span - first_own))
        average = jnp.where(same, 1.0 / span, average)
    average = average.astype(jnp.bfloat16)
    used = SUB * ENTRIES
    high, middle, low = three_parts(jnp.concatenate([mats[0, 0:used], mats[1, 0:used]], axis=1))
    levels = (dot(high, average) + dot(middle, average)) + dot(low, average)

    row = lax.broadcasted_iota(jnp.int32, (SUB, wide), 1)
    weight = jnp.zeros((SUB, wide), jnp.float32) + DIFFUSION
    whole = jnp.zeros((SUB, wide), jnp.int32)
    limit = jnp.zeros((SUB, wide), jnp.int32)
    for level, first_own in enumerate((O0, O1, O2, O3)):
        here = row >= TABLE_AT[level]
        weight = jnp.where(here, DIFFUSION / 4.0**level, weight)
        whole = jnp.where(here, row - TABLE_AT[level] - first_own + device * (OWN >> level), whole)
        limit = jnp.where(here, devices * (OWN >> level), limit)
    inside = (whole >= 0) & (whole < limit)
    scale = jnp.where(inside, RELAXATION * weight, 0.0)
    unscale = 1.0 / weight

    n = FIELDS
    block = [[levels[SUB * (n * i + j) : SUB * (n * i + j + 1)] for j in range(n)] for i in range(n)]
    for i in range(n):
        block[i][i] = block[i][i] + 4.0 * weight
    entries = [block[i][j] * unscale for i in range(n) for j in range(n)]
    right = [[None] * n for _ in range(n)]
    for i in range(n):
        right[i][i] = jnp.ones((SUB, wide), jnp.float32)
    for c in range(n):
        lead = 1.0 / block[c][c]
        for j in range(c + 1, n):
            block[c][j] = block[c][j] * lead
        for j in range(n):
            if right[c][j] is not None:
                right[c][j] = right[c][j] * lead
        for i in range(n):
            if i == c:
                continue
            factor = block[i][c]
            for j in range(c + 1, n):
                block[i][j] = block[i][j] - factor * block[c][j]
            for j in range(n):
                if right[c][j] is not None:
                    term = factor * right[c][j]
                    right[i][j] = -term if right[i][j] is None else right[i][j] - term
    entries = [right[i][j] * scale for i in range(n) for j in range(n)] + entries

    group = FIELDS
    into = lax.broadcasted_iota(jnp.int32, (LANES, group * LANES), 0)
    out = lax.broadcasted_iota(jnp.int32, (LANES, group * LANES), 1)
    same = (into // (3 * SUB) == out // LANES) & (into % SUB == out % LANES // SPREAD)
    widen = same.astype(jnp.float32).astype(jnp.bfloat16)
    parts[...] = jnp.zeros_like(parts)
    for first in range(0, len(entries), group):
        for i in range(group):
            for p, part in enumerate(three_parts(entries[first + i])):
                start = (3 * i + p) * SUB
                parts[start : start + SUB, :] = part.astype(jnp.float32)
        turned = jnp.transpose(parts[...])[0:TABLE_ROWS].astype(jnp.bfloat16)
        wide_rows = dot(turned, widen)
        for i in range(group):
            table[first + i] = wide_rows[:, i * LANES : (i + 1) * LANES]


def turn(first_sub, inward):
    into = lax.broadcasted_iota(jnp.int32, (SUB * LANES, 2 * LANES), 0)
    out = lax.broadcasted_iota(jnp.int32, (1, 2 * LANES), 1)
    if inward:
        wanted = (out % LANES) * SUB + first_sub + out // LANES
    else:
        cell = out + first_sub * LANES
        wanted = (cell % SUB) * LANES + cell // SUB
    return (into == wanted).astype(jnp.float32).astype(jnp.bfloat16)


def split_kernel(where_ref, state_ref, forcing_ref, state_rows, forcing_rows, send_a, send_b, parts, held_in, sems):
    copies = [
        pltpu.make_async_copy(source, held_in.at[i], sems.at[i])
        for i, source in enumerate((state_ref, forcing_ref))
    ]
    for copy in copies:
        copy.start()
    odd = where_ref[0] % 2
    held = 2 * FIELDS * OWN
    for which, copy in enumerate(copies):
        copy.wait()
        for field in range(FIELDS):
            for p, part in enumerate(three_parts(held_in[which, field])[:HELD_PARTS]):
                start = p * held + (which * FIELDS + field) * OWN
                parts[start : start + OWN, :] = part

    def two_subs(index):
        values = dot(parts[...], turn(2 * index, True))
        values = values[:held] + values[held:]
        for which, target in enumerate((state_rows, forcing_rows)):
            for field in range(FIELDS):
                start = (which * FIELDS + field) * OWN
                for half in range(2):
                    target[field, pl.ds(2 * index + half, OWN, stride=SUB), :] = values[
                        start : start + OWN, half * LANES : (half + 1) * LANES
                    ]

    rows_loop(0, SUB // 2, two_subs)
    low, high = 0, (OWN - FINE_HALO) * SUB
    size = FINE_HALO * SUB
    for which, rows in enumerate((state_rows, forcing_rows)):
        for field in range(FIELDS):
            first = rows[field, low : low + size, :]
            last = rows[field, high : high + size, :]
            send_a[which * FIELDS + field] = jnp.where(odd == 1, first, last)
            send_b[which * FIELDS + field] = jnp.where(odd == 1, last, first)


def place_halo(where_ref, buffer, own_rows, got_a, got_b, first, padded):
    odd = where_ref[0] % 2
    row_a = jnp.where(odd == 1, O0 - FINE_HALO, O0 + OWN)
    row_b = jnp.where(odd == 1, O0 + OWN, O0 - FINE_HALO)

    def put_row(field, row, value):
        if padded:
            put(buffer, field, row, 0, value)
        else:
            buffer[field, row] = value

    def own(row):
        start = pl.multiple_of(row * SUB, SUB)
        for field in range(FIELDS):
            put_row(field, O0 + row, own_rows[field, pl.ds(start, SUB), :])

    def halo(row):
        start = pl.multiple_of(row * SUB, SUB)
        for field in range(FIELDS):
            put_row(field, row_a + row, got_a[first + field, pl.ds(start, SUB), :])
            put_row(field, row_b + row, got_b[first + field, pl.ds(start, SUB), :])

    if own_rows is not None:
        rows_loop(0, OWN, own)
    rows_loop(0, FINE_HALO, halo)


def interior_kernel(where_ref, state, f0, table, v0, tmp0, c1, q1, tmp1):
    def own(row):
        start = pl.multiple_of(row * SUB, SUB)
        for field in range(FIELDS):
            put(v0, field, O0 + row, 0, state[field, pl.ds(start, SUB), :])

    rows_loop(0, OWN, own)
    edges(v0, 0, O0, O0 + OWN)
    source = lambda field, row: f0[field, row]
    sweep(source, v0, tmp0, table, 0, O0 + 1, O0 + OWN - 1, batch=5)
    sweep(source, tmp0, v0, table, 0, O0 + 2, O0 + OWN - 2, batch=4)
    descend(source, v0, table, 0, c1, q1, tmp1, O1 + INNER, O1 + OWN // 2 - INNER)


def down_kernel(fresh, *refs):
    half = OWN // 2
    low, high = O0 - FINE_HALO, O0 + OWN + FINE_HALO
    if fresh:
        where_ref, state, force, got_a, got_b, table, v0, v1, s1, c1, send, f0, tmp0, tmp1, q1 = refs
        place_halo(where_ref, v0, state, got_a, got_b, 0, True)
        edges(v0, 0, low, high)
        place_halo(where_ref, f0, force, got_a, got_b, FIELDS, False)
    else:
        (where_ref, v0_in, tmp0_in, c1_in, q1_in, tmp1_in, got_a, got_b, f0, table,
         v0, v1, s1, c1, send, tmp0, tmp1, q1) = refs

        def take(target, source, level, first, last):
            rows = slice(at(first, level) - 2**level, at(last, level) - 2**level)
            target[:, rows, :] = source[:, rows, :]

        take(v0, v0_in, 0, O0, O0 + OWN)
        take(tmp0, tmp0_in, 0, O0 + 1, O0 + 3)
        take(tmp0, tmp0_in, 0, O0 + OWN - 3, O0 + OWN - 1)
        inner = slice(O1 + INNER, O1 + half - INNER)
        take(c1, c1_in, 1, inner.start, inner.stop)
        take(tmp1, tmp1_in, 1, inner.start, inner.stop)
        q1[:, inner] = q1_in[:, inner]
        place_halo(where_ref, v0, None, got_a, got_b, 0, True)
        edges(v0, 0, low, O0)
        edges(v0, 0, O0 + OWN, high)
    fine_source = lambda field, row: f0[field, row]
    if fresh:
        sweep(fine_source, v0, tmp0, table, 0, low + 1, high - 1)
        sweep(fine_source, tmp0, v0, table, 0, low + 2, high - 2)
        descend(fine_source, v0, table, 0, c1, q1, tmp1, O1 - 4, O1 + half + 4)
    else:
        for swept, (old, new) in enumerate(((v0, tmp0), (tmp0, v0))):
            for first in (low + swept, O0 + OWN - 1 - swept):
                sweep(fine_source, old, new, table, 0, first, first + FINE_HALO + 1)
        for first in (O1 - 4, O1 + half - INNER):
            descend(fine_source, v0, table, 0, c1, q1, tmp1, first, first + 4 + INNER)
    make_source(c1, q1, s1, table, 1, O1 - 3, O1 + half + 3)
    first_source = lambda field, row: s1[field, row]
    sweep(first_source, tmp1, v1, table, 1, O1 - 3, O1 + half + 3)

    sub = sub_iota()

    def to_second(index):
        coarse, rest = coarsen(first_source, v1, table, 1, index + O1 // 2)
        return coarse + rest

    def pack(index, values):
        group, place = index // GROUP, index % GROUP
        mine = (sub & (GROUP - 1)) == place
        for which in range(2 * FIELDS):
            send[group, which] = jnp.where(mine, values[which], send[group, which])

    send[...] = jnp.zeros_like(send)
    batches(0, OWN // 4, COARSEN_BATCH, to_second, pack)


def spread(source, index, which, place):
    take = lambda sub: jnp.broadcast_to(source[index, which, sub : sub + 1, :], (SUB, LANES))
    return jnp.where(sub_iota() < GROUP, take(place), take(GROUP + place))


def up_kernel(last, *refs):
    if last:
        (where_ref, own, got_a, got_b, got_a2, v0, f0, v1, s1, c1, table, out,
         parts, tmp0, work0, tmp1, work1, c2, q2, s2, v2, tmp2, c3, q3, s3, v3, tmp3) = refs
    else:
        (where_ref, own, got_a, got_b, got_a2, v0, f0, v1, s1, c1, table, out,
         send_a, send_b, tmp0, work0, tmp1, work1, c2, q2, s2, v2, tmp2, c3, q3, s3, v3, tmp3) = refs
    odd = where_ref[0] % 2

    def unpack(source, index, group):
        for place in range(GROUP):
            row = group * GROUP + place
            coarse = [spread(source, index, f, place) for f in range(FIELDS)]
            rest = [spread(source, index, FIELDS + f, place) for f in range(FIELDS)]
            start = first_sweep(coarse, rest, table, 2, row)
            for field in range(FIELDS):
                put(c2, field, row, 2, coarse[field])
                q2[field, row] = rest[field]
                put(tmp2, field, row, 2, start[field])

    pick = lambda a, b: jnp.where(odd == 1, b, a)
    rows_loop(0, 2, lambda i: unpack(own, i, 4 + i))
    rows_loop(0, 2, lambda i: unpack(got_a, i, pick(6, 2) + i))
    rows_loop(0, 3, lambda i: unpack(got_b, i, pick(1, 6) + i))
    rows_loop(0, 1, lambda i: unpack(got_a2, pick(0, 2) + i, pick(8, 1) + i))

    quarter, eighth = OWN // 4, OWN // 8
    for ref in (c2, tmp2):
        edges(ref, 2, O2 - 12, O2 + quarter + 12)
    make_source(c2, q2, s2, table, 2, O2 - 11, O2 + quarter + 11)
    second_source = lambda field, row: s2[field, row]
    sweep(second_source, tmp2, v2, table, 2, O2 - 11, O2 + quarter + 11)

    descend(second_source, v2, table, 2, c3, q3, tmp3, O3 - 5, O3 + eighth + 5)
    make_source(c3, q3, s3, table, 3, O3 - 4, O3 + eighth + 4)
    third_source = lambda field, row: s3[field, row]
    sweep(third_source, tmp3, v3, table, 3, O3 - 4, O3 + eighth + 4)
    sweep(third_source, v3, tmp3, table, 3, O3 - 3, O3 + eighth + 3)
    sweep(third_source, tmp3, v3, table, 3, O3 - 2, O3 + eighth + 2, False)
    correct(v2, v2, v3, c3, 2, 0, O2 - 4, O2 + quarter + 4)
    sweep(second_source, v2, tmp2, table, 2, O2 - 3, O2 + quarter + 3)
    sweep(second_source, tmp2, v2, table, 2, O2 - 2, O2 + quarter + 2, False)

    half = OWN // 2
    first_source = lambda field, row: s1[field, row]
    correct(work1, v1, v2, c2, 1, O2 - O1 // 2, O1 - 3, O1 + half + 3)
    sweep(first_source, work1, tmp1, table, 1, O1 - 2, O1 + half + 2)
    sweep(first_source, tmp1, work1, table, 1, O1 - 1, O1 + half + 1, False)

    fine_source = lambda field, row: f0[field, row]
    correct(work0, v0, work1, c1, 0, 0, O0 - 2, O0 + OWN + 2)
    sweep(fine_source, work0, tmp0, table, 0, O0 - 1, O0 + OWN + 1)
    sweep(fine_source, tmp0, work0, table, 0, O0, O0 + OWN, False)

    if last:
        held = FIELDS * OWN
        for field in range(FIELDS):
            for sub in range(SUB):
                value = work0[field, pl.ds(at(O0, 0) + sub, OWN, stride=stride_of(0)), :]
                for p, part in enumerate(three_parts(value)[:HELD_PARTS]):
                    start = p * held + field * OWN
                    parts[start : start + OWN, sub * LANES : (sub + 1) * LANES] = part

        def columns_out(index):
            values = dot(parts[...], turn(2 * index, False))
            values = values[:held] + values[held:]
            cells = pl.ds(pl.multiple_of(index * 2 * LANES, 2 * LANES), 2 * LANES)
            for field in range(FIELDS):
                out[field, :, cells] = values[field * OWN : (field + 1) * OWN]

        rows_loop(0, SUB // 2, columns_out)
        return

    def leave(row):
        start = pl.multiple_of(row * SUB, SUB)
        for field in range(FIELDS):
            out[field, pl.ds(start, SUB), :] = tile(work0, field, O0 + row, 0)

    rows_loop(0, OWN, leave)
    from_a, from_b = pick(OWN - FINE_HALO, 0), pick(0, OWN - FINE_HALO)

    def edge(row):
        start = pl.multiple_of(row * SUB, SUB)
        for field in range(FIELDS):
            send_a[field, pl.ds(start, SUB), :] = tile(work0, field, O0 + from_a + row, 0)
            send_b[field, pl.ds(start, SUB), :] = tile(work0, field, O0 + from_b + row, 0)

    rows_loop(0, FINE_HALO, edge)


def relay_kernel(where_ref, own, beside, row):
    odd = where_ref[0] % 2
    row[odd] = own[0]
    row[odd + 1] = own[1]
    row[2 - 2 * odd] = beside[odd]


VMEM = pl.BlockSpec(memory_space=pltpu.VMEM)
SMEM = pl.BlockSpec(memory_space=pltpu.SMEM)
HBM = pl.BlockSpec(memory_space=pltpu.HBM)


def f32(*shape):
    return jax.ShapeDtypeStruct(shape, jnp.float32)


def scratch(*shape):
    return pltpu.VMEM(shape, jnp.float32)


def padded(rows, level):
    return (FIELDS, padded_rows(rows, level), LANES)


def plain(rows):
    return (FIELDS, rows, SUB, LANES)


def call(kernel, name, grant, outs, operands, scratches=(), raw=()):
    return pl.pallas_call(
        kernel,
        out_shape=outs,
        in_specs=[SMEM] + [HBM if i in raw else VMEM for i in range(1, len(operands))],
        out_specs=[VMEM] * len(outs),
        scratch_shapes=list(scratches),
        name=name,
        compiler_params=pltpu.CompilerParams(vmem_limit_bytes=grant * 1024 * 1024),
    )(*operands)


def in_hbm(array):
    return pltpu.with_memory_space_constraint(array, pltpu.HBM)


def per_device(initial_state, forcing, coefficients, region_ids):
    size = lax.axis_size("axial")
    device = lax.axis_index("axial")
    assert initial_state.shape == (FIELDS, OWN, SUB * LANES)
    assert region_ids.shape == (OWN, SUB)
    where_ref = jnp.stack([device, jnp.int32(size)]).astype(jnp.int32)
    odd = device % 2
    pair_a = [(i, i ^ 1) for i in range(size)]
    pair_b = [(i, i + 1 if i % 2 else i - 1) for i in range(1, size - 1)]
    swap_a = lambda x: lax.ppermute(x, "axial", pair_a)
    swap_b = lambda x: lax.ppermute(x, "axial", pair_b)

    share = coefficients.shape[1]
    regions = share * size
    per_tile = LANES // OWN
    (gathered,) = call(
        functools.partial(prep_kernel, share),
        "prep",
        4,
        [f32(regions + SUB * -(-size // per_tile), LANES)],
        [where_ref, in_hbm(coefficients.T), in_hbm(region_ids.T)],
        [
            scratch(share, ENTRIES),
            pltpu.VMEM((SUB, OWN), jnp.int32),
            pltpu.SemaphoreType.DMA((2,)),
        ],
        (1, 2),
    )

    def doubled(held, step):
        return held + lax.ppermute(held, "axial", [(i, i ^ step) for i in range(size)])

    state, force, send_a, send_b = call(
        split_kernel,
        "split",
        12,
        [f32(FIELDS, OWN * SUB, LANES)] * 2 + [f32(2 * FIELDS, FINE_HALO * SUB, LANES)] * 2,
        [where_ref, in_hbm(initial_state), in_hbm(forcing)],
        [
            pltpu.VMEM((HELD_PARTS * 2 * FIELDS * OWN, SUB * LANES), jnp.bfloat16),
            scratch(2, FIELDS, OWN, SUB * LANES),
            pltpu.SemaphoreType.DMA((2,)),
        ],
        (1, 2),
    )
    step = 1
    while step < min(size, 8):
        gathered = doubled(gathered, step)
        step *= 2
    gathered, send_a, send_b = lax.optimization_barrier((gathered, send_a, send_b))
    got_b, got_a = swap_b(send_b), swap_a(send_a)
    if step < size:
        free = [i for i in range(size) if i % 2 != i // 2 % 2]
        while step < size:
            gathered = gathered + lax.ppermute(gathered, "axial", [(i, i ^ step) for i in free])
            step *= 2
        gathered = jnp.where(odd != device // 2 % 2, gathered, swap_a(gathered))
    (table,) = call(
        functools.partial(tables_kernel, regions),
        "tables", 12,
        [f32(2 * ENTRIES, TABLE_ROWS, LANES)],
        [where_ref, gathered],
        [scratch(2, 32 * SUB, LANES), scratch(LANES, 2 * LANES)],
    )

    f0 = None
    for cycle in range(CYCLES):
        outs = [f32(*padded(T0, 0)), f32(*padded(T1, 1)), f32(*plain(T1)), f32(*padded(T1, 1)),
                f32(2, 2 * FIELDS, SUB, LANES)]
        temps = [scratch(*padded(T0, 0)), scratch(*padded(T1, 1)), scratch(*plain(T1))]
        if cycle == 0:
            v0, v1, s1, c1, own, f0 = call(
                functools.partial(down_kernel, True), "down_fresh", 14, outs + [f32(*plain(T0))],
                [where_ref, state, force, got_a, got_b, table], temps,
            )
        else:
            inner = call(
                interior_kernel, "interior", 4,
                [f32(*padded(T0, 0))] * 2 + [f32(*padded(T1, 1)), f32(*plain(T1)), f32(*padded(T1, 1))],
                [where_ref, state, f0, table],
            )
            v0, v1, s1, c1, own = call(
                functools.partial(down_kernel, False), "down", 14, outs,
                [where_ref, *inner, got_a, got_b, f0, table], temps,
            )
        beside = swap_a(own)
        (row,) = call(
            relay_kernel, "relay", 2, [f32(3, 2 * FIELDS, SUB, LANES)], [where_ref, own, beside]
        )
        far = swap_b(row)
        beyond = swap_a(far)
        operands = [where_ref, own, beside, far, beyond, v0, f0, v1, s1, c1, table]
        temps = [scratch(*padded(T0, 0))] * 2 + [scratch(*padded(T1, 1))] * 2
        temps += [scratch(*padded(T2, 2)), scratch(*plain(T2)), scratch(*plain(T2)), scratch(*padded(T2, 2)), scratch(*padded(T2, 2))]
        temps += [scratch(*padded(T3, 3)), scratch(*plain(T3)), scratch(*plain(T3)), scratch(*padded(T3, 3)), scratch(*padded(T3, 3))]
        if cycle == CYCLES - 1:
            return call(
                functools.partial(up_kernel, True), "up_last", 26,
                [f32(FIELDS, OWN, SUB * LANES)], operands,
                [pltpu.VMEM((HELD_PARTS * FIELDS * OWN, SUB * LANES), jnp.bfloat16)] + temps,
            )[0]
        state, send_a, send_b = call(
            functools.partial(up_kernel, False), "up", 26,
            [f32(FIELDS, OWN * SUB, LANES)] + [f32(FIELDS, FINE_HALO * SUB, LANES)] * 2,
            operands, temps,
        )
        got_b, got_a = swap_b(send_b), swap_a(send_a)


def solution(mesh):
    placed = (
        P("sample", "axial", None),
        P("sample", "axial", None),
        P("sample", "axial"),
        P("axial", None),
    )
    return jax.shard_map(
        per_device,
        mesh=mesh,
        in_specs=placed,
        out_specs=P("sample", "axial", None),
        check_vma=False,
    )
```
